32 devices in a mesh: ia: 2 (over x), ja: 4 (over z), ka: 4 (over y, core).
Axes of the slice: x: 2, y: 2, z: 4, core: 2. Of those that a mesh axis runs over, the one named last changes fastest.
Arguments:
- flow_state: float32 [5, 4, 64, 64, 128], P(None, 'ka', 'ia', 'ja'), may hold values from -6 to 6
- spectral: float32 [3, 4, 64, 64, 128], P(None, 'ka', 'ia', 'ja'), may hold values from 0.5 to 50
- wave_speed: float32 [3, 4, 5], P(None, 'ka'), may hold values from 0.05 to 2
- left_map: float32 [4, 5, 5], P('ka')
- right_map: float32 [4, 5, 5], P('ka')
- donor_block: int32 [32, 32, 1], P(('ia', 'ja', 'ka')), may hold values from 0 to 127
- receiver_block: int32 [32, 32, 1], P(('ia', 'ja', 'ka')), may hold values from 0 to 127, as said below
- fringe_count: int32 [32, 32], P(('ia', 'ja', 'ka')), may hold values from 0 to 1, as said below
- fringe_weight: float32 [3, 32, 32, 1], P(None, ('ia', 'ja', 'ka')), may hold values from 0 to 1
Outputs:
- advanced: float32 [5, 4, 64, 64, 128], P(None, 'ka', 'ia', 'ja')
- increment: float32 [5, 4, 64, 64, 128], P(None, 'ka', 'ia', 'ja')
The draws below stay inside these ranges and needn't reach their ends.
Inputs may be any that keep to these rules, and one draw needn't show every extreme that they name: `receiver_block`: on each receiving device the cube numbers over all sources and slots are distinct. `fringe_count`: in every draw some receiving device has 1 live slots from every source.
All inputs are finite; a program needn't handle non-finite values.
Results may differ from the reference program's by a relative error of at most 0.0003.
Values sent between devices are 32-bit elements; how exact they have to be, the bound alone decides.
A program may use at most 128 MiB of HBM per device.

```python
import jax
import jax.numpy as jnp
from jax import lax

V = 5
GRID_DEV = 1
CI = 32
CJ = 16
NK = 128
BS = 8
CAP = 1
GRIDS = 4
NI = 64
NJ = 64
BLK_DEV = 128
N_IA = 2
N_JA = 4
N_KA = 4


def transform_draw(key):
    noise = jax.random.uniform(key, (GRIDS, V, V), jnp.float32, -0.3, 0.3)
    diagonal = (jnp.arange(V)[:, None] == jnp.arange(V)[None, :]).astype(jnp.float32)
    return diagonal + noise


def draw_left_map(key, part):
    return transform_draw(jax.random.fold_in(key, 11))


def draw_right_map(key, part):
    return transform_draw(jax.random.fold_in(key, 23))


def draw_spectral(key, part):
    unit = jax.random.uniform(jax.random.fold_in(key, 31), (3, GRIDS, NI, NJ, NK), jnp.float32)
    lower = jnp.full((3, 1, 1, 1, 1), 0.5, jnp.float32)
    upper = jnp.full((3, 1, 1, 1, 1), 50.0, jnp.float32)
    return jnp.exp(jnp.log(lower) + unit * (jnp.log(upper) - jnp.log(lower)))


def draw_wave_speed(key, part):
    unit = jax.random.uniform(jax.random.fold_in(key, 37), (3, GRIDS, V), jnp.float32)
    speeds = jnp.exp(jnp.log(0.05) + unit * (jnp.log(2.0) - jnp.log(0.05)))
    return speeds


def draw_fringe_count(key, part):
    devices = N_IA * N_JA * N_KA
    counts = jax.random.randint(jax.random.fold_in(key, 1), (devices, devices), 0, CAP + 1)
    heavy = jax.random.randint(jax.random.fold_in(key, 2), (), 0, devices)
    receivers = jnp.arange(devices)[:, None]
    senders = jnp.arange(devices)[None, :]
    counts = jnp.where(receivers == heavy, CAP, counts)
    counts = jnp.where(senders == (receivers + 1) % devices, CAP, counts)
    return counts.astype(jnp.int32)


def permute_one(subkey):
    return jax.random.permutation(subkey, BLK_DEV)


def draw_receiver_block(key, part):
    devices = N_IA * N_JA * N_KA
    subkeys = jax.random.split(jax.random.fold_in(key, 5), devices)
    orders = jax.vmap(permute_one)(subkeys)
    return orders[:, :devices * CAP].reshape(devices, devices, CAP).astype(jnp.int32)


def place_ends(result, stream_key, least, high):
    index_at = [jax.random.randint(jax.random.fold_in(stream_key, axis), (), 0, length) for axis, length in enumerate(result.shape)]
    main_axis = result.shape.index(max(result.shape))
    neighbour = index_at[:main_axis] + [(index_at[main_axis] + 1) % result.shape[main_axis]] + index_at[main_axis + 1:]
    return result.at[tuple(index_at)].set(least).at[tuple(neighbour)].set(high)


def shard_levels(rng, shape, cuts, low, largest):
    gain = 1.0
    for dim, parts in cuts:
        steps = jax.random.uniform(jax.random.fold_in(jax.random.fold_in(rng, 6), dim), (parts,), jnp.float32, low / len(cuts), largest / len(cuts))
        gain = gain * jnp.repeat(jnp.exp(steps), shape[dim] // parts).reshape((-1,) + (1,) * (len(shape) - 1 - dim))
    return gain


def normal_values(key, extent, deviation, limit, cuts=(), kind=jnp.bfloat16):
    entries = jax.random.normal(key, extent, jnp.float32) * deviation
    if len(cuts) > 0:
        entries = shard_levels(key, extent, cuts, -0.22, 0.18) * entries
    return jnp.clip(entries, min=-limit, max=limit).astype(kind)


def setup_inputs(seed: int = 0) -> dict:
    keys = jax.random.split(jax.random.key(seed), 10)
    return {
        "flow_state": normal_values(keys[0], (V, GRIDS, NI, NJ, NK), 1.0, 6.0, ((1, 4), (2, 2), (3, 4)), jnp.float32),
        "spectral": draw_spectral(jax.random.fold_in(keys[9], 71), 0),
        "wave_speed": draw_wave_speed(jax.random.fold_in(keys[9], 71), 0),
        "left_map": draw_left_map(jax.random.fold_in(keys[9], 71), 0),
        "right_map": draw_right_map(jax.random.fold_in(keys[9], 71), 0),
        "donor_block": place_ends(jax.random.randint(keys[5], (N_IA * N_JA * N_KA, N_IA * N_JA * N_KA, CAP), 0, BLK_DEV), jax.random.fold_in(keys[5], 1), 0, BLK_DEV - 1).astype(jnp.int32),
        "receiver_block": draw_receiver_block(jax.random.fold_in(keys[9], 71), 0),
        "fringe_count": draw_fringe_count(jax.random.fold_in(keys[9], 71), 0),
        "fringe_weight": jnp.clip(1.0 * jax.random.uniform(keys[8], (3, N_IA * N_JA * N_KA, N_IA * N_JA * N_KA, CAP), jnp.float32) ** shard_levels(keys[8], (3, N_IA * N_JA * N_KA, N_IA * N_JA * N_KA, CAP), ((1, 32),), -0.2, 0.2), 0.0, 1.0),
    }


QUARTER = 0.25


def forward_step(carried, inputs):
    older_first, older_second, older_value, last_first, last_second, last_value = carried
    source, coupling = inputs
    fourth = QUARTER * coupling
    coupled = -coupling + fourth * older_first
    pivots = 1.0 + 2.0 * coupling + 2.0 * fourth + fourth * older_second - last_first * coupled
    first_gain = (-coupling - last_second * coupled) / pivots
    second_gain = -fourth / pivots
    reduced = (source + fourth * older_value - coupled * last_value) / pivots
    return (last_first, last_second, last_value, first_gain, second_gain, reduced), (first_gain, second_gain, reduced)


def backward_step(carried, inputs):
    next_value, after_next = carried
    first_gain, second_gain, reduced = inputs
    solved = reduced - first_gain * next_value - second_gain * after_next
    return (solved, next_value), solved


def solve_lines(source, coupling):
    zeros_plane = jnp.zeros(source.shape[1:], jnp.float32)
    ignored, factors = lax.scan(forward_step, (zeros_plane,) * 6, (source, coupling))
    ignored, solved = lax.scan(backward_step, (zeros_plane, zeros_plane), factors, reverse=True)
    return solved


def blend_axis(blocks, weight, along_dim):
    size_along = blocks.shape[along_dim]
    shifted = jnp.concatenate([lax.slice_in_dim(blocks, 1, size_along, axis=along_dim), lax.slice_in_dim(blocks, size_along - 1, size_along, axis=along_dim)], axis=along_dim)
    return (1.0 - weight) * blocks + weight * shifted


def interpolate(blocks, weights):
    expanded = weights[..., None, None, None, None]
    blocks = blend_axis(blocks, expanded[0], blocks.ndim - 3)
    blocks = blend_axis(blocks, expanded[1], blocks.ndim - 2)
    return blend_axis(blocks, expanded[2], blocks.ndim - 1)


def to_cubes(field):
    shaped = field.reshape(V, N_KA, GRID_DEV, N_IA, CI // BS, BS, N_JA, CJ // BS, BS, NK // BS, BS)
    ordered = shaped.transpose(3, 6, 1, 2, 4, 7, 9, 0, 5, 8, 10)
    return ordered.reshape(N_IA * N_JA * N_KA, BLK_DEV, V * BS ** 3)


def from_cubes(cube_rows):
    shaped = cube_rows.reshape(N_IA, N_JA, N_KA, GRID_DEV, CI // BS, CJ // BS, NK // BS, V, BS, BS, BS)
    return shaped.transpose(7, 2, 3, 0, 4, 8, 1, 5, 9, 6, 10).reshape(V, GRIDS, NI, NJ, NK)


def place_cubes(device_cubes, device_target, device_values):
    return device_cubes.at[device_target].set(device_values, mode="drop")


def grid_step(inputs):
    residual, spectral, speeds, left_grid, right_grid = inputs
    characteristic = jnp.einsum("vu,uijk->vijk", left_grid, residual, precision=lax.Precision.HIGHEST)
    moved = jnp.moveaxis(characteristic, 1, 0)
    coupling = speeds[0][None, :, None, None] * spectral[0][:, None, :, :]
    characteristic = jnp.moveaxis(solve_lines(moved, coupling), 0, 1)
    moved = jnp.moveaxis(characteristic, 2, 0)
    coupling = speeds[1][None, :, None, None] * jnp.moveaxis(spectral[1], 1, 0)[:, None, :, :]
    characteristic = jnp.moveaxis(solve_lines(moved, coupling), 0, 2)
    moved = jnp.moveaxis(characteristic, 3, 0)
    coupling = speeds[2][None, :, None, None] * jnp.moveaxis(spectral[2], 2, 0)[:, None, :, :]
    characteristic = jnp.moveaxis(solve_lines(moved, coupling), 0, 3)
    return jnp.einsum("vu,uijk->vijk", right_grid, characteristic, precision=lax.Precision.HIGHEST)


def reference(flow_state, spectral, wave_speed, left_map, right_map, donor_block, receiver_block, fringe_count, fringe_weight):
    devices = N_IA * N_JA * N_KA
    cube_rows = to_cubes(flow_state)
    sources = jnp.arange(devices, dtype=jnp.int32)
    outbound = cube_rows[sources[:, None, None], donor_block]
    arrived = jnp.swapaxes(outbound, 0, 1)
    blocks = arrived.reshape(devices, devices, CAP, V, BS, BS, BS)
    blended = interpolate(blocks, fringe_weight)
    live_slot = jnp.arange(CAP, dtype=jnp.int32)[None, None, :] < fringe_count[:, :, None]
    target = jnp.where(live_slot, receiver_block, BLK_DEV).astype(jnp.int32)
    cube_rows = jax.vmap(place_cubes)(cube_rows, target.reshape(devices, devices * CAP), blended.reshape(devices, devices * CAP, V * BS ** 3))
    filled = from_cubes(cube_rows)
    padded = jnp.pad(filled, ((0, 0), (0, 0), (1, 1), (1, 1), (1, 1)))
    center = filled
    along_i = padded[:, :, 2:, 1:-1, 1:-1] + padded[:, :, :-2, 1:-1, 1:-1] - 2.0 * center
    along_j = padded[:, :, 1:-1, 2:, 1:-1] + padded[:, :, 1:-1, :-2, 1:-1] - 2.0 * center
    along_k = padded[:, :, 1:-1, 1:-1, 2:] + padded[:, :, 1:-1, 1:-1, :-2] - 2.0 * center
    residual = spectral[0][None] * along_i + spectral[1][None] * along_j + spectral[2][None] * along_k
    per_grid = (jnp.swapaxes(residual, 0, 1), jnp.swapaxes(spectral, 0, 1), jnp.swapaxes(wave_speed, 0, 1), left_map, right_map)
    increment = jnp.swapaxes(lax.map(grid_step, per_grid), 0, 1)
    return filled + increment, increment
```

```python
import functools
import math
import types

import jax
import jax.numpy as jnp
from jax import lax
from jax.experimental import pallas as pl
from jax.experimental.pallas import tpu as pltpu
from jax.sharding import PartitionSpec as P

BS = 8
LANES = 128
GROUPS = LANES // BS
QUARTER = 0.25
BATCH = 4
LAG = 3
VMEM = pl.BlockSpec(memory_space=pltpu.VMEM)
HBM = pl.BlockSpec(memory_space=pltpu.HBM)
MESH = pl.DeviceIdType.MESH
F32 = jnp.float32


def shape(*dims):
    return jax.ShapeDtypeStruct(dims, F32)


def lane_iota(rows=BS):
    return lax.broadcasted_iota(jnp.int32, (rows, LANES), 1)


def row_iota(rows=BS):
    return lax.broadcasted_iota(jnp.int32, (rows, LANES), 0)


def diagonals(tiles):
    group = lane_iota() // BS
    distance = 1
    while distance < GROUPS:
        odd = (group // distance) % 2 == 1
        tiles = [jnp.where(odd, tiles[(a + distance) % GROUPS], tiles[a]) for a in range(GROUPS)]
        distance *= 2
    return [tiles[(GROUPS - g) % GROUPS] for g in range(GROUPS)]


def turned_by(tile, groups):
    return tile if groups % GROUPS == 0 else pltpu.roll(tile, groups % GROUPS * BS, 1)


def tile_row(block, rows_j, g):
    blocks_j = rows_j // BS
    return (block // blocks_j) * (BS * rows_j) + (block % blocks_j) * BS + (g % BS) * rows_j


def rows_at(start, size):
    return pl.ds(pl.multiple_of(start, BS), size)


def pack_set(rows_j, q, flow, packed):
    groups = flow.shape[0] * BS
    first = q * GROUPS
    count = min(GROUPS, groups - first)

    def one(block, carry):
        tiles = [
            turned_by(flow[g // BS, rows_at(tile_row(block, rows_j, g), BS), :], g - first)
            for g in range(first, first + count)
        ]
        tiles = diagonals(tiles + tiles[:1] * (GROUPS - count))
        for k in range(GROUPS):
            packed[block * GROUPS + k, q * BS : (q + 1) * BS, :] = tiles[k]
        return carry

    lax.fori_loop(0, packed.shape[0] // GROUPS, one, 0)


def gather_all(capacity, donor, packed, outbound):
    slots, packed_rows, lanes = outbound.shape
    low = lane_iota() < LANES // 2
    tiles = packed_rows // BS

    def some(batch, carry):
        fresh = []
        for n in range(BATCH):
            slot = batch * BATCH + n
            cube = donor[0, slot % capacity, slot // capacity]
            shift = (GROUPS - cube % GROUPS) % GROUPS * BS
            for q in range(tiles):
                tile = pltpu.roll(packed[cube, q * BS : (q + 1) * BS, :], shift, 1)
                if q == tiles - 1:
                    folded = pltpu.roll(pltpu.roll(tile, BS // 2, 0), LANES // 2, 1)
                    tile = jnp.where(low, tile, folded)
                fresh.append((slot, q, tile))
        for slot, q, tile in fresh:
            outbound[slot, q * BS : (q + 1) * BS, :] = tile
        return carry

    lax.fori_loop(0, slots // BATCH, some, 0)


def blend(cubes, shifted, weight):
    return (1.0 - weight) * cubes + weight * shifted


def interpolate(capacity, weights, receiver, slots, arrived):
    lane, row = lane_iota(), row_iota()
    tiles = arrived.shape[1] // BS
    held = [arrived[slot, q * BS : (q + 1) * BS, :] for slot in slots for q in range(tiles)]
    fresh = []
    for n, cubes in enumerate(held):
        slot, q = slots[n // tiles], n % tiles
        d, c = slot // capacity, slot % capacity
        shift = receiver[0, c, d] % GROUPS * BS
        if q == tiles - 1:
            unfolded = pltpu.roll(pltpu.roll(cubes, BS // 2, 0), LANES // 2, 1)
            cubes = jnp.where(row < BS // 2, cubes, unfolded)
        after = jnp.where(lane % (BS * BS) >= BS * (BS - 1), cubes, pltpu.roll(cubes, LANES - BS, 1))
        cubes = blend(cubes, after, weights[0, c, d])
        after = jnp.where(row == BS - 1, cubes, pltpu.roll(cubes, BS - 1, 0))
        cubes = blend(cubes, after, weights[1, c, d])
        after = jnp.where(lane % BS == BS - 1, cubes, pltpu.roll(cubes, LANES - 1, 1))
        cubes = blend(cubes, after, weights[2, c, d])
        fresh.append(pltpu.roll(cubes, shift, 1))
    for n, cubes in enumerate(fresh):
        q = n % tiles
        arrived[slots[n // tiles], q * BS : (q + 1) * BS, :] = cubes


def source_of(capacity, slots, receiver, count):
    lane = lane_iota()

    def one(slot, found):
        d, c = slot // capacity, slot % capacity
        target = jnp.where(count[0, d] > c, receiver[0, c, d], -1)
        return jnp.where(lane == target, slot, found)

    return lax.fori_loop(0, slots, one, jnp.full((BS, LANES), -1, jnp.int32), unroll=BATCH)


def unpack_all(rows_j, source, arrived, flow, padded):
    groups = flow.shape[0] * BS
    group = lane_iota() // BS

    def one(block, carry):
        slots = [source[0, block * GROUPS + k] for k in range(GROUPS)]
        owner = jnp.full((BS, LANES), -1, jnp.int32)
        for k in range(GROUPS):
            owner = jnp.where(group == k, slots[k], owner)
        live = owner >= 0
        for first in range(0, groups, GROUPS):
            q = first // GROUPS
            tiles = diagonals(
                [arrived[jnp.maximum(slots[k], 0), q * BS : (q + 1) * BS, :] for k in range(GROUPS)]
            )
            for g in range(first, min(first + GROUPS, groups)):
                row = tile_row(block, rows_j, g)
                fresh = turned_by(tiles[g - first], GROUPS - (g - first))
                kept = flow[g // BS, rows_at(row, BS), :]
                padded[g // BS, rows_at(row + rows_j, BS), :] = jnp.where(live, fresh, kept)
        return carry

    lax.fori_loop(0, flow.shape[1] * flow.shape[2] // BS**3 // GROUPS, one, 0)


def row_of(n, count, lower):
    return jnp.where(lower, n, count - 1 - n)


def gains_of(state):
    older, newer, lead = state
    return lead, -QUARTER * older, (QUARTER * lead - 1.0) * newer, -QUARTER * newer


def meet_factors(near, far):
    f0, s0, f1, s1 = gains_of(near)
    g0, t0, g1, t1 = gains_of(far)
    cross = g1 - t1 * f0
    a11 = 1.0 - t1 * s0 - cross * f1
    a12 = -cross * s1
    a21 = g0 - t0 * f1
    a22 = 1.0 - t0 * s1
    scale = 1.0 / (a11 * a22 - a12 * a21)
    return a22 * scale, a12 * scale, a21 * scale, a11 * scale, t1, cross, t0


def meet(factors, near, far):
    m11, m12, m21, m22, t1, cross, t0 = factors
    r0, r1 = near
    q0, q1 = far
    b1 = q1 - t1 * r0 - cross * r1
    b2 = q0 - t0 * r1
    return b1 * m11 - m12 * b2, m22 * b2 - m21 * b1


def eliminated(pivot, carry):
    older, newer, lead, square = carry
    inverse = 1.0 / (pivot - 0.0625 * older - square)
    gain = QUARTER * lead - 1.0
    lead = gain * inverse
    return inverse, lead, (newer, inverse, lead, gain * gain * inverse)


def begin_factor(older, newer, lead):
    gain = QUARTER * lead - 1.0
    lead = gain * newer
    return older, newer, lead, gain * lead


def invert_rho(direction, rows, stride, spectral, inverse):
    plane = inverse.shape[0] // rows

    def one(row, carry):
        at = rows_at(row * plane, plane)
        if stride is None:
            inverse[at, :] = 1.0 / spectral[direction, at, :]
        else:
            inverse[at, :] = 1.0 / spectral[direction, pl.ds(row, plane, stride=stride), :]
        return carry

    lax.fori_loop(0, rows, one, 0, unroll=2)


def factor_pass(direction, rows, lower, group, paces, inverse, start, u_ref, l_ref, last):
    variables, total, lanes = u_ref.shape
    plane = total // rows
    for first in range(0, variables, group):
        vs = range(first, min(first + group, variables))

        def one(n, carry):
            at = rows_at(row_of(n, rows, lower) * plane, plane)
            ratio = inverse[at, :]
            fresh = []
            for v, held in zip(vs, carry):
                pace = paces[direction * variables + v, :plane, :]
                u, l, held = eliminated(pace * ratio + 2.5, held)
                u_ref[v, at, :] = u
                l_ref[v, at, :] = l
                fresh.append(held)
            return tuple(fresh)

        lax.fori_loop(0, rows, one, tuple(begin_factor(start[v, 0], start[v, 1], start[v, 2]) for v in vs))
    newest = rows_at(row_of(rows - 1, rows, lower) * plane, plane)
    older = rows_at(row_of(rows - 2, rows, lower) * plane, plane)
    for v in range(variables):
        last[v, 0] = u_ref[v, older, :]
        last[v, 1] = u_ref[v, newest, :]
        last[v, 2] = l_ref[v, older, :]


def forward_pass(vs, rows, lower, values, scale, u_ref, l_ref, gains, start, ends):
    variables, total, lanes = values.shape
    plane = total // rows

    def one(n, carry):
        at = rows_at(row_of(n, rows, lower) * plane, plane)
        fresh = []
        for v, (product, older, newer) in zip(vs, carry):
            value = scale(v, at, values[v, at, :]) + QUARTER * older - product
            reduced = u_ref[v, at, :] * value
            values[v, at, :] = reduced
            fresh.append((l_ref[v, at, :] * value, newer, reduced))
        return tuple(fresh)

    begin = tuple(((QUARTER * gains[v, 2] - 1.0) * start[v, 1], start[v, 0], start[v, 1]) for v in vs)
    for v, (product, older, newer) in zip(vs, lax.fori_loop(0, rows, one, begin, unroll=4)):
        ends[v, 0] = older
        ends[v, 1] = newer


def backward_pass(vs, rows, lower, values, u_ref, l_ref, nexts, solved, store):
    variables, total, lanes = values.shape
    plane = total // rows

    def one(step, carry):
        row = row_of(rows - 1 - step, rows, lower)
        at = rows_at(row * plane, plane)
        fresh = []
        for v, (nearer, farther) in zip(vs, carry):
            value = values[v, at, :] + QUARTER * u_ref[v, at, :] * farther - l_ref[v, at, :] * nearer
            store(v, row, at, value)
            fresh.append((value, nearer))
        return tuple(fresh)

    begin = tuple((nexts[v, 0], nexts[v, 1]) for v in vs)
    for v, (nearer, farther) in zip(vs, lax.fori_loop(0, rows, one, begin, unroll=4)):
        if solved is not None:
            solved[v, 0] = nearer
            solved[v, 1] = farther


def residual_rows(rows_i, first, count, padded, spectral, left, paces, inverse, values):
    variables, total, lanes = values.shape
    rows_j = total // rows_i
    lane, row_id = lane_iota(rows_j), row_iota(rows_j)

    def one(row, carry):
        base = row * rows_j
        at = rows_at(base, rows_j)
        rho = [spectral[e, at, :] for e in range(3)]
        ratio = inverse[at, :]
        residual = []
        for v in range(variables):
            center = padded[v, rows_at(base + rows_j, rows_j), :]
            twice = 2.0 * center
            along_i = padded[v, rows_at(base + 2 * rows_j, rows_j), :] + padded[v, at, :] - twice
            after = jnp.where(row_id == rows_j - 1, 0.0, pltpu.roll(center, rows_j - 1, 0))
            before = jnp.where(row_id == 0, 0.0, pltpu.roll(center, 1, 0))
            along_j = after + before - twice
            after = jnp.where(lane == lanes - 1, 0.0, pltpu.roll(center, lanes - 1, 1))
            before = jnp.where(lane == 0, 0.0, pltpu.roll(center, 1, 1))
            along_k = after + before - twice
            residual.append(rho[0] * along_i + rho[1] * along_j + rho[2] * along_k)
        for v in range(variables):
            total_v = left[v, 0, 0] * residual[0]
            for u in range(1, variables):
                total_v = total_v + left[v, 0, u] * residual[u]
            values[v, at, :] = total_v * (ratio * paces[v, :rows_j, :])
        return carry

    lax.fori_loop(first, first + count, one, 0)


def edge_rows(rows_i, halo, spectral, left, paces, inverse, values):
    variables, total, lanes = values.shape
    rows_j = total // rows_i
    for side, first in enumerate((0, rows_j - 1)):
        at = pl.ds(first, rows_i, stride=rows_j)
        rho = spectral[1, at, :] * inverse[at, :]
        parts = [rho * halo[side, u] for u in range(variables)]
        for v in range(variables):
            total_v = left[v, 0, 0] * parts[0]
            for u in range(1, variables):
                total_v = total_v + left[v, 0, u] * parts[u]
            values[v, at, :] = values[v, at, :] + total_v * paces[v, :rows_i, :]


class Line:
    def __init__(self, axis):
        self.axis = axis
        self.members = lax.axis_size(axis)
        self.half = self.members // 2
        self.place = lax.axis_index(axis)
        self.lower = self.place < self.half
        depth = jnp.where(self.lower, self.place, self.members - 1 - self.place)
        self.inner = jnp.where(self.lower, self.place + 1, self.place - 1)
        self.outer = jnp.where(self.lower, self.place - 1, self.place + 1)
        self.middle = depth == self.half - 1
        self.end = depth == 0

    def send(self, source, target, sems, device):
        return pltpu.make_async_remote_copy(
            src_ref=source,
            dst_ref=target,
            send_sem=sems.at[0],
            recv_sem=sems.at[1],
            device_id={self.axis: device},
            device_id_type=MESH,
        )

    def sides(self):
        return (self.place > 0, self.place - 1), (self.place < self.members - 1, self.place + 1)


def span(vs):
    return pl.ds(vs[0], len(vs))


class Sweep:
    def __init__(self, line, s, chunks):
        self.line, self.s, self.chunks = line, s, chunks

    def gains_in(self):
        line, s = self.line, self.s
        if line.half > 1:

            @pl.when(jnp.logical_not(line.end))
            def _():
                line.send(s.last, s.gains, s.gain_sems.at[0], line.inner).wait_recv()

    def gains_out(self, wait=False):
        line, s = self.line, self.s

        def act(copy):
            copy.wait_send() if wait else copy.start()

        if line.half > 1:

            @pl.when(jnp.logical_not(line.middle))
            def _():
                act(line.send(s.last, s.gains, s.gain_sems.at[0], line.inner))

        @pl.when(line.middle)
        def _():
            act(line.send(s.last, s.far_gains, s.gain_sems.at[1], line.inner))

    def prepare(self):
        line, s = self.line, self.s

        @pl.when(line.middle)
        def _():
            line.send(s.last, s.far_gains, s.gain_sems.at[1], line.inner).wait_recv()
            for v in range(s.last.shape[0]):
                near = [s.last[v, m] for m in range(3)]
                far = [s.far_gains[v, m] for m in range(3)]
                for m, factor in enumerate(meet_factors(near, far)):
                    s.meeting[v, m] = factor

    def inward(self, c):
        line, s, at = self.line, self.s, span(self.chunks[c])
        return line.send(s.ends.at[at], s.start.at[at], s.sems.at[0, c], line.inner)

    def across(self, c):
        line, s, at = self.line, self.s, span(self.chunks[c])
        return line.send(s.ends.at[at], s.far.at[at], s.sems.at[1, c], line.inner)

    def outward(self, c):
        line, s, at = self.line, self.s, span(self.chunks[c])
        return line.send(s.solved.at[at], s.nexts.at[at], s.sems.at[2, c], line.outer)

    def start_in(self, c):
        if self.line.half > 1:

            @pl.when(jnp.logical_not(self.line.end))
            def _():
                self.inward(c).wait_recv()

    def ends_out(self, c, wait=False):
        line = self.line

        def act(copy):
            copy.wait_send() if wait else copy.start()

        if line.half > 1:

            @pl.when(jnp.logical_not(line.middle))
            def _():
                act(self.inward(c))

        @pl.when(line.middle)
        def _():
            act(self.across(c))

    def nexts_in(self, c):
        line, s = self.line, self.s

        @pl.when(line.middle)
        def _():
            self.across(c).wait_recv()
            for v in self.chunks[c]:
                pair = meet(
                    [s.meeting[v, m] for m in range(7)],
                    [s.ends[v, m] for m in range(2)],
                    [s.far[v, m] for m in range(2)],
                )
                s.nexts[v, 0], s.nexts[v, 1] = pair

        if line.half > 1:

            @pl.when(jnp.logical_not(line.middle))
            def _():
                self.outward(c).wait_recv()

    def solved_out(self, c, wait=False):
        line = self.line
        if line.half > 1:

            @pl.when(jnp.logical_not(line.end))
            def _():
                self.outward(c).wait_send() if wait else self.outward(c).start()

    def clear(self):
        line, s = self.line, self.s

        @pl.when(line.end)
        def _():
            s.gains[...] = jnp.zeros(s.gains.shape, F32)
            s.start[...] = jnp.zeros(s.start.shape, F32)


def step_body(axes, capacity, rows_i, rows_j, chunks, names, *refs):
    s = types.SimpleNamespace(**dict(zip(names, refs)))
    flow, rho, padded = s.flow, s.rho, s.padded
    variables, total, lanes = flow.shape
    line_i, line_j = Line("ia"), Line("ja")

    def part(letter):
        return types.SimpleNamespace(**{k[2:]: r for k, r in vars(s).items() if k[:2] == letter + "_"})

    si, sj = part("i"), part("j")
    sweep_i, sweep_j = Sweep(line_i, si, chunks), Sweep(line_j, sj, chunks)
    sizes = [lax.axis_size(axis) for axis in axes]
    here = [lax.axis_index(axis) for axis in axes]
    devices = math.prod(sizes)
    slots = devices * capacity

    fields = [pltpu.make_async_copy(s.flow_in.at[v], flow.at[v], s.in_sems.at[v]) for v in range(variables)]
    fields += [pltpu.make_async_copy(s.rho_in.at[e], rho.at[e], s.in_sems.at[variables + e]) for e in range(3)]
    small = [
        pltpu.make_async_copy(getattr(s, name + "_in"), getattr(s, name), s.small_sems.at[n])
        for n, name in enumerate(("speeds", "left", "right", "donor", "receiver", "count", "weights"))
    ]
    for copy in fields[:variables] + small + fields[variables:]:
        copy.start()

    far_j = sorted(range(sizes[1]), key=lambda d: -min(d, sizes[1] - d))
    rest = devices // sizes[1]

    def peer(offset_j, n, sign):
        off = (n // sizes[2], offset_j, n % sizes[2])
        place = [(h + sign * o + size) % size for h, o, size in zip(here, off, sizes)]
        number = (place[0] * sizes[1] + place[1]) * sizes[2] + place[2]
        return number, dict(zip(axes, place))

    me = (here[0] * sizes[1] + here[1]) * sizes[2] + here[2]
    barrier = pltpu.get_barrier_semaphore()
    with jax.named_scope("greet"):
        for offset_j in far_j:

            def greet(n, carry):
                pl.semaphore_signal(barrier, inc=1, device_id=peer(offset_j, n, 1)[1], device_id_type=MESH)
                return carry

            lax.fori_loop(0 if offset_j else 1, rest, greet, 0)

    with jax.named_scope("pack"):
        packed_tiles = s.packed.shape[1] // BS
        for q in range(packed_tiles):
            for copy in fields[q * 2 : min(q * 2 + 2, variables)]:
                copy.wait()
            pack_set(rows_j, q, flow, s.packed)
    with jax.named_scope("gather"):
        for copy in small:
            copy.wait()
        gather_all(capacity, s.donor, s.packed, s.outbound)
    with jax.named_scope("entered"):
        pl.semaphore_wait(barrier, devices - 1)

    used = variables * BS**3 // LANES

    def cubes(step, to, place, of):
        def at(device):
            return pl.ds(device * capacity, capacity), pl.ds(0, used)

        return pltpu.make_async_remote_copy(
            src_ref=s.outbound.at[at(to)],
            dst_ref=s.arrived.at[at(of)],
            send_sem=s.cube_sems.at[0, step],
            recv_sem=s.cube_sems.at[1, step],
            device_id=place,
            device_id_type=MESH,
        )

    with jax.named_scope("send_cubes"):
        for m, offset_j in enumerate(far_j):

            def begin(n, carry):
                to, place = peer(offset_j, n, 1)
                cubes(m * rest + n, to, place, me).start()
                return carry

            lax.fori_loop(0 if offset_j else 1, rest, begin, 0)
        own = pl.ds(me * capacity, capacity)
        s.arrived[own] = s.outbound[own]

    def pace(n, carry):
        value = jnp.full((BS, LANES), s.speeds[n // variables, 0, n % variables], F32)
        value = 1.0 / value
        for first in range(0, s.paces.shape[1], BS):
            s.paces[n, first : first + BS, :] = value
        return carry

    def factor_j():
        with jax.named_scope("factor_j"):
            sweep_j.gains_in()
            factor_pass(1, rows_j, line_j.lower, 2, s.paces, sj.inverse, sj.gains, sj.u, sj.l, sj.last)
            sweep_j.gains_out()

    with jax.named_scope("prepare"):
        lax.fori_loop(0, 3 * variables, pace, 0)
        sweep_i.clear()
        sweep_j.clear()
        for copy in fields[variables:]:
            copy.wait()
        invert_rho(1, rows_j, rows_j, rho, sj.inverse)
        pl.when(line_j.end)(factor_j)
    with jax.named_scope("factor_i"):
        invert_rho(0, rows_i, None, rho, si.inverse)
        sweep_i.gains_in()
        factor_pass(0, rows_i, line_i.lower, 3, s.paces, si.inverse, si.gains, si.u, si.l, si.last)
        sweep_i.gains_out()
    with jax.named_scope("sources"):
        s.found[...] = source_of(capacity, slots, s.receiver, s.count)
        found = pltpu.make_async_copy(s.found, s.source, s.small_sems.at[0])
        found.start()
    with jax.named_scope("factor_k"):
        factor_k(rows_j, variables, s)
    with jax.named_scope("arrivals"):
        for m, offset_j in enumerate(far_j):

            def arrive(batch, carry):
                for n in range(BATCH):
                    n = batch * BATCH + n
                    of, place = peer(offset_j, n, -1)

                    def wait():
                        cubes(m * rest + n, me, place, of).wait_recv()

                    wait() if offset_j else pl.when(n > 0)(wait)
                sources = [peer(offset_j, batch * BATCH + n, -1)[0] for n in range(BATCH)]
                for c in range(capacity):
                    interpolate(capacity, s.weights, s.receiver, [of * capacity + c for of in sources], s.arrived)
                return carry

            lax.fori_loop(0, rest // BATCH, arrive, 0)
    with jax.named_scope("unpack"):
        found.wait()
        unpack_all(rows_j, s.source, s.arrived, flow, padded)

    def halo(line, axis_number, side, device):
        if axis_number == 1:
            source, target = s.edge.at[side], s.halo.at[1 - side]
        else:
            here, there = (rows_j, rows_j + total) if side == 0 else (total, 0)
            source = padded.at[:, pl.ds(here, rows_j), :]
            target = padded.at[:, pl.ds(there, rows_j), :]
        return line.send(source, target, s.halo_sems.at[axis_number * 2 + side], device)

    borders = ((1, line_j), (0, line_i))
    with jax.named_scope("send_halos"):
        for v in range(variables):
            s.edge[0, v] = padded[v, pl.ds(rows_j, rows_i, stride=rows_j), :]
            s.edge[1, v] = padded[v, pl.ds(2 * rows_j - 1, rows_i, stride=rows_j), :]
        for axis_number, line in borders:
            for side, (there, device) in enumerate(line.sides()):

                @pl.when(there)
                def _():
                    halo(line, axis_number, side, device).start()

    if line_j.half > 1:
        pl.when(jnp.logical_not(line_j.end))(factor_j)
    with jax.named_scope("prepare_i"):
        sweep_i.prepare()
    rest_of = (padded, rho, s.left, s.paces, si.inverse, si.values)
    with jax.named_scope("residual"):
        residual_rows(rows_i, 1, rows_i - 2, *rest_of)
    with jax.named_scope("halos"):
        for axis_number, line in borders[::-1]:
            for side, (there, device) in enumerate(line.sides()):

                @pl.when(there)
                def _():
                    halo(line, axis_number, 1 - side, device).wait_recv()

                @pl.when(jnp.logical_not(there))
                def _():
                    if axis_number == 1:
                        s.halo[side] = jnp.zeros(s.halo.shape[1:], F32)
                    else:
                        first = 0 if side == 0 else rows_j + total
                        padded[:, first : first + rows_j, :] = jnp.zeros((variables, rows_j, lanes), F32)
    with jax.named_scope("edges"):
        residual_rows(rows_i, 0, 1, *rest_of)
        residual_rows(rows_i, rows_i - 1, 1, *rest_of)
        edge_rows(rows_i, s.halo, rho, s.left, s.paces, si.inverse, si.values)

    def plain(v, at, value):
        return value

    def scaled(v, at, value):
        return value * (sj.inverse[at, :] * s.paces[variables + v, :rows_i, :])

    def store_turned(v, row, at, value):
        sj.values[v, pl.ds(row, rows_j, stride=rows_i), :] = value

    def store_lines(v, row, at, value):
        sj.values[v, at, :] = value

    def forward_i(c):
        sweep_i.start_in(c)
        forward_pass(chunks[c], rows_i, line_i.lower, si.values, plain, si.u, si.l, si.gains, si.start, si.ends)
        sweep_i.ends_out(c)

    def back_i(c):
        sweep_i.nexts_in(c)
        solved = si.solved if line_i.half > 1 else None
        backward_pass(chunks[c], rows_i, line_i.lower, si.values, si.u, si.l, si.nexts, solved, store_turned)
        sweep_i.solved_out(c)

    def forward_j(c):
        sweep_j.start_in(c)
        forward_pass(chunks[c], rows_j, line_j.lower, sj.values, scaled, sj.u, sj.l, sj.gains, sj.start, sj.ends)
        sweep_j.ends_out(c)

    def back_j(c):
        sweep_j.nexts_in(c)
        solved = sj.solved if line_j.half > 1 else None
        backward_pass(chunks[c], rows_j, line_j.lower, sj.values, sj.u, sj.l, sj.nexts, solved, store_lines)
        sweep_j.solved_out(c)

    numbers = range(len(chunks))
    with jax.named_scope("forward_i"):
        for c in numbers:
            forward_i(c)
    with jax.named_scope("prepare_j"):
        sweep_j.prepare()
    with jax.named_scope("back_i"):
        for c in numbers:
            back_i(c)
            pl.when(line_j.end)(functools.partial(forward_j, c))
    with jax.named_scope("solve_j"):
        for c in range(len(chunks) + LAG):
            if c < len(chunks) and line_j.half > 1:
                pl.when(jnp.logical_not(line_j.end))(functools.partial(forward_j, c))
            if c >= LAG:
                back_j(c - LAG)

    with jax.named_scope("close"):
        for axis_number, line in borders:
            for side, (there, device) in enumerate(line.sides()):

                @pl.when(there)
                def _():
                    halo(line, axis_number, side, device).wait_send()

        for m, offset_j in enumerate(far_j):

            def close(n, carry):
                to, place = peer(offset_j, n, 1)
                cubes(m * rest + n, to, place, me).wait_send()
                return carry

            lax.fori_loop(0 if offset_j else 1, rest, close, 0)
        for sweep in (sweep_i, sweep_j):
            sweep.gains_out(wait=True)
            for c in numbers:
                sweep.ends_out(c, wait=True)
                sweep.solved_out(c, wait=True)
    finish(rows_j, variables, s)


def sides_of(lanes, depth, step):
    for k in (step, lanes - 1 - step):
        yield rows_at(k * depth, depth)


def factor_k(rows_j, variables, s):
    total, lanes = s.rho.shape[1:]
    rows_i = total // rows_j
    quarters = total // LANES
    per_quarter = LANES // rows_i
    depth = s.k_u.shape[0] // lanes
    for q in range(quarters):
        rho = jnp.concatenate(
            [s.rho[2, pl.ds(q * per_quarter + j, rows_i, stride=rows_j), :] for j in range(per_quarter)],
            axis=0,
        )
        ratio = (1.0 / rho).T
        for v in range(variables):
            s.k_ratio[pl.ds(v * quarters + q, lanes, stride=depth), :] = ratio * s.paces[2 * variables + v, :1, :]
    for spare in range(variables * quarters, depth):
        at = pl.ds(spare, lanes, stride=depth)
        s.k_ratio[at, :] = jnp.zeros((lanes, lanes), F32)
        s.k_values[at, :] = jnp.zeros((lanes, lanes), F32)

    half = lanes // 2
    s.k_zero[...] = jnp.zeros((depth, lanes), F32)
    zero = s.k_zero[...]

    def one(n, carry):
        fresh = []
        for at, held in zip(sides_of(lanes, depth, n), carry):
            u, l, held = eliminated(s.k_ratio[at, :] + 2.5, held)
            s.k_u[at, :] = u
            s.k_l[at, :] = l
            fresh.append(held)
        return tuple(fresh)

    lax.fori_loop(0, half, one, (begin_factor(zero, zero, zero),) * 2)
    pair = []
    for older, newer in zip(sides_of(lanes, depth, half - 2), sides_of(lanes, depth, half - 1)):
        pair.append((s.k_u[older, :], s.k_u[newer, :], s.k_l[older, :]))
    for side in range(2):
        for m, factor in enumerate(meet_factors(pair[side], pair[1 - side])):
            s.k_meeting[side, m] = factor


def finish(rows_j, variables, s):
    lines, values = s.j_values, s.k_values
    total, lanes = s.rho.shape[1:]
    rows_i = total // rows_j
    quarters = total // LANES
    per_quarter = LANES // rows_i
    depth = s.k_u.shape[0] // lanes
    half = lanes // 2
    with jax.named_scope("turn_k"):
        for v in range(variables):
            for q in range(quarters):
                at = pl.ds(v * quarters + q, lanes, stride=depth)
                values[at, :] = lines[v, q * LANES : (q + 1) * LANES, :].T
    zero = s.k_zero[...]

    def ahead(n, carry):
        fresh = []
        for at, (product, older, newer) in zip(sides_of(lanes, depth, n), carry):
            value = values[at, :] * s.k_ratio[at, :] + QUARTER * older - product
            reduced = s.k_u[at, :] * value
            values[at, :] = reduced
            fresh.append((s.k_l[at, :] * value, newer, reduced))
        return tuple(fresh)

    with jax.named_scope("forward_k"):
        ends = [end[1:] for end in lax.fori_loop(0, half, ahead, ((zero,) * 3,) * 2, unroll=2)]
        nexts = tuple(
            meet([s.k_meeting[side, m] for m in range(7)], ends[side], ends[1 - side]) for side in range(2)
        )

    def back(step, carry):
        fresh = []
        for at, (nearer, farther) in zip(sides_of(lanes, depth, half - 1 - step), carry):
            value = values[at, :] + QUARTER * s.k_u[at, :] * farther - s.k_l[at, :] * nearer
            values[at, :] = value
            fresh.append((value, nearer))
        return tuple(fresh)

    with jax.named_scope("back_k"):
        lax.fori_loop(0, half, back, nexts, unroll=2)
    with jax.named_scope("out"):
        for q in range(quarters):
            solved = [values[pl.ds(u * quarters + q, lanes, stride=depth), :] for u in range(variables)]
            for v in range(variables):
                total_v = s.right[v, 0, 0] * solved[0]
                for u in range(1, variables):
                    total_v = total_v + s.right[v, 0, u] * solved[u]
                turned = total_v.T
                for j in range(per_quarter):
                    first = q * per_quarter + j
                    piece = turned[j * rows_i : (j + 1) * rows_i]
                    s.increment[v, pl.ds(first, rows_i, stride=rows_j), :] = piece
                    filled = s.padded[v, pl.ds(rows_j + first, rows_i, stride=rows_j), :]
                    s.advanced[v, pl.ds(first, rows_i, stride=rows_j), :] = filled + piece


def local(
    flow_state, spectral, wave_speed, left_map, right_map,
    donor_block, receiver_block, fringe_count, fringe_weight,
):
    variables, grids, rows_i, rows_j, rows_k = flow_state.shape
    assert grids == 1 and rows_k == LANES
    total = rows_i * rows_j
    devices, capacity = donor_block.shape[1:]
    slots = devices * capacity
    cube_count = total // (BS * BS) * (rows_k // BS)
    assert cube_count == LANES
    packed_rows = -(-variables * BS // GROUPS) * BS
    depth = -(-variables * (total // LANES) // BS) * BS
    axes = ("ia", "ja", "ka")
    chunks = tuple((v,) for v in range(variables))
    operands = dict(
        flow_in=flow_state.reshape(variables, total, rows_k),
        rho_in=spectral.reshape(3, total, rows_k),
        speeds_in=wave_speed,
        left_in=left_map.transpose(1, 0, 2),
        right_in=right_map.transpose(1, 0, 2),
        donor_in=donor_block.transpose(0, 2, 1),
        receiver_in=receiver_block.transpose(0, 2, 1),
        count_in=fringe_count,
        weights_in=fringe_weight.transpose(0, 1, 3, 2).reshape(3, capacity, devices),
    )
    dma = pltpu.SemaphoreType.DMA

    def held(*dims):
        return pltpu.VMEM(dims, F32)

    scratch = dict(
        flow=held(variables, total, rows_k),
        rho=held(3, total, rows_k),
        padded=held(variables, total + 2 * rows_j, rows_k),
        packed=held(cube_count, packed_rows, LANES),
        outbound=held(slots, packed_rows, LANES),
        arrived=held(slots, packed_rows, LANES),
        found=pltpu.VMEM((BS, LANES), jnp.int32),
        source=pltpu.SMEM((BS, LANES), jnp.int32),
        paces=held(3 * variables, max(rows_i, rows_j), LANES),
        edge=held(2, variables, rows_i, rows_k),
        halo=held(2, variables, rows_i, rows_k),
        in_sems=dma((variables + 3,)),
        small_sems=dma((7,)),
        cube_sems=dma((2, devices)),
        halo_sems=dma((4, 2)),
    )
    for name in ("speeds", "left", "right", "donor", "receiver", "count", "weights"):
        array = operands[name + "_in"]
        scratch[name] = pltpu.SMEM(array.shape, array.dtype)
    for letter, plane in (("i_", rows_j), ("j_", rows_i)):
        for name in ("u", "l", "values"):
            scratch[letter + name] = held(variables, total, rows_k)
        scratch[letter + "inverse"] = held(total, rows_k)
        for name in ("last", "gains", "far_gains"):
            scratch[letter + name] = held(variables, 3, plane, rows_k)
        for name in ("ends", "start", "far", "nexts", "solved"):
            scratch[letter + name] = held(variables, 2, plane, rows_k)
        scratch[letter + "meeting"] = held(variables, 7, plane, rows_k)
        scratch[letter + "gain_sems"] = dma((2, 2))
        scratch[letter + "sems"] = dma((3, len(chunks), 2))
    for name in ("u", "l", "ratio", "values"):
        scratch["k_" + name] = held(rows_k * depth, LANES)
    scratch["k_zero"] = held(depth, LANES)
    scratch["k_meeting"] = held(2, 7, depth, LANES)

    field = shape(variables, total, rows_k)
    names = (*operands, "advanced", "increment", *scratch)
    moved = sum(a.size * 4 for a in operands.values()) + 2 * field.size * 4
    used = sum(math.prod(r.shape) * 4 for r in scratch.values() if math.prod(r.shape) > 1024)
    advanced, increment = pl.pallas_call(
        functools.partial(step_body, axes, capacity, rows_i, rows_j, chunks, names),
        out_shape=[field, field],
        in_specs=[HBM] * len(operands),
        out_specs=[VMEM] * 2,
        scratch_shapes=list(scratch.values()),
        compiler_params=pltpu.CompilerParams(
            vmem_limit_bytes=60 << 20, collective_id=0, has_side_effects=True
        ),
        cost_estimate=pl.CostEstimate(flops=60_000_000, bytes_accessed=moved, transcendentals=0),
    )(*operands.values())
    return advanced.reshape(flow_state.shape), increment.reshape(flow_state.shape)


def solution(mesh):
    return jax.shard_map(
        local,
        mesh=mesh,
        in_specs=(
            P(None, "ka", "ia", "ja", None),
            P(None, "ka", "ia", "ja", None),
            P(None, "ka", None),
            P("ka", None, None),
            P("ka", None, None),
            P(("ia", "ja", "ka"), None, None),
            P(("ia", "ja", "ka"), None, None),
            P(("ia", "ja", "ka"), None),
            P(None, ("ia", "ja", "ka"), None, None),
        ),
        out_specs=(P(None, "ka", "ia", "ja", None), P(None, "ka", "ia", "ja", None)),
        check_vma=False,
    )
```

```python
import functools
import math
import types

import jax
import jax.numpy as jnp
from jax import lax
from jax.experimental import pallas as pl
from jax.experimental.pallas import tpu as pltpu
from jax.sharding import PartitionSpec as P

BS = 8
LANES = 128
GROUPS = LANES // BS
QUARTER = 0.25
BATCH = 4
LIMIT = 44 << 20
VMEM = pl.BlockSpec(memory_space=pltpu.VMEM)
HBM = pl.BlockSpec(memory_space=pltpu.HBM)
MESH = pl.DeviceIdType.MESH
F32 = jnp.float32


def in_hbm(array):
    return pltpu.with_memory_space_constraint(array, pltpu.HBM)


def lane_iota(rows=BS):
    return lax.broadcasted_iota(jnp.int32, (rows, LANES), 1)


def row_iota(rows=BS):
    return lax.broadcasted_iota(jnp.int32, (rows, LANES), 0)


def diagonals(tiles):
    group = lane_iota() // BS
    distance = 1
    while distance < GROUPS:
        odd = (group // distance) % 2 == 1
        tiles = [jnp.where(odd, tiles[(a + distance) % GROUPS], tiles[a]) for a in range(GROUPS)]
        distance *= 2
    return [tiles[(GROUPS - g) % GROUPS] for g in range(GROUPS)]


def turned_by(tile, groups):
    return tile if groups % GROUPS == 0 else pltpu.roll(tile, groups % GROUPS * BS, 1)


def tile_row(block, rows_j, g):
    blocks_j = rows_j // BS
    return (block // blocks_j) * (BS * rows_j) + (block % blocks_j) * BS + (g % BS) * rows_j


def rows_at(start, size):
    return pl.ds(pl.multiple_of(start, BS), size)


def pack_set(rows_j, q, flow, packed):
    groups = flow.shape[0] * BS
    first = q * GROUPS
    count = min(GROUPS, groups - first)

    def one(block, carry):
        tiles = [
            turned_by(flow[g // BS, rows_at(tile_row(block, rows_j, g), BS), :], g - first)
            for g in range(first, first + count)
        ]
        tiles = diagonals(tiles + tiles[:1] * (GROUPS - count))
        for k in range(GROUPS):
            packed[block * GROUPS + k, q * BS : (q + 1) * BS, :] = tiles[k]
        return carry

    lax.fori_loop(0, packed.shape[0] // GROUPS, one, 0, unroll=2)


def gather(capacity, donor, packed, slots, outbound):
    low = lane_iota() < LANES // 2
    tiles = outbound.shape[1] // BS
    fresh = []
    for slot in slots:
        cube = donor[0, slot % capacity, slot // capacity]
        shift = (GROUPS - cube % GROUPS) % GROUPS * BS
        for q in range(tiles):
            held = packed[cube, q * BS : (q + 1) * BS, :]
            tile = pltpu.roll(held, shift, 1)
            if q == tiles - 1:
                folded = pltpu.roll(pltpu.roll(held, BS // 2, 0), (shift + LANES // 2) % LANES, 1)
                tile = jnp.where(low, tile, folded)
            fresh.append((slot, q, tile))
    for slot, q, tile in fresh:
        outbound[slot, q * BS : (q + 1) * BS, :] = tile


def blend(cubes, shifted, weight):
    return (1.0 - weight) * cubes + weight * shifted


def interpolate(capacity, weights, receiver, slots, arrived):
    lane, row = lane_iota(), row_iota()
    tiles = arrived.shape[1] // BS
    held = [arrived[slot, q * BS : (q + 1) * BS, :] for slot in slots for q in range(tiles)]
    fresh = []
    for n, cubes in enumerate(held):
        slot, q = slots[n // tiles], n % tiles
        d, c = slot // capacity, slot % capacity
        shift = receiver[0, c, d] % GROUPS * BS
        if q == tiles - 1:
            unfolded = pltpu.roll(pltpu.roll(cubes, BS // 2, 0), LANES // 2, 1)
            cubes = jnp.where(row < BS // 2, cubes, unfolded)
        after = jnp.where(lane % (BS * BS) >= BS * (BS - 1), cubes, pltpu.roll(cubes, LANES - BS, 1))
        cubes = blend(cubes, after, weights[0, c, d])
        after = jnp.where(row == BS - 1, cubes, pltpu.roll(cubes, BS - 1, 0))
        cubes = blend(cubes, after, weights[1, c, d])
        after = jnp.where(lane % BS == BS - 1, cubes, pltpu.roll(cubes, LANES - 1, 1))
        cubes = blend(cubes, after, weights[2, c, d])
        fresh.append(pltpu.roll(cubes, shift, 1))
    for n, cubes in enumerate(fresh):
        q = n % tiles
        arrived[slots[n // tiles], q * BS : (q + 1) * BS, :] = cubes


def source_of(capacity, slots, receiver, count):
    lane = lane_iota()

    def one(slot, found):
        d, c = slot // capacity, slot % capacity
        target = jnp.where(count[0, d] > c, receiver[0, c, d], -1)
        return jnp.where(lane == target, slot, found)

    return lax.fori_loop(0, slots, one, jnp.full((BS, LANES), -1, jnp.int32), unroll=BATCH)


def unpack_all(rows_j, source, arrived, flow, padded):
    groups = flow.shape[0] * BS
    group = lane_iota() // BS

    def one(block, carry):
        slots = [source[0, block * GROUPS + k] for k in range(GROUPS)]
        owner = jnp.full((BS, LANES), -1, jnp.int32)
        for k in range(GROUPS):
            owner = jnp.where(group == k, slots[k], owner)
        live = owner >= 0
        for first in range(0, groups, GROUPS):
            q = first // GROUPS
            tiles = diagonals(
                [arrived[jnp.maximum(slots[k], 0), q * BS : (q + 1) * BS, :] for k in range(GROUPS)]
            )
            for g in range(first, min(first + GROUPS, groups)):
                row = tile_row(block, rows_j, g)
                fresh = turned_by(tiles[g - first], GROUPS - (g - first))
                kept = flow[g // BS, rows_at(row, BS), :]
                padded[g // BS, rows_at(row + rows_j, BS), :] = jnp.where(live, fresh, kept)
        return carry

    lax.fori_loop(0, flow.shape[1] * flow.shape[2] // BS**3 // GROUPS, one, 0)


def row_of(n, count, lower):
    return jnp.where(lower, n, count - 1 - n)


def gains_of(state):
    older, newer, lead = state
    return lead, -QUARTER * older, (QUARTER * lead - 1.0) * newer, -QUARTER * newer


def meet_factors(near, far):
    f0, s0, f1, s1 = gains_of(near)
    g0, t0, g1, t1 = gains_of(far)
    cross = g1 - t1 * f0
    a11 = 1.0 - t1 * s0 - cross * f1
    a12 = -cross * s1
    a21 = g0 - t0 * f1
    a22 = 1.0 - t0 * s1
    scale = 1.0 / (a11 * a22 - a12 * a21)
    return a22 * scale, a12 * scale, a21 * scale, a11 * scale, t1, cross, t0


def meet(factors, near, far):
    m11, m12, m21, m22, t1, cross, t0 = factors
    r0, r1 = near
    q0, q1 = far
    b1 = q1 - t1 * r0 - cross * r1
    b2 = q0 - t0 * r1
    return b1 * m11 - m12 * b2, m22 * b2 - m21 * b1


def eliminated(pivot, carry):
    older, newer, lead, square = carry
    inverse = 1.0 / (pivot - 0.0625 * older - square)
    gain = QUARTER * lead - 1.0
    lead = gain * inverse
    return inverse, lead, (newer, inverse, lead, gain * gain * inverse)


def begin_factor(older, newer, lead):
    gain = QUARTER * lead - 1.0
    lead = gain * newer
    return older, newer, lead, gain * lead


def invert_rho(direction, rows, stride, spectral, inverse):
    plane = inverse.shape[0] // rows

    def one(row, carry):
        at = rows_at(row * plane, plane)
        if stride is None:
            inverse[at, :] = 1.0 / spectral[direction, at, :]
        else:
            inverse[at, :] = 1.0 / spectral[direction, pl.ds(row, plane, stride=stride), :]
        return carry

    lax.fori_loop(0, rows, one, 0, unroll=2)


def factor_pass(direction, rows, lower, group, paces, inverse, start, u_ref, l_ref, last):
    variables, total, lanes = u_ref.shape
    plane = total // rows
    for first in range(0, variables, group):
        vs = range(first, min(first + group, variables))

        def one(n, carry):
            at = rows_at(row_of(n, rows, lower) * plane, plane)
            ratio = inverse[at, :]
            fresh = []
            for v, held in zip(vs, carry):
                pace = paces[direction * variables + v, :plane, :]
                u, l, held = eliminated(pace * ratio + 2.5, held)
                u_ref[v, at, :] = u
                l_ref[v, at, :] = l
                fresh.append(held)
            return tuple(fresh)

        lax.fori_loop(0, rows, one, tuple(begin_factor(start[v, 0], start[v, 1], start[v, 2]) for v in vs))
    newest = rows_at(row_of(rows - 1, rows, lower) * plane, plane)
    older = rows_at(row_of(rows - 2, rows, lower) * plane, plane)
    for v in range(variables):
        last[v, 0] = u_ref[v, older, :]
        last[v, 1] = u_ref[v, newest, :]
        last[v, 2] = l_ref[v, older, :]


def forward_pass(vs, rows, lower, values, reduced_ref, scale, u_ref, l_ref, gains, start, ends):
    variables, total, lanes = values.shape
    plane = total // rows

    def one(n, carry):
        at = rows_at(row_of(n, rows, lower) * plane, plane)
        fresh = []
        for v, (product, older, newer) in zip(vs, carry):
            value = scale(v, at, values[v, at, :]) + QUARTER * older - product
            reduced = u_ref[v, at, :] * value
            reduced_ref[v, at, :] = reduced
            fresh.append((l_ref[v, at, :] * value, newer, reduced))
        return tuple(fresh)

    begin = tuple(((QUARTER * gains[v, 2] - 1.0) * start[v, 1], start[v, 0], start[v, 1]) for v in vs)
    for v, (product, older, newer) in zip(vs, lax.fori_loop(0, rows, one, begin, unroll=4)):
        ends[v, 0] = older
        ends[v, 1] = newer


def backward_pass(vs, rows, lower, values, u_ref, l_ref, nexts, solved, store):
    variables, total, lanes = values.shape
    plane = total // rows

    def one(step, carry):
        row = row_of(rows - 1 - step, rows, lower)
        at = rows_at(row * plane, plane)
        fresh = []
        for v, (nearer, farther) in zip(vs, carry):
            value = values[v, at, :] + QUARTER * u_ref[v, at, :] * farther - l_ref[v, at, :] * nearer
            store(v, row, at, value)
            fresh.append((value, nearer))
        return tuple(fresh)

    begin = tuple((nexts[v, 0], nexts[v, 1]) for v in vs)
    for v, (nearer, farther) in zip(vs, lax.fori_loop(0, rows, one, begin, unroll=4)):
        if solved is not None:
            solved[v, 0] = nearer
            solved[v, 1] = farther


def residual_rows(rows_i, first, count, padded, spectral, left, paces, inverse, values):
    variables, total, lanes = values.shape
    rows_j = total // rows_i
    lane, row_id = lane_iota(rows_j), row_iota(rows_j)

    def one(row, carry):
        base = row * rows_j
        at = rows_at(base, rows_j)
        rho = [spectral[e, at, :] for e in range(3)]
        ratio = inverse[at, :]
        residual = []
        for v in range(variables):
            center = padded[v, rows_at(base + rows_j, rows_j), :]
            twice = 2.0 * center
            along_i = padded[v, rows_at(base + 2 * rows_j, rows_j), :] + padded[v, at, :] - twice
            after = jnp.where(row_id == rows_j - 1, 0.0, padded[v, pl.ds(base + rows_j + 1, rows_j), :])
            before = jnp.where(row_id == 0, 0.0, padded[v, pl.ds(base + rows_j - 1, rows_j), :])
            along_j = after + before - twice
            after = jnp.where(lane == lanes - 1, 0.0, pltpu.roll(center, lanes - 1, 1))
            before = jnp.where(lane == 0, 0.0, pltpu.roll(center, 1, 1))
            along_k = after + before - twice
            residual.append(rho[0] * along_i + rho[1] * along_j + rho[2] * along_k)
        for v in range(variables):
            total_v = left[v, 0, 0] * residual[0]
            for u in range(1, variables):
                total_v = total_v + left[v, 0, u] * residual[u]
            values[v, at, :] = total_v * (ratio * paces[v, :rows_j, :])
        return carry

    lax.fori_loop(first, first + count, one, 0, unroll=2 if count % 2 == 0 else 1)


def edge_rows(rows_i, halo, spectral, left, paces, inverse, values):
    variables, total, lanes = values.shape
    rows_j = total // rows_i
    for side, first in enumerate((0, rows_j - 1)):
        at = pl.ds(first, rows_i, stride=rows_j)
        rho = spectral[1, at, :] * inverse[at, :]
        parts = [rho * halo[side, u] for u in range(variables)]
        for v in range(variables):
            total_v = left[v, 0, 0] * parts[0]
            for u in range(1, variables):
                total_v = total_v + left[v, 0, u] * parts[u]
            values[v, at, :] = values[v, at, :] + total_v * paces[v, :rows_i, :]


class Line:
    def __init__(self, axis):
        self.axis = axis
        self.members = lax.axis_size(axis)
        self.half = self.members // 2
        self.place = lax.axis_index(axis)
        self.lower = self.place < self.half
        depth = jnp.where(self.lower, self.place, self.members - 1 - self.place)
        self.inner = jnp.where(self.lower, self.place + 1, self.place - 1)
        self.outer = jnp.where(self.lower, self.place - 1, self.place + 1)
        self.middle = depth == self.half - 1
        self.end = depth == 0

    def send(self, source, target, send_sem, recv_sem, device):
        return pltpu.make_async_remote_copy(
            src_ref=source,
            dst_ref=target,
            send_sem=send_sem,
            recv_sem=recv_sem,
            device_id={self.axis: device},
            device_id_type=MESH,
        )

    def sides(self):
        return (self.place > 0, self.place - 1), (self.place < self.members - 1, self.place + 1)


def span(vs):
    return pl.ds(vs[0], len(vs))


class Sweep:
    def __init__(self, line, s, chunks):
        self.line, self.s, self.chunks = line, s, chunks

    def gains_to(self, target, number):
        s = self.s
        return self.line.send(s.last, target, s.gain_sems.at[0], s.gain_sems.at[number], self.line.inner)

    def gains_in(self):
        line, s = self.line, self.s
        if line.half > 1:

            @pl.when(jnp.logical_not(line.end))
            def _():
                self.gains_to(s.gains, 2).wait_recv()

    def gains_out(self):
        line, s = self.line, self.s
        if line.half > 1:

            @pl.when(jnp.logical_not(line.middle))
            def _():
                self.gains_to(s.gains, 2).start()

        @pl.when(line.middle)
        def _():
            self.gains_to(s.far_gains, 1).start()

    def prepare(self):
        line, s = self.line, self.s

        @pl.when(line.middle)
        def _():
            self.gains_to(s.far_gains, 1).wait_recv()
            for v in range(s.last.shape[0]):
                near = [s.last[v, m] for m in range(3)]
                far = [s.far_gains[v, m] for m in range(3)]
                for m, factor in enumerate(meet_factors(near, far)):
                    s.meeting[v, m] = factor

    def part(self, c):
        return span(self.chunks[c]) if c is not None else span(range(self.s.last.shape[0]))

    def inward(self, c):
        s, at = self.s, self.part(c)
        recv = s.sems.at[2 + len(self.chunks) + (c or 0)]
        return self.line.send(s.ends.at[at], s.start.at[at], s.sems.at[0], recv, self.line.inner)

    def across(self, c):
        s, at = self.s, self.part(c)
        recv = s.sems.at[1 + (c or 0)]
        return self.line.send(s.ends.at[at], s.far.at[at], s.sems.at[0], recv, self.line.inner)

    def outward(self, c):
        s, at = self.s, self.part(c)
        recv = s.sems.at[2 + 2 * len(self.chunks) + (c or 0)]
        return self.line.send(s.solved.at[at], s.nexts.at[at], s.sems.at[1 + len(self.chunks)], recv, self.line.outer)

    def start_in(self, c):
        if self.line.half > 1:

            @pl.when(jnp.logical_not(self.line.end))
            def _():
                self.inward(c).wait_recv()

    def ends_out(self, c):
        line = self.line
        if line.half > 1:

            @pl.when(jnp.logical_not(line.middle))
            def _():
                self.inward(c).start()

        @pl.when(line.middle)
        def _():
            self.across(c).start()

    def nexts_in(self, c):
        line, s = self.line, self.s

        @pl.when(line.middle)
        def _():
            self.across(c).wait_recv()
            for v in self.chunks[c]:
                pair = meet(
                    [s.meeting[v, m] for m in range(7)],
                    [s.ends[v, m] for m in range(2)],
                    [s.far[v, m] for m in range(2)],
                )
                s.nexts[v, 0], s.nexts[v, 1] = pair

        if line.half > 1:

            @pl.when(jnp.logical_not(line.middle))
            def _():
                self.outward(c).wait_recv()

    def solved_out(self, c):
        line = self.line
        if line.half > 1:

            @pl.when(jnp.logical_not(line.end))
            def _():
                self.outward(c).start()

    def close(self):
        line = self.line
        self.gains_to(self.s.far_gains, 1).wait_send()
        self.across(None).wait_send()
        if line.half > 1:

            @pl.when(jnp.logical_not(line.end))
            def _():
                self.outward(None).wait_send()

    def clear(self):
        line, s = self.line, self.s

        @pl.when(line.end)
        def _():
            s.gains[...] = jnp.zeros(s.gains.shape, F32)
            s.start[...] = jnp.zeros(s.start.shape, F32)


def step_body(axes, capacity, rows_i, rows_j, chunks, tiles, names, *refs):
    s = types.SimpleNamespace(**dict(zip(names, refs)))
    flow, rho, padded = s.flow, s.rho, s.padded
    variables, total, lanes = flow.shape
    line_i, line_j = Line("ia"), Line("ja")

    def part(letter):
        return types.SimpleNamespace(**{k[2:]: r for k, r in vars(s).items() if k[:2] == letter + "_"})

    si, sj = part("i"), part("j")
    sweep_i, sweep_j = Sweep(line_i, si, chunks), Sweep(line_j, sj, chunks)
    sizes = [lax.axis_size(axis) for axis in axes]
    here = [lax.axis_index(axis) for axis in axes]
    devices = math.prod(sizes)
    slots = devices * capacity

    packed_tiles = s.packed.shape[1] // BS
    fields = []
    for q in range(packed_tiles):
        at = pl.ds(2 * q, min(2, variables - 2 * q))
        fields.append(pltpu.make_async_copy(s.flow_in.at[at], flow.at[at], s.in_sems.at[q]))
    fields.append(pltpu.make_async_copy(s.rho_in, rho, s.in_sems.at[packed_tiles]))
    small = [
        pltpu.make_async_copy(getattr(s, name + "_in"), getattr(s, name), s.small_sems.at[n])
        for n, name in enumerate(("speeds", "left", "right", "donor", "receiver", "count", "weights"))
    ]
    for copy in fields[:-1] + small + fields[-1:]:
        copy.start()

    far_j = sorted(range(sizes[1]), key=lambda d: -min(d, sizes[1] - d))
    rest = devices // sizes[1]

    def peer(offset_j, n, sign):
        off = (n // sizes[2], offset_j, n % sizes[2])
        place = [(h + sign * o + size) % size for h, o, size in zip(here, off, sizes)]
        number = (place[0] * sizes[1] + place[1]) * sizes[2] + place[2]
        return number, dict(zip(axes, place))

    me = (here[0] * sizes[1] + here[1]) * sizes[2] + here[2]
    barrier = pltpu.get_barrier_semaphore()
    with jax.named_scope("greet"):
        for offset_j in far_j:

            def greet(n, carry):
                pl.semaphore_signal(barrier, inc=1, device_id=peer(offset_j, n, 1)[1], device_id_type=MESH)
                return carry

            lax.fori_loop(0 if offset_j else 1, rest, greet, 0)

    with jax.named_scope("pack"):
        for q in range(packed_tiles):
            fields[q].wait()
            pack_set(rows_j, q, flow, s.packed)
    for copy in small:
        copy.wait()
    with jax.named_scope("entered"):
        pl.semaphore_wait(barrier, devices - 1)

    used = variables * BS**3 // LANES

    def cubes(step, to, place, of, count=1):
        def at(device):
            return pl.ds(device * capacity, count * capacity), pl.ds(0, used)

        return pltpu.make_async_remote_copy(
            src_ref=s.outbound.at[at(to)],
            dst_ref=s.arrived.at[at(of)],
            send_sem=s.cube_sems.at[0],
            recv_sem=s.cube_sems.at[1 + step // BATCH],
            device_id=place,
            device_id_type=MESH,
        )

    with jax.named_scope("send_cubes"):
        for m, offset_j in enumerate(far_j):

            def begin(batch, carry, skip=0):
                first = batch * 2 * BATCH
                numbers = [peer(offset_j, first + n, 1)[0] for n in range(2 * BATCH)]
                for c in range(capacity):
                    gather(capacity, s.donor, s.packed, [to * capacity + c for to in numbers], s.outbound)
                for n in range(skip, 2 * BATCH):
                    to, place = peer(offset_j, first + n, 1)
                    cubes(m * rest + first + n, to, place, me).start()
                return carry

            if offset_j == 0:
                begin(0, 0, 1)
            lax.fori_loop(0 if offset_j else 1, rest // (2 * BATCH), begin, 0)
        own = pl.ds(me * capacity, capacity)
        s.arrived[own] = s.outbound[own]

    def pace(n, carry):
        value = jnp.full((BS, LANES), s.speeds[n // variables, 0, n % variables], F32)
        value = 1.0 / value
        for first in range(0, s.paces.shape[1], BS):
            s.paces[n, first : first + BS, :] = value
        return carry

    def factor_j():
        with jax.named_scope("factor_j"):
            sweep_j.gains_in()
            factor_pass(1, rows_j, line_j.lower, 2, s.paces, sj.inverse, sj.gains, sj.u, sj.l, sj.last)
            sweep_j.gains_out()

    with jax.named_scope("prepare"):
        lax.fori_loop(0, 3 * variables, pace, 0)
        for v in range(variables):
            for u in range(variables):
                s.maps[v, u] = jnp.full((BS, LANES), s.right[v, 0, u], F32)
        sweep_i.clear()
        sweep_j.clear()
        fields[-1].wait()
        invert_rho(1, rows_j, rows_j, rho, sj.inverse)
        pl.when(line_j.end)(factor_j)
    with jax.named_scope("factor_i"):
        invert_rho(0, rows_i, None, rho, si.inverse)
        sweep_i.gains_in()
        factor_pass(0, rows_i, line_i.lower, 3, s.paces, si.inverse, si.gains, si.u, si.l, si.last)
        sweep_i.gains_out()
    with jax.named_scope("sources"):
        s.found[...] = source_of(capacity, slots, s.receiver, s.count)
        found = pltpu.make_async_copy(s.found, s.source, s.small_sems.at[0])
        found.start()
    with jax.named_scope("factor_k"):
        factor_k(tiles, s)
    with jax.named_scope("arrivals"):
        for m, offset_j in enumerate(far_j):

            def arrive(batch, carry, count=BATCH):
                first = batch * BATCH
                cubes(m * rest + first, 0, peer(offset_j, first + BATCH - 1, 1)[1], 0, count).wait_recv()
                sources = [peer(offset_j, first + n, -1)[0] for n in range(BATCH)]
                for c in range(capacity):
                    interpolate(capacity, s.weights, s.receiver, [of * capacity + c for of in sources], s.arrived)
                return carry

            if offset_j == 0:
                arrive(0, 0, BATCH - 1)
            lax.fori_loop(0 if offset_j else 1, rest // BATCH, arrive, 0)
    with jax.named_scope("unpack"):
        found.wait()
        unpack_all(rows_j, s.source, s.arrived, flow, padded)

    def halo(line, axis_number, side, device):
        if axis_number == 1:
            source, target = s.edge.at[side], s.halo.at[1 - side]
        else:
            here, there = (rows_j, rows_j + total) if side == 0 else (total, 0)
            source = padded.at[:, pl.ds(here, rows_j), :]
            target = padded.at[:, pl.ds(there, rows_j), :]
        sems = s.halo_sems.at[axis_number * 2 + side]
        return line.send(source, target, sems.at[0], sems.at[1], device)

    borders = ((1, line_j), (0, line_i))
    with jax.named_scope("send_halos"):
        for v in range(variables):
            s.edge[0, v] = padded[v, pl.ds(rows_j, rows_i, stride=rows_j), :]
            s.edge[1, v] = padded[v, pl.ds(2 * rows_j - 1, rows_i, stride=rows_j), :]
        for axis_number, line in borders:
            for side, (there, device) in enumerate(line.sides()):

                @pl.when(there)
                def _():
                    halo(line, axis_number, side, device).start()

    with jax.named_scope("prepare_i"):
        sweep_i.prepare()
    rest_of = (padded, rho, s.left, s.paces, si.inverse, si.values)
    with jax.named_scope("residual"):
        residual_rows(rows_i, 1, rows_i - 2, *rest_of)
    with jax.named_scope("halos"):
        for axis_number, line in borders[::-1]:
            for side, (there, device) in enumerate(line.sides()):

                @pl.when(there)
                def _():
                    halo(line, axis_number, 1 - side, device).wait_recv()

                @pl.when(jnp.logical_not(there))
                def _():
                    if axis_number == 1:
                        s.halo[side] = jnp.zeros(s.halo.shape[1:], F32)
                    else:
                        first = 0 if side == 0 else rows_j + total
                        padded[:, first : first + rows_j, :] = jnp.zeros((variables, rows_j, lanes), F32)
    with jax.named_scope("edges"):
        residual_rows(rows_i, 0, 1, *rest_of)
        residual_rows(rows_i, rows_i - 1, 1, *rest_of)
        edge_rows(rows_i, s.halo, rho, s.left, s.paces, si.inverse, si.values)

    def plain(v, at, value):
        return value

    def scaled(v, at, value):
        return value * (sj.inverse[at, :] * s.paces[variables + v, :rows_i, :])

    def store_turned(v, row, at, value):
        sj.values[v, pl.ds(row, rows_j, stride=rows_i), :] = value

    def store_lines(v, row, at, value):
        s.lines[v, pl.ds(row, rows_i, stride=rows_j), :] = value

    def forward_i(c):
        sweep_i.start_in(c)
        forward_pass(chunks[c], rows_i, line_i.lower, si.values, si.reduced, plain, si.u, si.l, si.gains, si.start, si.ends)
        sweep_i.ends_out(c)

    def back_i(c):
        sweep_i.nexts_in(c)
        solved = si.solved if line_i.half > 1 else None
        backward_pass(chunks[c], rows_i, line_i.lower, si.reduced, si.u, si.l, si.nexts, solved, store_turned)
        sweep_i.solved_out(c)

    def forward_j(c):
        sweep_j.start_in(c)
        forward_pass(chunks[c], rows_j, line_j.lower, sj.values, sj.reduced, scaled, sj.u, sj.l, sj.gains, sj.start, sj.ends)
        sweep_j.ends_out(c)

    def back_j(c):
        sweep_j.nexts_in(c)
        solved = sj.solved if line_j.half > 1 else None
        backward_pass(chunks[c], rows_j, line_j.lower, sj.reduced, sj.u, sj.l, sj.nexts, solved, store_lines)
        sweep_j.solved_out(c)

    numbers = range(len(chunks))
    with jax.named_scope("forward_i"):
        for c in numbers:
            forward_i(c)
    if line_j.half > 1:
        pl.when(jnp.logical_not(line_j.end))(factor_j)
    with jax.named_scope("back_i"):
        for c in numbers:
            back_i(c)
            pl.when(line_j.end)(functools.partial(forward_j, c))
    with jax.named_scope("solve_j"):
        if line_j.half > 1:
            for c in numbers:
                pl.when(jnp.logical_not(line_j.end))(functools.partial(forward_j, c))
        sweep_j.prepare()
        for c in numbers:
            back_j(c)
            for t, vs in enumerate(tiles[:-1]):
                if vs[-1] == chunks[c][-1]:
                    pl.when(line_j.end)(functools.partial(solve_k, t, vs, s))
        for t, vs in enumerate(tiles[:-1]):
            pl.when(jnp.logical_not(line_j.end))(functools.partial(solve_k, t, vs, s))
        solve_k(len(tiles) - 1, tiles[-1], s)

    with jax.named_scope("close"):
        for axis_number, line in borders:
            for side, (there, device) in enumerate(line.sides()):

                @pl.when(there)
                def _():
                    halo(line, axis_number, side, device).wait_send()

        cubes(0, 0, peer(far_j[0], 0, 1)[1], 0, devices - 1).wait_send()
        sweep_i.close()
        sweep_j.close()


def sides_of(lanes, step):
    for k in (step, lanes - 1 - step):
        yield rows_at(k * BS, BS)


def factor_k(chunks, s):
    total, lanes = s.rho.shape[1:]
    variables = s.flow.shape[0]
    quarters = total // LANES
    for q in range(quarters):
        ratio = (1.0 / s.rho[2, q * LANES : (q + 1) * LANES, :]).T
        for c, vs in enumerate(chunks):
            for m, v in enumerate(vs):
                at = pl.ds(m * quarters + q, lanes, stride=BS)
                s.k_ratio[c, at, :] = ratio * s.paces[2 * variables + v, :1, :]
    for c, vs in enumerate(chunks):
        for spare in range(len(vs) * quarters, BS):
            at = pl.ds(spare, lanes, stride=BS)
            s.k_ratio[c, at, :] = jnp.zeros((lanes, lanes), F32)
            s.k_turned[c, at, :] = jnp.zeros((lanes, lanes), F32)
    half = lanes // 2
    s.k_zero[...] = jnp.zeros((BS, lanes), F32)
    zero = s.k_zero[...]
    numbers = range(len(chunks))

    def one(n, carry):
        fresh = []
        for c in numbers:
            for at, held in zip(sides_of(lanes, n), carry[c]):
                u, l, held = eliminated(s.k_ratio[c, at, :] + 2.5, held)
                s.k_u[c, at, :] = u
                s.k_l[c, at, :] = l
                fresh.append(held)
        return tuple(zip(fresh[::2], fresh[1::2]))

    lax.fori_loop(0, half, one, ((begin_factor(zero, zero, zero),) * 2,) * len(chunks))
    for c in numbers:
        pair = []
        for older, newer in zip(sides_of(lanes, half - 2), sides_of(lanes, half - 1)):
            pair.append((s.k_u[c, older, :], s.k_u[c, newer, :], s.k_l[c, older, :]))
        for side in range(2):
            for m, factor in enumerate(meet_factors(pair[side], pair[1 - side])):
                s.k_meeting[c, side, m] = factor


def solve_k(c, vs, s):
    total, lanes = s.rho.shape[1:]
    quarters = total // LANES
    half = lanes // 2
    turned, reduced_ref, values = s.k_turned.at[c], s.k_reduced.at[c], s.k_values.at[c]
    ratio, u_ref, l_ref = s.k_ratio.at[c], s.k_u.at[c], s.k_l.at[c]
    with jax.named_scope("turn_k"):
        for m, v in enumerate(vs):
            for q in range(quarters):
                at = pl.ds(m * quarters + q, lanes, stride=BS)
                turned[at, :] = s.lines[v, q * LANES : (q + 1) * LANES, :].T * ratio[at, :]
    zero = s.k_zero[...]

    def ahead(n, carry):
        fresh = []
        for at, (product, older, newer) in zip(sides_of(lanes, n), carry):
            value = turned[at, :] + QUARTER * older - product
            reduced = u_ref[at, :] * value
            reduced_ref[at, :] = reduced
            fresh.append((l_ref[at, :] * value, newer, reduced))
        return tuple(fresh)

    with jax.named_scope("forward_k"):
        ends = [end[1:] for end in lax.fori_loop(0, half, ahead, ((zero,) * 3,) * 2, unroll=8)]
        nexts = tuple(
            meet([s.k_meeting[c, side, m] for m in range(7)], ends[side], ends[1 - side]) for side in range(2)
        )

    def back(step, carry):
        fresh = []
        for at, (nearer, farther) in zip(sides_of(lanes, half - 1 - step), carry):
            value = reduced_ref[at, :] + QUARTER * u_ref[at, :] * farther - l_ref[at, :] * nearer
            values[at, :] = value
            fresh.append((value, nearer))
        return tuple(fresh)

    with jax.named_scope("back_k"):
        lax.fori_loop(0, half, back, nexts, unroll=8)


def finish(chunks, padded, values, maps, advanced_out, increment_out, advanced, increment, sems):
    variables, total, lanes = advanced.shape
    rows_j = (padded.shape[1] - total) // 2
    quarters = total // LANES
    places = {v: (c, m) for c, vs in enumerate(chunks) for m, v in enumerate(vs)}

    def copies(q):
        at = (pl.ds(0, variables), pl.ds(q * LANES, LANES))
        return [
            pltpu.make_async_copy(source.at[at], target.at[at], sems.at[n, q])
            for n, (source, target) in enumerate(((advanced, advanced_out), (increment, increment_out)))
        ]

    for q in range(quarters):
        first = q * LANES
        solved = []
        for u in range(variables):
            c, m = places[u]
            solved.append(values[c, pl.ds(m * quarters + q, lanes, stride=BS), :])
        for v in range(variables):
            total_v = maps[v, 0, :1, :] * solved[0]
            for u in range(1, variables):
                total_v = total_v + maps[v, u, :1, :] * solved[u]
            piece = total_v.T
            increment[v, first : first + LANES, :] = piece
            advanced[v, first : first + LANES, :] = padded[v, rows_j + first : rows_j + first + LANES, :] + piece
        for copy in copies(q):
            copy.start()
    for q in range(quarters):
        for copy in copies(q):
            copy.wait()


def local(
    flow_state, spectral, wave_speed, left_map, right_map,
    donor_block, receiver_block, fringe_count, fringe_weight,
):
    variables, grids, rows_i, rows_j, rows_k = flow_state.shape
    assert grids == 1 and rows_k == LANES
    total = rows_i * rows_j
    devices, capacity = donor_block.shape[1:]
    slots = devices * capacity
    cube_count = total // (BS * BS) * (rows_k // BS)
    assert cube_count == LANES
    packed_rows = -(-variables * BS // GROUPS) * BS
    together = BS * LANES // total
    axes = ("ia", "ja", "ka")
    chunks = tuple((v,) for v in range(variables))
    tiles = tuple(tuple(range(v, min(v + together, variables))) for v in range(0, variables, together))
    operands = dict(
        flow_in=flow_state.reshape(variables, total, rows_k),
        rho_in=spectral.reshape(3, total, rows_k),
        speeds_in=wave_speed,
        left_in=left_map.transpose(1, 0, 2),
        right_in=right_map.transpose(1, 0, 2),
        donor_in=donor_block.transpose(0, 2, 1),
        receiver_in=receiver_block.transpose(0, 2, 1),
        count_in=fringe_count,
        weights_in=fringe_weight.transpose(0, 1, 3, 2).reshape(3, capacity, devices),
    )
    dma = pltpu.SemaphoreType.DMA

    def held(*dims):
        return pltpu.VMEM(dims, F32)

    scratch = dict(
        flow=held(variables, total, rows_k),
        rho=held(3, total, rows_k),
        lines=held(variables, total, rows_k),
        packed=held(cube_count, packed_rows, LANES),
        outbound=held(slots, packed_rows, LANES),
        arrived=held(slots, packed_rows, LANES),
        found=pltpu.VMEM((BS, LANES), jnp.int32),
        source=pltpu.SMEM((BS, LANES), jnp.int32),
        paces=held(3 * variables, max(rows_i, rows_j), LANES),
        edge=held(2, variables, rows_i, rows_k),
        halo=held(2, variables, rows_i, rows_k),
        in_sems=dma((packed_rows // BS + 1,)),
        small_sems=dma((7,)),
        cube_sems=dma((1 + devices // BATCH,)),
        halo_sems=dma((4, 2)),
    )
    for name in ("speeds", "left", "right", "donor", "receiver", "count", "weights"):
        array = operands[name + "_in"]
        scratch[name] = pltpu.SMEM(array.shape, array.dtype)
    for letter, plane in (("i_", rows_j), ("j_", rows_i)):
        for name in ("u", "l", "values", "reduced"):
            scratch[letter + name] = held(variables, total, rows_k)
        scratch[letter + "inverse"] = held(total, rows_k)
        for name in ("last", "gains", "far_gains"):
            scratch[letter + name] = held(variables, 3, plane, rows_k)
        for name in ("ends", "start", "far", "nexts", "solved"):
            scratch[letter + name] = held(variables, 2, plane, rows_k)
        scratch[letter + "meeting"] = held(variables, 7, plane, rows_k)
        scratch[letter + "gain_sems"] = dma((3,))
        kinds = 3 if lax.axis_size(letter[0] + "a") > 2 else 1
        scratch[letter + "sems"] = dma((kinds * len(chunks) + (2 if kinds > 1 else 1),))
    for name in ("u", "l", "ratio", "turned", "reduced"):
        scratch["k_" + name] = held(len(tiles), rows_k * BS, LANES)
    scratch["k_zero"] = held(BS, LANES)
    scratch["k_meeting"] = held(len(tiles), 2, 7, BS, LANES)

    field = pltpu.HBM((variables, total, rows_k), F32)
    outs = dict(
        padded=pltpu.VMEM((variables, total + 2 * rows_j, rows_k), F32),
        k_values=pltpu.VMEM((len(tiles), rows_k * BS, LANES), F32),
        maps=pltpu.VMEM((variables, variables, BS, LANES), F32),
    )
    names = (*operands, *outs, *scratch)
    moved = sum(a.size * 4 for a in operands.values()) + 2 * variables * total * rows_k * 4
    handed = pl.pallas_call(
        functools.partial(step_body, axes, capacity, rows_i, rows_j, chunks, tiles, names),
        out_shape=list(outs.values()),
        in_specs=[HBM] * len(operands),
        out_specs=[VMEM] * len(outs),
        scratch_shapes=list(scratch.values()),
        compiler_params=pltpu.CompilerParams(
            vmem_limit_bytes=LIMIT, collective_id=0, has_side_effects=True
        ),
        cost_estimate=pl.CostEstimate(flops=60_000_000, bytes_accessed=moved, transcendentals=0),
    )(*(in_hbm(a) for a in operands.values()))
    advanced, increment = pl.pallas_call(
        functools.partial(finish, tiles),
        out_shape=[field, field],
        in_specs=[VMEM] * len(outs),
        out_specs=[HBM] * 2,
        scratch_shapes=[
            held(variables, total, rows_k),
            held(variables, total, rows_k),
            dma((2, total // LANES)),
        ],
        compiler_params=pltpu.CompilerParams(vmem_limit_bytes=16 << 20),
        cost_estimate=pl.CostEstimate(flops=6_000_000, bytes_accessed=moved, transcendentals=0),
    )(*handed)
    return advanced.reshape(flow_state.shape), increment.reshape(flow_state.shape)


def solution(mesh):
    return jax.shard_map(
        local,
        mesh=mesh,
        in_specs=(
            P(None, "ka", "ia", "ja", None),
            P(None, "ka", "ia", "ja", None),
            P(None, "ka", None),
            P("ka", None, None),
            P("ka", None, None),
            P(("ia", "ja", "ka"), None, None),
            P(("ia", "ja", "ka"), None, None),
            P(("ia", "ja", "ka"), None),
            P(None, ("ia", "ja", "ka"), None, None),
        ),
        out_specs=(P(None, "ka", "ia", "ja", None), P(None, "ka", "ia", "ja", None)),
        check_vma=False,
    )
```

```python
import functools
import math
import types

import jax
import jax.numpy as jnp
from jax import lax
from jax.experimental import pallas as pl
from jax.experimental.pallas import tpu as pltpu
from jax.sharding import PartitionSpec as P

BS = 8
LANES = 128
GROUPS = LANES // BS
QUARTER = 0.25
BATCH = 8
PARTS = 2
LIMIT = 44 << 20
VMEM = pl.BlockSpec(memory_space=pltpu.VMEM)
HBM = pl.BlockSpec(memory_space=pltpu.HBM)
MESH = pl.DeviceIdType.MESH
F32 = jnp.float32


def in_hbm(array):
    return pltpu.with_memory_space_constraint(array, pltpu.HBM)


def lane_iota(rows=BS):
    return lax.broadcasted_iota(jnp.int32, (rows, LANES), 1)


def row_iota(rows=BS):
    return lax.broadcasted_iota(jnp.int32, (rows, LANES), 0)


def diagonals(tiles):
    group = lane_iota() // BS
    distance = 1
    while distance < GROUPS:
        odd = (group // distance) % 2 == 1
        tiles = [jnp.where(odd, tiles[(a + distance) % GROUPS], tiles[a]) for a in range(GROUPS)]
        distance *= 2
    return [tiles[(GROUPS - g) % GROUPS] for g in range(GROUPS)]


def turned_by(tile, groups):
    return tile if groups % GROUPS == 0 else pltpu.roll(tile, groups % GROUPS * BS, 1)


def tile_row(block, rows_j, g):
    blocks_j = rows_j // BS
    return (block // blocks_j) * (BS * rows_j) + (block % blocks_j) * BS + (g % BS) * rows_j


def rows_at(start, size):
    return pl.ds(pl.multiple_of(start, BS), size)


def pack_set(rows_j, q, flow, packed):
    groups = flow.shape[0] * BS
    first = q * GROUPS
    count = min(GROUPS, groups - first)

    def one(block, carry):
        tiles = [
            turned_by(flow[g // BS, rows_at(tile_row(block, rows_j, g), BS), :], g - first)
            for g in range(first, first + count)
        ]
        tiles = diagonals(tiles + tiles[:1] * (GROUPS - count))
        for k in range(GROUPS):
            packed[block * GROUPS + k, q * BS : (q + 1) * BS, :] = tiles[k]
        return carry

    lax.fori_loop(0, packed.shape[0] // GROUPS, one, 0, unroll=4)


def gather(capacity, donor, packed, slots, outbound):
    low = lane_iota() < LANES // 2
    tiles = outbound.shape[1] // BS
    fresh = []
    for slot in slots:
        cube = donor[0, slot % capacity, slot // capacity]
        shift = (GROUPS - cube % GROUPS) % GROUPS * BS
        for q in range(tiles):
            held = packed[cube, q * BS : (q + 1) * BS, :]
            tile = pltpu.roll(held, shift, 1)
            if q == tiles - 1:
                folded = pltpu.roll(pltpu.roll(held, BS // 2, 0), (shift + LANES // 2) % LANES, 1)
                tile = jnp.where(low, tile, folded)
            fresh.append((slot, q, tile))
    for slot, q, tile in fresh:
        outbound[slot, q * BS : (q + 1) * BS, :] = tile


def blend(cubes, shifted, weight):
    return (1.0 - weight) * cubes + weight * shifted


def interpolate(capacity, weights, receiver, slots, arrived):
    lane, row = lane_iota(), row_iota()
    tiles = arrived.shape[1] // BS
    held = [arrived[slot, q * BS : (q + 1) * BS, :] for slot in slots for q in range(tiles)]
    fresh = []
    for n, cubes in enumerate(held):
        slot, q = slots[n // tiles], n % tiles
        d, c = slot // capacity, slot % capacity
        shift = receiver[0, c, d] % GROUPS * BS
        if q == tiles - 1:
            unfolded = pltpu.roll(pltpu.roll(cubes, BS // 2, 0), LANES // 2, 1)
            cubes = jnp.where(row < BS // 2, cubes, unfolded)
        after = jnp.where(lane % (BS * BS) >= BS * (BS - 1), cubes, pltpu.roll(cubes, LANES - BS, 1))
        cubes = blend(cubes, after, weights[0, c, d])
        after = jnp.where(row == BS - 1, cubes, pltpu.roll(cubes, BS - 1, 0))
        cubes = blend(cubes, after, weights[1, c, d])
        after = jnp.where(lane % BS == BS - 1, cubes, pltpu.roll(cubes, LANES - 1, 1))
        cubes = blend(cubes, after, weights[2, c, d])
        fresh.append(pltpu.roll(cubes, shift, 1))
    for n, cubes in enumerate(fresh):
        q = n % tiles
        arrived[slots[n // tiles], q * BS : (q + 1) * BS, :] = cubes


def source_of(capacity, slots, receiver, count):
    lane = lane_iota()

    def one(slot, found):
        d, c = slot // capacity, slot % capacity
        target = jnp.where(count[0, d] > c, receiver[0, c, d], -1)
        return jnp.where(lane == target, slot, found)

    return lax.fori_loop(0, slots, one, jnp.full((BS, LANES), -1, jnp.int32), unroll=BATCH)


def unpack_part(rows_j, part, source, arrived, flow, padded):
    groups = flow.shape[0] * BS
    group = lane_iota() // BS

    def one(block, carry):
        slots = [source[0, block * GROUPS + k] for k in range(GROUPS)]
        owner = jnp.full((BS, LANES), -1, jnp.int32)
        for k in range(GROUPS):
            owner = jnp.where(group == k, slots[k], owner)
        live = owner >= 0
        for first in range(0, groups, GROUPS):
            q = first // GROUPS
            tiles = diagonals(
                [arrived[jnp.maximum(slots[k], 0), q * BS : (q + 1) * BS, :] for k in range(GROUPS)]
            )
            for g in range(first, min(first + GROUPS, groups)):
                row = tile_row(block, rows_j, g)
                fresh = turned_by(tiles[g - first], GROUPS - (g - first))
                kept = flow[g // BS, rows_at(row, BS), :]
                padded[g // BS, rows_at(row + rows_j, BS), :] = jnp.where(live, fresh, kept)
        return carry

    count = flow.shape[1] * flow.shape[2] // BS**3 // GROUPS // PARTS
    lax.fori_loop(part * count, (part + 1) * count, one, 0, unroll=2)


def row_of(n, count, lower):
    return jnp.where(lower, n, count - 1 - n)


def gains_of(state):
    older, newer, lead = state
    return lead, -QUARTER * older, (QUARTER * lead - 1.0) * newer, -QUARTER * newer


def meet_factors(near, far):
    f0, s0, f1, s1 = gains_of(near)
    g0, t0, g1, t1 = gains_of(far)
    cross = g1 - t1 * f0
    a11 = 1.0 - t1 * s0 - cross * f1
    a12 = -cross * s1
    a21 = g0 - t0 * f1
    a22 = 1.0 - t0 * s1
    scale = 1.0 / (a11 * a22 - a12 * a21)
    return a22 * scale, a12 * scale, a21 * scale, a11 * scale, t1, cross, t0


def meet(factors, near, far):
    m11, m12, m21, m22, t1, cross, t0 = factors
    r0, r1 = near
    q0, q1 = far
    b1 = q1 - t1 * r0 - cross * r1
    b2 = q0 - t0 * r1
    return b1 * m11 - m12 * b2, m22 * b2 - m21 * b1


def eliminated(pivot, carry):
    older, newer, lead, square = carry
    inverse = 1.0 / (pivot - 0.0625 * older - square)
    gain = QUARTER * lead - 1.0
    lead = gain * inverse
    return inverse, lead, (newer, inverse, lead, gain * gain * inverse)


def begin_factor(older, newer, lead):
    gain = QUARTER * lead - 1.0
    lead = gain * newer
    return older, newer, lead, gain * lead


def invert_rho(direction, rows, stride, spectral, inverse):
    plane = inverse.shape[0] // rows

    def one(row, carry):
        at = rows_at(row * plane, plane)
        if stride is None:
            inverse[at, :] = 1.0 / spectral[direction, at, :]
        else:
            inverse[at, :] = 1.0 / spectral[direction, pl.ds(row, plane, stride=stride), :]
        return carry

    lax.fori_loop(0, rows, one, 0, unroll=2)


def factor_pass(direction, rows, lower, group, paces, inverse, start, u_ref, l_ref, last):
    variables, total, lanes = u_ref.shape
    plane = total // rows
    for first in range(0, variables, group):
        vs = range(first, min(first + group, variables))

        def one(n, carry):
            at = rows_at(row_of(n, rows, lower) * plane, plane)
            ratio = inverse[at, :]
            fresh = []
            for v, held in zip(vs, carry):
                pace = paces[direction * variables + v, :plane, :]
                u, l, held = eliminated(pace * ratio + 2.5, held)
                u_ref[v, at, :] = u
                l_ref[v, at, :] = l
                fresh.append(held)
            return tuple(fresh)

        lax.fori_loop(0, rows, one, tuple(begin_factor(start[v, 0], start[v, 1], start[v, 2]) for v in vs))
    newest = rows_at(row_of(rows - 1, rows, lower) * plane, plane)
    older = rows_at(row_of(rows - 2, rows, lower) * plane, plane)
    for v in range(variables):
        last[v, 0] = u_ref[v, older, :]
        last[v, 1] = u_ref[v, newest, :]
        last[v, 2] = l_ref[v, older, :]


def forward_pass(vs, rows, lower, values, reduced_ref, scale, u_ref, l_ref, gains, start, ends):
    variables, total, lanes = values.shape
    plane = total // rows

    def one(n, carry):
        at = rows_at(row_of(n, rows, lower) * plane, plane)
        fresh = []
        for v, (product, older, newer) in zip(vs, carry):
            value = scale(v, at, values[v, at, :]) + QUARTER * older - product
            reduced = u_ref[v, at, :] * value
            reduced_ref[v, at, :] = reduced
            fresh.append((l_ref[v, at, :] * value, newer, reduced))
        return tuple(fresh)

    begin = tuple(((QUARTER * gains[v, 2] - 1.0) * start[v, 1], start[v, 0], start[v, 1]) for v in vs)
    for v, (product, older, newer) in zip(vs, lax.fori_loop(0, rows, one, begin, unroll=4)):
        ends[v, 0] = older
        ends[v, 1] = newer


def backward_pass(vs, rows, lower, values, u_ref, l_ref, nexts, solved, store):
    variables, total, lanes = values.shape
    plane = total // rows

    def one(step, carry):
        row = row_of(rows - 1 - step, rows, lower)
        at = rows_at(row * plane, plane)
        fresh = []
        for v, (nearer, farther) in zip(vs, carry):
            value = values[v, at, :] + QUARTER * u_ref[v, at, :] * farther - l_ref[v, at, :] * nearer
            store(v, row, at, value)
            fresh.append((value, nearer))
        return tuple(fresh)

    begin = tuple((nexts[v, 0], nexts[v, 1]) for v in vs)
    for v, (nearer, farther) in zip(vs, lax.fori_loop(0, rows, one, begin, unroll=4)):
        if solved is not None:
            solved[v, 0] = nearer
            solved[v, 1] = farther


def residual_rows(rows_i, first, count, padded, spectral, left, paces, inverse, values):
    variables, total, lanes = values.shape
    rows_j = total // rows_i
    lane, row_id = lane_iota(rows_j), row_iota(rows_j)

    def one(row, carry):
        base = row * rows_j
        at = rows_at(base, rows_j)
        rho = [spectral[e, at, :] for e in range(3)]
        ratio = inverse[at, :]
        residual = []
        for v in range(variables):
            center = padded[v, rows_at(base + rows_j, rows_j), :]
            twice = 2.0 * center
            along_i = padded[v, rows_at(base + 2 * rows_j, rows_j), :] + padded[v, at, :] - twice
            after = jnp.where(row_id == rows_j - 1, 0.0, padded[v, pl.ds(base + rows_j + 1, rows_j), :])
            before = jnp.where(row_id == 0, 0.0, padded[v, pl.ds(base + rows_j - 1, rows_j), :])
            along_j = after + before - twice
            after = jnp.where(lane == lanes - 1, 0.0, pltpu.roll(center, lanes - 1, 1))
            before = jnp.where(lane == 0, 0.0, pltpu.roll(center, 1, 1))
            along_k = after + before - twice
            residual.append(rho[0] * along_i + rho[1] * along_j + rho[2] * along_k)
        for v in range(variables):
            total_v = left[v, 0, 0] * residual[0]
            for u in range(1, variables):
                total_v = total_v + left[v, 0, u] * residual[u]
            values[v, at, :] = total_v * (ratio * paces[v, :rows_j, :])
        return carry

    lax.fori_loop(first, first + count, one, 0, unroll=2 if count % 2 == 0 else 1)


def edge_rows(rows_i, halo, spectral, left, paces, inverse, values):
    variables, total, lanes = values.shape
    rows_j = total // rows_i
    size = rows_i // PARTS
    for part in range(PARTS):
        for side, first in enumerate((0, rows_j - 1)):
            at = pl.ds(part * size * rows_j + first, size, stride=rows_j)
            rho = spectral[1, at, :] * inverse[at, :]
            parts = [rho * halo[part, side, u] for u in range(variables)]
            for v in range(variables):
                total_v = left[v, 0, 0] * parts[0]
                for u in range(1, variables):
                    total_v = total_v + left[v, 0, u] * parts[u]
                values[v, at, :] = values[v, at, :] + total_v * paces[v, :size, :]


class Line:
    def __init__(self, axis):
        self.axis = axis
        self.members = lax.axis_size(axis)
        self.half = self.members // 2
        self.place = lax.axis_index(axis)
        self.lower = self.place < self.half
        depth = jnp.where(self.lower, self.place, self.members - 1 - self.place)
        self.inner = jnp.where(self.lower, self.place + 1, self.place - 1)
        self.outer = jnp.where(self.lower, self.place - 1, self.place + 1)
        self.middle = depth == self.half - 1
        self.end = depth == 0

    def send(self, source, target, send_sem, recv_sem, device):
        return pltpu.make_async_remote_copy(
            src_ref=source,
            dst_ref=target,
            send_sem=send_sem,
            recv_sem=recv_sem,
            device_id={self.axis: device},
            device_id_type=MESH,
        )

    def sides(self):
        return (self.place > 0, self.place - 1), (self.place < self.members - 1, self.place + 1)


def span(vs):
    return pl.ds(vs[0], len(vs))


class Sweep:
    def __init__(self, line, s, chunks, sent):
        self.line, self.s, self.chunks, self.sent = line, s, chunks, sent

    def gains_to(self, target, number):
        s = self.s
        return self.line.send(s.last, target, self.sent[0], s.gain_sems.at[number], self.line.inner)

    def gains_in(self):
        line, s = self.line, self.s
        if line.half > 1:

            @pl.when(jnp.logical_not(line.end))
            def _():
                self.gains_to(s.gains, 1).wait_recv()

    def gains_out(self):
        line, s = self.line, self.s
        if line.half > 1:

            @pl.when(jnp.logical_not(line.middle))
            def _():
                self.gains_to(s.gains, 1).start()

        @pl.when(line.middle)
        def _():
            self.gains_to(s.far_gains, 0).start()

    def prepare(self):
        line, s = self.line, self.s

        @pl.when(line.middle)
        def _():
            self.gains_to(s.far_gains, 0).wait_recv()
            for v in range(s.last.shape[0]):
                near = [s.last[v, m] for m in range(3)]
                far = [s.far_gains[v, m] for m in range(3)]
                for m, factor in enumerate(meet_factors(near, far)):
                    s.meeting[v, m] = factor

    def part(self, c):
        return span(self.chunks[c]) if c is not None else span(range(self.s.last.shape[0]))

    def inward(self, c):
        s, at = self.s, self.part(c)
        recv = s.sems.at[len(self.chunks) + (c or 0)]
        return self.line.send(s.ends.at[at], s.start.at[at], self.sent[1], recv, self.line.inner)

    def across(self, c):
        s, at = self.s, self.part(c)
        recv = s.sems.at[c or 0]
        return self.line.send(s.ends.at[at], s.far.at[at], self.sent[1], recv, self.line.inner)

    def outward(self, c):
        s, at = self.s, self.part(c)
        recv = s.sems.at[2 * len(self.chunks) + (c or 0)]
        return self.line.send(s.solved.at[at], s.nexts.at[at], self.sent[2], recv, self.line.outer)

    def start_in(self, c):
        if self.line.half > 1:

            @pl.when(jnp.logical_not(self.line.end))
            def _():
                self.inward(c).wait_recv()

    def ends_out(self, c):
        line = self.line
        if line.half > 1:

            @pl.when(jnp.logical_not(line.middle))
            def _():
                self.inward(c).start()

        @pl.when(line.middle)
        def _():
            self.across(c).start()

    def nexts_in(self, c):
        line, s = self.line, self.s

        @pl.when(line.middle)
        def _():
            self.across(c).wait_recv()
            for v in self.chunks[c]:
                pair = meet(
                    [s.meeting[v, m] for m in range(7)],
                    [s.ends[v, m] for m in range(2)],
                    [s.far[v, m] for m in range(2)],
                )
                s.nexts[v, 0], s.nexts[v, 1] = pair

        if line.half > 1:

            @pl.when(jnp.logical_not(line.middle))
            def _():
                self.outward(c).wait_recv()

    def solved_out(self, c):
        line = self.line
        if line.half > 1:

            @pl.when(jnp.logical_not(line.end))
            def _():
                self.outward(c).start()

    def close(self):
        line = self.line
        self.gains_to(self.s.far_gains, 0).wait_send()
        self.across(None).wait_send()
        if line.half > 1:

            @pl.when(jnp.logical_not(line.end))
            def _():
                self.outward(None).wait_send()

    def clear(self):
        line, s = self.line, self.s

        @pl.when(line.end)
        def _():
            s.gains[...] = jnp.zeros(s.gains.shape, F32)
            s.start[...] = jnp.zeros(s.start.shape, F32)


def step_body(axes, capacity, rows_i, rows_j, chunks, tiles, names, *refs):
    s = types.SimpleNamespace(**dict(zip(names, refs)))
    flow, rho, padded = s.flow, s.rho, s.padded
    variables, total, lanes = flow.shape
    line_i, line_j = Line("ia"), Line("ja")

    def part(letter):
        return types.SimpleNamespace(**{k[2:]: r for k, r in vars(s).items() if k[:2] == letter + "_"})

    si, sj = part("i"), part("j")
    first = 4 + 2 * PARTS
    sweep_i, sweep_j = (
        Sweep(line, part, chunks, [s.own_sems.at[first + 3 * n + m] for m in range(3)])
        for n, (line, part) in enumerate(((line_i, si), (line_j, sj)))
    )
    sizes = [lax.axis_size(axis) for axis in axes]
    here = [lax.axis_index(axis) for axis in axes]
    devices = math.prod(sizes)
    slots = devices * capacity

    packed_tiles = s.packed.shape[1] // BS
    fields = []
    for q in range(packed_tiles):
        at = pl.ds(2 * q, min(2, variables - 2 * q))
        fields.append(pltpu.make_async_copy(s.flow_in.at[at], flow.at[at], s.own_sems.at[q]))
    fields.append(pltpu.make_async_copy(s.rho_in, rho, s.own_sems.at[packed_tiles]))
    small = [
        pltpu.make_async_copy(getattr(s, name + "_in"), getattr(s, name), s.own_sems.at[packed_tiles + 1 + n])
        for n, name in enumerate(("speeds", "left", "right", "donor", "receiver", "count", "weights"))
    ]
    for copy in fields[:-1] + small + fields[-1:]:
        copy.start()

    far_j = sorted(range(sizes[1]), key=lambda d: -min(d, sizes[1] - d))
    rest = devices // sizes[1]

    def peer(offset_j, n, sign):
        off = (n // sizes[2], offset_j, n % sizes[2])
        place = [(h + sign * o + size) % size for h, o, size in zip(here, off, sizes)]
        number = (place[0] * sizes[1] + place[1]) * sizes[2] + place[2]
        return number, dict(zip(axes, place))

    around = [[(h + o) % size for o in range(size)] for h, size in zip(here, sizes)]
    me = (here[0] * sizes[1] + here[1]) * sizes[2] + here[2]
    barrier = pltpu.get_barrier_semaphore()
    with jax.named_scope("greet"):
        for offset_j in far_j:
            for n in range(0 if offset_j else 1, rest):
                place = around[0][n // sizes[2]], around[1][offset_j], around[2][n % sizes[2]]
                pl.semaphore_signal(barrier, inc=1, device_id=dict(zip(axes, place)), device_id_type=MESH)

    with jax.named_scope("pack"):
        for q in range(packed_tiles):
            with jax.named_scope(f"flow{q}"):
                fields[q].wait()
            with jax.named_scope(f"pack{q}"):
                pack_set(rows_j, q, flow, s.packed)
    for copy in small:
        copy.wait()
    with jax.named_scope("entered"):
        pl.semaphore_wait(barrier, devices - 1)

    used = variables * BS**3 // LANES

    def cubes(step, to, place, of, count=1):
        def at(device):
            return pl.ds(device * capacity, count * capacity), pl.ds(0, used)

        return pltpu.make_async_remote_copy(
            src_ref=s.outbound.at[at(to)],
            dst_ref=s.arrived.at[at(of)],
            send_sem=s.own_sems.at[1],
            recv_sem=s.cube_sems.at[step // BATCH],
            device_id=place,
            device_id_type=MESH,
        )

    with jax.named_scope("send_cubes"):
        for m, offset_j in enumerate(far_j):

            def begin(batch, carry, skip=0):
                first = batch * BATCH
                numbers = [peer(offset_j, first + n, 1)[0] for n in range(BATCH)]
                for c in range(capacity):
                    gather(capacity, s.donor, s.packed, [to * capacity + c for to in numbers], s.outbound)
                for n in range(skip, BATCH):
                    to, place = peer(offset_j, first + n, 1)
                    cubes(m * rest + first + n, to, place, me).start()
                return carry

            if offset_j == 0:
                begin(0, 0, 1)
            lax.fori_loop(0 if offset_j else 1, rest // BATCH, begin, 0)
        own = pl.ds(me * capacity, capacity)
        s.arrived[own] = s.outbound[own]

    def pace(n, carry):
        value = jnp.full((BS, LANES), s.speeds[n // variables, 0, n % variables], F32)
        value = 1.0 / value
        for first in range(0, s.paces.shape[1], BS):
            s.paces[n, first : first + BS, :] = value
        return carry

    def factor_j():
        with jax.named_scope("factor_j"):
            sweep_j.gains_in()
            factor_pass(1, rows_j, line_j.lower, 2, s.paces, sj.inverse, sj.gains, sj.u, sj.l, sj.last)
            sweep_j.gains_out()

    with jax.named_scope("prepare"):
        lax.fori_loop(0, 3 * variables, pace, 0)
        for v in range(variables):
            for u in range(variables):
                s.maps[v, u] = jnp.full((BS, LANES), s.right[v, 0, u], F32)
        sweep_i.clear()
        sweep_j.clear()
        fields[-1].wait()
        invert_rho(1, rows_j, rows_j, rho, sj.inverse)
        pl.when(line_j.end)(factor_j)
    with jax.named_scope("factor_i"):
        invert_rho(0, rows_i, None, rho, si.inverse)
        sweep_i.gains_in()
        factor_pass(0, rows_i, line_i.lower, 3, s.paces, si.inverse, si.gains, si.u, si.l, si.last)
        sweep_i.gains_out()
    with jax.named_scope("sources"):
        s.found[...] = source_of(capacity, slots, s.receiver, s.count)
        found = pltpu.make_async_copy(s.found, s.source, s.own_sems.at[0])
        found.start()
    with jax.named_scope("factor_k"):
        factor_k(tiles, s)
    with jax.named_scope("arrivals"):
        for m, offset_j in list(enumerate(far_j))[::-1]:

            def arrive(batch, carry, count=BATCH):
                first = batch * BATCH
                cubes(m * rest + first, 0, peer(offset_j, first + BATCH - 1, 1)[1], 0, count).wait_recv()
                sources = [peer(offset_j, first + n, -1)[0] for n in range(BATCH)]
                for c in range(capacity):
                    interpolate(capacity, s.weights, s.receiver, [of * capacity + c for of in sources], s.arrived)
                return carry

            if offset_j == 0:
                arrive(0, 0, BATCH - 1)
            lax.fori_loop(0 if offset_j else 1, rest // BATCH, arrive, 0)
    rows_part = rows_i // PARTS

    def halo_i(side, device):
        mine, other = (rows_j, rows_j + total) if side == 0 else (total, 0)
        source = padded.at[:, pl.ds(mine, rows_j), :]
        target = padded.at[:, pl.ds(other, rows_j), :]
        return line_i.send(source, target, s.own_sems.at[2 + side], s.halo_sems.at[side], device)

    def halo_j(side, device, part):
        n = 2 + 2 * part + side
        source, target = s.edge.at[part, side], s.halo.at[part, 1 - side]
        return line_j.send(source, target, s.own_sems.at[2 + n], s.halo_sems.at[n], device)

    def at_borders(line, act, otherwise=None):
        for side, (there, device) in enumerate(line.sides()):
            pl.when(there)(functools.partial(act, side, device))
            if otherwise is not None:
                pl.when(jnp.logical_not(there))(functools.partial(otherwise, side))

    for part in range(PARTS):
        with jax.named_scope("unpack"):
            if part == 0:
                found.wait()
            unpack_part(rows_j, part, s.source, s.arrived, flow, padded)
        with jax.named_scope("send_halos"):
            for side, row in enumerate((rows_j, 2 * rows_j - 1)):
                at = pl.ds(row + part * rows_part * rows_j, rows_part, stride=rows_j)
                for v in range(variables):
                    s.edge[part, side, v] = padded[v, at, :]
            at_borders(line_j, lambda side, device: halo_j(side, device, part).start())
    with jax.named_scope("send_halos"):
        at_borders(line_i, lambda side, device: halo_i(side, device).start())

    rest_of = (padded, rho, s.left, s.paces, si.inverse, si.values)
    with jax.named_scope("residual"):
        residual_rows(rows_i, 1, rows_i - 2, *rest_of)
    if line_j.half > 1:
        pl.when(jnp.logical_not(line_j.end))(factor_j)
    with jax.named_scope("halos"):

        def no_i(side):
            first = 0 if side == 0 else rows_j + total
            padded[:, first : first + rows_j, :] = jnp.zeros((variables, rows_j, lanes), F32)

        def no_j(part, side):
            s.halo[part, side] = jnp.zeros(s.halo.shape[2:], F32)

        at_borders(line_i, lambda side, device: halo_i(1 - side, device).wait_recv(), no_i)
        for part in range(PARTS):
            at_borders(
                line_j, lambda side, device: halo_j(1 - side, device, part).wait_recv(), functools.partial(no_j, part)
            )
    with jax.named_scope("edges"):
        residual_rows(rows_i, 0, 1, *rest_of)
        residual_rows(rows_i, rows_i - 1, 1, *rest_of)
        edge_rows(rows_i, s.halo, rho, s.left, s.paces, si.inverse, si.values)

    def plain(v, at, value):
        return value

    def scaled(v, at, value):
        return value * (sj.inverse[at, :] * s.paces[variables + v, :rows_i, :])

    def store_turned(v, row, at, value):
        sj.values[v, pl.ds(row, rows_j, stride=rows_i), :] = value

    def store_lines(v, row, at, value):
        s.lines[v, pl.ds(row, rows_i, stride=rows_j), :] = value

    def forward_i(c):
        sweep_i.start_in(c)
        forward_pass(chunks[c], rows_i, line_i.lower, si.values, si.reduced, plain, si.u, si.l, si.gains, si.start, si.ends)
        sweep_i.ends_out(c)

    def back_i(c):
        sweep_i.nexts_in(c)
        solved = si.solved if line_i.half > 1 else None
        backward_pass(chunks[c], rows_i, line_i.lower, si.reduced, si.u, si.l, si.nexts, solved, store_turned)
        sweep_i.solved_out(c)

    def forward_j(c):
        sweep_j.start_in(c)
        forward_pass(chunks[c], rows_j, line_j.lower, sj.values, sj.reduced, scaled, sj.u, sj.l, sj.gains, sj.start, sj.ends)
        sweep_j.ends_out(c)

    def back_j(c):
        sweep_j.nexts_in(c)
        solved = sj.solved if line_j.half > 1 else None
        backward_pass(chunks[c], rows_j, line_j.lower, sj.reduced, sj.u, sj.l, sj.nexts, solved, store_lines)
        sweep_j.solved_out(c)

    numbers = range(len(chunks))
    with jax.named_scope("forward_i"):
        for c in numbers:
            forward_i(c)
    with jax.named_scope("prepare_i"):
        sweep_i.prepare()
    with jax.named_scope("back_i"):
        for c in numbers:
            back_i(c)
            pl.when(line_j.end)(functools.partial(forward_j, c))
    with jax.named_scope("solve_j"):
        if line_j.half > 1:
            for c in numbers:
                pl.when(jnp.logical_not(line_j.end))(functools.partial(forward_j, c))
        sweep_j.prepare()
        for c in numbers:
            back_j(c)
            for t, vs in enumerate(tiles[:-1]):
                if vs[-1] == chunks[c][-1]:
                    pl.when(line_j.end)(functools.partial(solve_k, t, vs, s))
        for t, vs in enumerate(tiles[:-1]):
            pl.when(jnp.logical_not(line_j.end))(functools.partial(solve_k, t, vs, s))
        solve_k(len(tiles) - 1, tiles[-1], s)

    with jax.named_scope("close"):
        at_borders(line_i, lambda side, device: halo_i(side, device).wait_send())
        for part in range(PARTS):
            at_borders(line_j, lambda side, device: halo_j(side, device, part).wait_send())
        cubes(0, 0, peer(far_j[0], 0, 1)[1], 0, devices - 1).wait_send()
        sweep_i.close()
        sweep_j.close()


def sides_of(lanes, step):
    for k in (step, lanes - 1 - step):
        yield rows_at(k * BS, BS)


def factor_k(chunks, s):
    total, lanes = s.rho.shape[1:]
    variables = s.flow.shape[0]
    quarters = total // LANES
    for q in range(quarters):
        ratio = (1.0 / s.rho[2, q * LANES : (q + 1) * LANES, :]).T
        for c, vs in enumerate(chunks):
            for m, v in enumerate(vs):
                at = pl.ds(m * quarters + q, lanes, stride=BS)
                s.k_ratio[c, at, :] = ratio * s.paces[2 * variables + v, :1, :]
    for c, vs in enumerate(chunks):
        for spare in range(len(vs) * quarters, BS):
            at = pl.ds(spare, lanes, stride=BS)
            s.k_ratio[c, at, :] = jnp.zeros((lanes, lanes), F32)
            s.k_turned[c, at, :] = jnp.zeros((lanes, lanes), F32)
    half = lanes // 2
    s.k_zero[...] = jnp.zeros((BS, lanes), F32)
    zero = s.k_zero[...]
    numbers = range(len(chunks))

    def one(n, carry):
        fresh = []
        for c in numbers:
            for at, held in zip(sides_of(lanes, n), carry[c]):
                u, l, held = eliminated(s.k_ratio[c, at, :] + 2.5, held)
                s.k_u[c, at, :] = u
                s.k_l[c, at, :] = l
                fresh.append(held)
        return tuple(zip(fresh[::2], fresh[1::2]))

    lax.fori_loop(0, half, one, ((begin_factor(zero, zero, zero),) * 2,) * len(chunks))
    for c in numbers:
        pair = []
        for older, newer in zip(sides_of(lanes, half - 2), sides_of(lanes, half - 1)):
            pair.append((s.k_u[c, older, :], s.k_u[c, newer, :], s.k_l[c, older, :]))
        for side in range(2):
            for m, factor in enumerate(meet_factors(pair[side], pair[1 - side])):
                s.k_meeting[c, side, m] = factor


def solve_k(c, vs, s):
    total, lanes = s.rho.shape[1:]
    quarters = total // LANES
    half = lanes // 2
    turned, reduced_ref, values = s.k_turned.at[c], s.k_reduced.at[c], s.k_values.at[c]
    ratio, u_ref, l_ref = s.k_ratio.at[c], s.k_u.at[c], s.k_l.at[c]
    with jax.named_scope("turn_k"):
        for m, v in enumerate(vs):
            for q in range(quarters):
                at = pl.ds(m * quarters + q, lanes, stride=BS)
                turned[at, :] = s.lines[v, q * LANES : (q + 1) * LANES, :].T * ratio[at, :]
    zero = s.k_zero[...]

    def ahead(n, carry):
        fresh = []
        for at, (product, older, newer) in zip(sides_of(lanes, n), carry):
            value = turned[at, :] + QUARTER * older - product
            reduced = u_ref[at, :] * value
            reduced_ref[at, :] = reduced
            fresh.append((l_ref[at, :] * value, newer, reduced))
        return tuple(fresh)

    with jax.named_scope("forward_k"):
        ends = [end[1:] for end in lax.fori_loop(0, half, ahead, ((zero,) * 3,) * 2, unroll=8)]
        nexts = tuple(
            meet([s.k_meeting[c, side, m] for m in range(7)], ends[side], ends[1 - side]) for side in range(2)
        )

    def back(step, carry):
        fresh = []
        for at, (nearer, farther) in zip(sides_of(lanes, half - 1 - step), carry):
            value = reduced_ref[at, :] + QUARTER * u_ref[at, :] * farther - l_ref[at, :] * nearer
            values[at, :] = value
            fresh.append((value, nearer))
        return tuple(fresh)

    with jax.named_scope("back_k"):
        lax.fori_loop(0, half, back, nexts, unroll=8)


def finish(chunks, padded, values, maps, advanced_out, increment_out, advanced, increment, sems):
    variables, total, lanes = advanced.shape
    rows_j = (padded.shape[1] - total) // 2
    quarters = total // LANES
    places = {v: (c, m) for c, vs in enumerate(chunks) for m, v in enumerate(vs)}

    def copies(at):
        return [
            pltpu.make_async_copy(source.at[at], target.at[at], sems.at[n])
            for n, (source, target) in enumerate(((advanced, advanced_out), (increment, increment_out)))
        ]

    for q in range(quarters):
        first = q * LANES
        solved = []
        for u in range(variables):
            c, m = places[u]
            solved.append(values[c, pl.ds(m * quarters + q, lanes, stride=BS), :])
        for v in range(variables):
            total_v = maps[v, 0, :1, :] * solved[0]
            for u in range(1, variables):
                total_v = total_v + maps[v, u, :1, :] * solved[u]
            piece = total_v.T
            increment[v, first : first + LANES, :] = piece
            advanced[v, first : first + LANES, :] = padded[v, rows_j + first : rows_j + first + LANES, :] + piece
            for copy in copies((v, pl.ds(first, LANES))):
                copy.start()
    for copy in copies((pl.ds(0, variables), pl.ds(0, total))):
        copy.wait()


def local(
    flow_state, spectral, wave_speed, left_map, right_map,
    donor_block, receiver_block, fringe_count, fringe_weight,
):
    variables, grids, rows_i, rows_j, rows_k = flow_state.shape
    assert grids == 1 and rows_k == LANES
    total = rows_i * rows_j
    devices, capacity = donor_block.shape[1:]
    slots = devices * capacity
    cube_count = total // (BS * BS) * (rows_k // BS)
    assert cube_count == LANES
    packed_rows = -(-variables * BS // GROUPS) * BS
    together = BS * LANES // total
    axes = ("ia", "ja", "ka")
    chunks = tuple((v,) for v in range(variables))
    tiles = tuple(tuple(range(v, min(v + together, variables))) for v in range(0, variables, together))
    operands = dict(
        flow_in=flow_state.reshape(variables, total, rows_k),
        rho_in=spectral.reshape(3, total, rows_k),
        speeds_in=wave_speed,
        left_in=left_map.transpose(1, 0, 2),
        right_in=right_map.transpose(1, 0, 2),
        donor_in=donor_block.transpose(0, 2, 1),
        receiver_in=receiver_block.transpose(0, 2, 1),
        count_in=fringe_count,
        weights_in=fringe_weight.transpose(0, 1, 3, 2).reshape(3, capacity, devices),
    )
    dma = pltpu.SemaphoreType.DMA

    def held(*dims):
        return pltpu.VMEM(dims, F32)

    scratch = dict(
        flow=held(variables, total, rows_k),
        rho=held(3, total, rows_k),
        lines=held(variables, total, rows_k),
        packed=held(cube_count, packed_rows, LANES),
        outbound=held(slots, packed_rows, LANES),
        arrived=held(slots, packed_rows, LANES),
        found=pltpu.VMEM((BS, LANES), jnp.int32),
        source=pltpu.SMEM((BS, LANES), jnp.int32),
        paces=held(3 * variables, max(rows_i, rows_j), LANES),
        edge=held(PARTS, 2, variables, rows_i // PARTS, rows_k),
        halo=held(PARTS, 2, variables, rows_i // PARTS, rows_k),
        own_sems=dma((10 + 2 * PARTS,)),
        cube_sems=dma((devices // BATCH,)),
        halo_sems=dma((2 + 2 * PARTS,)),
    )
    for name in ("speeds", "left", "right", "donor", "receiver", "count", "weights"):
        array = operands[name + "_in"]
        scratch[name] = pltpu.SMEM(array.shape, array.dtype)
    for letter, plane in (("i_", rows_j), ("j_", rows_i)):
        for name in ("u", "l", "values", "reduced"):
            scratch[letter + name] = held(variables, total, rows_k)
        scratch[letter + "inverse"] = held(total, rows_k)
        for name in ("last", "gains", "far_gains"):
            scratch[letter + name] = held(variables, 3, plane, rows_k)
        for name in ("ends", "start", "far", "nexts", "solved"):
            scratch[letter + name] = held(variables, 2, plane, rows_k)
        scratch[letter + "meeting"] = held(variables, 7, plane, rows_k)
        chain = lax.axis_size(letter[0] + "a") > 2
        scratch[letter + "gain_sems"] = dma((2 if chain else 1,))
        scratch[letter + "sems"] = dma(((3 if chain else 1) * len(chunks),))
    for name in ("u", "l", "ratio", "turned", "reduced"):
        scratch["k_" + name] = held(len(tiles), rows_k * BS, LANES)
    scratch["k_zero"] = held(BS, LANES)
    scratch["k_meeting"] = held(len(tiles), 2, 7, BS, LANES)

    field = pltpu.HBM((variables, total, rows_k), F32)
    outs = dict(
        padded=pltpu.VMEM((variables, total + 2 * rows_j, rows_k), F32),
        k_values=pltpu.VMEM((len(tiles), rows_k * BS, LANES), F32),
        maps=pltpu.VMEM((variables, variables, BS, LANES), F32),
    )
    names = (*operands, *outs, *scratch)
    moved = sum(a.size * 4 for a in operands.values()) + 2 * variables * total * rows_k * 4
    handed = pl.pallas_call(
        functools.partial(step_body, axes, capacity, rows_i, rows_j, chunks, tiles, names),
        out_shape=list(outs.values()),
        in_specs=[HBM] * len(operands),
        out_specs=[VMEM] * len(outs),
        scratch_shapes=list(scratch.values()),
        compiler_params=pltpu.CompilerParams(
            vmem_limit_bytes=LIMIT, collective_id=0, has_side_effects=True
        ),
        cost_estimate=pl.CostEstimate(flops=60_000_000, bytes_accessed=moved, transcendentals=0),
    )(*(in_hbm(a) for a in operands.values()))
    advanced, increment = pl.pallas_call(
        functools.partial(finish, tiles),
        out_shape=[field, field],
        in_specs=[VMEM] * len(outs),
        out_specs=[HBM] * 2,
        scratch_shapes=[
            held(variables, total, rows_k),
            held(variables, total, rows_k),
            dma((2,)),
        ],
        compiler_params=pltpu.CompilerParams(vmem_limit_bytes=16 << 20),
        cost_estimate=pl.CostEstimate(flops=6_000_000, bytes_accessed=moved, transcendentals=0),
    )(*handed)
    return advanced.reshape(flow_state.shape), increment.reshape(flow_state.shape)


def solution(mesh):
    return jax.shard_map(
        local,
        mesh=mesh,
        in_specs=(
            P(None, "ka", "ia", "ja", None),
            P(None, "ka", "ia", "ja", None),
            P(None, "ka", None),
            P("ka", None, None),
            P("ka", None, None),
            P(("ia", "ja", "ka"), None, None),
            P(("ia", "ja", "ka"), None, None),
            P(("ia", "ja", "ka"), None),
            P(None, ("ia", "ja", "ka"), None, None),
        ),
        out_specs=(P(None, "ka", "ia", "ja", None), P(None, "ka", "ia", "ja", None)),
        check_vma=False,
    )
```

```python
import functools
import math
import types

import jax
import jax.numpy as jnp
from jax import lax
from jax.experimental import pallas as pl
from jax.experimental.pallas import tpu as pltpu
from jax.sharding import PartitionSpec as P

BS = 8
LANES = 128
GROUPS = LANES // BS
QUARTER = 0.25
BATCH = 8
PARTS = 2
LIMIT = 44 << 20
VMEM = pl.BlockSpec(memory_space=pltpu.VMEM)
HBM = pl.BlockSpec(memory_space=pltpu.HBM)
MESH = pl.DeviceIdType.MESH
F32 = jnp.float32


def in_hbm(array):
    return pltpu.with_memory_space_constraint(array, pltpu.HBM)


def lane_iota(rows=BS):
    return lax.broadcasted_iota(jnp.int32, (rows, LANES), 1)


def row_iota(rows=BS):
    return lax.broadcasted_iota(jnp.int32, (rows, LANES), 0)


def diagonals(tiles):
    group = lane_iota() // BS
    distance = 1
    while distance < GROUPS:
        odd = (group // distance) % 2 == 1
        tiles = [jnp.where(odd, tiles[(a + distance) % GROUPS], tiles[a]) for a in range(GROUPS)]
        distance *= 2
    return [tiles[(GROUPS - g) % GROUPS] for g in range(GROUPS)]


def turned_by(tile, groups):
    return tile if groups % GROUPS == 0 else pltpu.roll(tile, groups % GROUPS * BS, 1)


def tile_row(block, rows_j, g):
    blocks_j = rows_j // BS
    return (block // blocks_j) * (BS * rows_j) + (block % blocks_j) * BS + (g % BS) * rows_j


def rows_at(start, size):
    return pl.ds(pl.multiple_of(start, BS), size)


def pack_set(rows_j, q, flow, packed):
    groups = flow.shape[0] * BS
    first = q * GROUPS
    count = min(GROUPS, groups - first)

    def one(block, carry):
        tiles = [
            turned_by(flow[g // BS, rows_at(tile_row(block, rows_j, g), BS), :], g - first)
            for g in range(first, first + count)
        ]
        tiles = diagonals(tiles + tiles[:1] * (GROUPS - count))
        for k in range(GROUPS):
            packed[block * GROUPS + k, q * BS : (q + 1) * BS, :] = tiles[k]
        return carry

    lax.fori_loop(0, packed.shape[0] // GROUPS, one, 0, unroll=4)


def gather(capacity, donor, packed, slots, outbound):
    low = lane_iota() < LANES // 2
    tiles = outbound.shape[1] // BS
    fresh = []
    for slot in slots:
        cube = donor[0, slot % capacity, slot // capacity]
        shift = (GROUPS - cube % GROUPS) % GROUPS * BS
        for q in range(tiles):
            held = packed[cube, q * BS : (q + 1) * BS, :]
            tile = pltpu.roll(held, shift, 1)
            if q == tiles - 1:
                folded = pltpu.roll(pltpu.roll(held, BS // 2, 0), (shift + LANES // 2) % LANES, 1)
                tile = jnp.where(low, tile, folded)
            fresh.append((slot, q, tile))
    for slot, q, tile in fresh:
        outbound[slot, q * BS : (q + 1) * BS, :] = tile


def blend(cubes, shifted, weight):
    return (1.0 - weight) * cubes + weight * shifted


def interpolate(capacity, weights, receiver, slots, arrived):
    lane, row = lane_iota(), row_iota()
    tiles = arrived.shape[1] // BS
    held = [arrived[slot, q * BS : (q + 1) * BS, :] for slot in slots for q in range(tiles)]
    fresh = []
    for n, cubes in enumerate(held):
        slot, q = slots[n // tiles], n % tiles
        d, c = slot // capacity, slot % capacity
        shift = receiver[0, c, d] % GROUPS * BS
        if q == tiles - 1:
            unfolded = pltpu.roll(pltpu.roll(cubes, BS // 2, 0), LANES // 2, 1)
            cubes = jnp.where(row < BS // 2, cubes, unfolded)
        after = jnp.where(lane % (BS * BS) >= BS * (BS - 1), cubes, pltpu.roll(cubes, LANES - BS, 1))
        cubes = blend(cubes, after, weights[0, c, d])
        after = jnp.where(row == BS - 1, cubes, pltpu.roll(cubes, BS - 1, 0))
        cubes = blend(cubes, after, weights[1, c, d])
        after = jnp.where(lane % BS == BS - 1, cubes, pltpu.roll(cubes, LANES - 1, 1))
        cubes = blend(cubes, after, weights[2, c, d])
        fresh.append(pltpu.roll(cubes, shift, 1))
    for n, cubes in enumerate(fresh):
        q = n % tiles
        arrived[slots[n // tiles], q * BS : (q + 1) * BS, :] = cubes


def source_of(capacity, slots, receiver, count):
    lane = lane_iota()

    def one(slot, found):
        d, c = slot // capacity, slot % capacity
        target = jnp.where(count[0, d] > c, receiver[0, c, d], -1)
        return jnp.where(lane == target, slot, found)

    return lax.fori_loop(0, slots, one, jnp.full((BS, LANES), -1, jnp.int32), unroll=BATCH)


def unpack_part(rows_j, part, source, arrived, flow, padded):
    groups = flow.shape[0] * BS
    group = lane_iota() // BS

    def one(block, carry):
        slots = [source[0, block * GROUPS + k] for k in range(GROUPS)]
        owner = jnp.full((BS, LANES), -1, jnp.int32)
        for k in range(GROUPS):
            owner = jnp.where(group == k, slots[k], owner)
        live = owner >= 0
        for first in range(0, groups, GROUPS):
            q = first // GROUPS
            tiles = diagonals(
                [arrived[jnp.maximum(slots[k], 0), q * BS : (q + 1) * BS, :] for k in range(GROUPS)]
            )
            for g in range(first, min(first + GROUPS, groups)):
                row = tile_row(block, rows_j, g)
                fresh = turned_by(tiles[g - first], GROUPS - (g - first))
                kept = flow[g // BS, rows_at(row, BS), :]
                padded[g // BS, rows_at(row + rows_j, BS), :] = jnp.where(live, fresh, kept)
        return carry

    count = flow.shape[1] * flow.shape[2] // BS**3 // GROUPS // PARTS
    lax.fori_loop(part * count, (part + 1) * count, one, 0, unroll=2)


def row_of(n, count, lower):
    return jnp.where(lower, n, count - 1 - n)


def gains_of(state):
    older, newer, lead = state
    return lead, -QUARTER * older, (QUARTER * lead - 1.0) * newer, -QUARTER * newer


def meet_factors(near, far):
    f0, s0, f1, s1 = gains_of(near)
    g0, t0, g1, t1 = gains_of(far)
    cross = g1 - t1 * f0
    a11 = 1.0 - t1 * s0 - cross * f1
    a12 = -cross * s1
    a21 = g0 - t0 * f1
    a22 = 1.0 - t0 * s1
    scale = 1.0 / (a11 * a22 - a12 * a21)
    return a22 * scale, a12 * scale, a21 * scale, a11 * scale, t1, cross, t0


def meet(factors, near, far):
    m11, m12, m21, m22, t1, cross, t0 = factors
    r0, r1 = near
    q0, q1 = far
    b1 = q1 - t1 * r0 - cross * r1
    b2 = q0 - t0 * r1
    return b1 * m11 - m12 * b2, m22 * b2 - m21 * b1


def eliminated(pivot, carry):
    older, newer, lead, square = carry
    inverse = 1.0 / (pivot - 0.0625 * older - square)
    gain = QUARTER * lead - 1.0
    lead = gain * inverse
    return inverse, lead, (newer, inverse, lead, gain * gain * inverse)


def begin_factor(older, newer, lead):
    gain = QUARTER * lead - 1.0
    lead = gain * newer
    return older, newer, lead, gain * lead


def invert_rho(direction, rows, stride, spectral, inverse):
    plane = inverse.shape[0] // rows

    def one(row, carry):
        at = rows_at(row * plane, plane)
        if stride is None:
            inverse[at, :] = 1.0 / spectral[direction, at, :]
        else:
            inverse[at, :] = 1.0 / spectral[direction, pl.ds(row, plane, stride=stride), :]
        return carry

    lax.fori_loop(0, rows, one, 0, unroll=2)


def factor_pass(direction, rows, lower, group, paces, inverse, start, u_ref, l_ref, last):
    variables, total, lanes = u_ref.shape
    plane = total // rows
    for first in range(0, variables, group):
        vs = range(first, min(first + group, variables))

        def one(n, carry):
            at = rows_at(row_of(n, rows, lower) * plane, plane)
            ratio = inverse[at, :]
            fresh = []
            for v, held in zip(vs, carry):
                pace = paces[direction * variables + v, :plane, :]
                u, l, held = eliminated(pace * ratio + 2.5, held)
                u_ref[v, at, :] = u
                l_ref[v, at, :] = l
                fresh.append(held)
            return tuple(fresh)

        lax.fori_loop(0, rows, one, tuple(begin_factor(start[v, 0], start[v, 1], start[v, 2]) for v in vs))
    newest = rows_at(row_of(rows - 1, rows, lower) * plane, plane)
    older = rows_at(row_of(rows - 2, rows, lower) * plane, plane)
    for v in range(variables):
        last[v, 0] = u_ref[v, older, :]
        last[v, 1] = u_ref[v, newest, :]
        last[v, 2] = l_ref[v, older, :]


def forward_pass(vs, rows, lower, values, reduced_ref, scale, u_ref, l_ref, gains, start, ends):
    variables, total, lanes = values.shape
    plane = total // rows

    def one(n, carry):
        at = rows_at(row_of(n, rows, lower) * plane, plane)
        fresh = []
        for v, (product, older, newer) in zip(vs, carry):
            value = scale(v, at, values[v, at, :]) + QUARTER * older - product
            reduced = u_ref[v, at, :] * value
            reduced_ref[v, at, :] = reduced
            fresh.append((l_ref[v, at, :] * value, newer, reduced))
        return tuple(fresh)

    begin = tuple(((QUARTER * gains[v, 2] - 1.0) * start[v, 1], start[v, 0], start[v, 1]) for v in vs)
    for v, (product, older, newer) in zip(vs, lax.fori_loop(0, rows, one, begin, unroll=4)):
        ends[v, 0] = older
        ends[v, 1] = newer


def backward_pass(vs, rows, lower, values, u_ref, l_ref, nexts, solved, store):
    variables, total, lanes = values.shape
    plane = total // rows

    def one(step, carry):
        row = row_of(rows - 1 - step, rows, lower)
        at = rows_at(row * plane, plane)
        fresh = []
        for v, (nearer, farther) in zip(vs, carry):
            value = values[v, at, :] + QUARTER * u_ref[v, at, :] * farther - l_ref[v, at, :] * nearer
            store(v, row, at, value)
            fresh.append((value, nearer))
        return tuple(fresh)

    begin = tuple((nexts[v, 0], nexts[v, 1]) for v in vs)
    for v, (nearer, farther) in zip(vs, lax.fori_loop(0, rows, one, begin, unroll=4)):
        if solved is not None:
            solved[v, 0] = nearer
            solved[v, 1] = farther


def residual_rows(rows_i, first, count, padded, spectral, left, paces, inverse, values):
    variables, total, lanes = values.shape
    rows_j = total // rows_i
    lane, row_id = lane_iota(rows_j), row_iota(rows_j)

    def one(row, carry):
        base = row * rows_j
        at = rows_at(base, rows_j)
        rho = [spectral[e, at, :] for e in range(3)]
        ratio = inverse[at, :]
        residual = []
        for v in range(variables):
            center = padded[v, rows_at(base + rows_j, rows_j), :]
            twice = 2.0 * center
            along_i = padded[v, rows_at(base + 2 * rows_j, rows_j), :] + padded[v, at, :] - twice
            after = jnp.where(row_id == rows_j - 1, 0.0, padded[v, pl.ds(base + rows_j + 1, rows_j), :])
            before = jnp.where(row_id == 0, 0.0, padded[v, pl.ds(base + rows_j - 1, rows_j), :])
            along_j = after + before - twice
            after = jnp.where(lane == lanes - 1, 0.0, pltpu.roll(center, lanes - 1, 1))
            before = jnp.where(lane == 0, 0.0, pltpu.roll(center, 1, 1))
            along_k = after + before - twice
            residual.append(rho[0] * along_i + rho[1] * along_j + rho[2] * along_k)
        for v in range(variables):
            total_v = left[v, 0, 0] * residual[0]
            for u in range(1, variables):
                total_v = total_v + left[v, 0, u] * residual[u]
            values[v, at, :] = total_v * (ratio * paces[v, :rows_j, :])
        return carry

    lax.fori_loop(first, first + count, one, 0, unroll=2 if count % 2 == 0 else 1)


def edge_rows(vs, rows_i, halo, spectral, left, paces, inverse, values):
    variables, total, lanes = values.shape
    rows_j = total // rows_i
    size = rows_i // PARTS
    for part in range(PARTS):
        for side, first in enumerate((0, rows_j - 1)):
            at = pl.ds(part * size * rows_j + first, size, stride=rows_j)
            rho = spectral[1, at, :] * inverse[at, :]
            parts = [rho * halo[part, side, u] for u in range(variables)]
            for v in vs:
                total_v = left[v, 0, 0] * parts[0]
                for u in range(1, variables):
                    total_v = total_v + left[v, 0, u] * parts[u]
                values[v, at, :] = values[v, at, :] + total_v * paces[v, :size, :]


class Line:
    def __init__(self, axis):
        self.axis = axis
        self.members = lax.axis_size(axis)
        self.half = self.members // 2
        self.place = lax.axis_index(axis)
        self.lower = self.place < self.half
        depth = jnp.where(self.lower, self.place, self.members - 1 - self.place)
        self.inner = jnp.where(self.lower, self.place + 1, self.place - 1)
        self.outer = jnp.where(self.lower, self.place - 1, self.place + 1)
        self.middle = depth == self.half - 1
        self.end = depth == 0

    def send(self, source, target, send_sem, recv_sem, device):
        return pltpu.make_async_remote_copy(
            src_ref=source,
            dst_ref=target,
            send_sem=send_sem,
            recv_sem=recv_sem,
            device_id={self.axis: device},
            device_id_type=MESH,
        )

    def sides(self):
        return (self.place > 0, self.place - 1), (self.place < self.members - 1, self.place + 1)


def span(vs):
    return pl.ds(vs[0], len(vs))


class Sweep:
    def __init__(self, line, s, chunks, sent):
        self.line, self.s, self.chunks, self.sent = line, s, chunks, sent

    def gains_to(self, target, number):
        s = self.s
        return self.line.send(s.last, target, self.sent[0], s.gain_sems.at[number], self.line.inner)

    def gains_in(self):
        line, s = self.line, self.s
        if line.half > 1:

            @pl.when(jnp.logical_not(line.end))
            def _():
                self.gains_to(s.gains, 1).wait_recv()

    def gains_out(self):
        line, s = self.line, self.s
        if line.half > 1:

            @pl.when(jnp.logical_not(line.middle))
            def _():
                self.gains_to(s.gains, 1).start()

        @pl.when(line.middle)
        def _():
            self.gains_to(s.far_gains, 0).start()

    def prepare(self):
        line, s = self.line, self.s

        @pl.when(line.middle)
        def _():
            self.gains_to(s.far_gains, 0).wait_recv()
            for v in range(s.last.shape[0]):
                near = [s.last[v, m] for m in range(3)]
                far = [s.far_gains[v, m] for m in range(3)]
                for m, factor in enumerate(meet_factors(near, far)):
                    s.meeting[v, m] = factor

    def part(self, c):
        return span(self.chunks[c]) if c is not None else span(range(self.s.last.shape[0]))

    def inward(self, c):
        s, at = self.s, self.part(c)
        recv = s.sems.at[len(self.chunks) + (c or 0)]
        return self.line.send(s.ends.at[at], s.start.at[at], self.sent[1], recv, self.line.inner)

    def across(self, c):
        s, at = self.s, self.part(c)
        recv = s.sems.at[c or 0]
        return self.line.send(s.ends.at[at], s.far.at[at], self.sent[1], recv, self.line.inner)

    def outward(self, c):
        s, at = self.s, self.part(c)
        recv = s.sems.at[2 * len(self.chunks) + (c or 0)]
        return self.line.send(s.solved.at[at], s.nexts.at[at], self.sent[2], recv, self.line.outer)

    def start_in(self, c):
        if self.line.half > 1:

            @pl.when(jnp.logical_not(self.line.end))
            def _():
                self.inward(c).wait_recv()

    def ends_out(self, c):
        line = self.line
        if line.half > 1:

            @pl.when(jnp.logical_not(line.middle))
            def _():
                self.inward(c).start()

        @pl.when(line.middle)
        def _():
            self.across(c).start()

    def nexts_in(self, c):
        line, s = self.line, self.s

        @pl.when(line.middle)
        def _():
            self.across(c).wait_recv()
            for v in self.chunks[c]:
                pair = meet(
                    [s.meeting[v, m] for m in range(7)],
                    [s.ends[v, m] for m in range(2)],
                    [s.far[v, m] for m in range(2)],
                )
                s.nexts[v, 0], s.nexts[v, 1] = pair

        if line.half > 1:

            @pl.when(jnp.logical_not(line.middle))
            def _():
                self.outward(c).wait_recv()

    def solved_out(self, c):
        line = self.line
        if line.half > 1:

            @pl.when(jnp.logical_not(line.end))
            def _():
                self.outward(c).start()

    def close(self):
        line = self.line
        self.gains_to(self.s.far_gains, 0).wait_send()
        self.across(None).wait_send()
        if line.half > 1:

            @pl.when(jnp.logical_not(line.end))
            def _():
                self.outward(None).wait_send()

    def clear(self):
        line, s = self.line, self.s

        @pl.when(line.end)
        def _():
            s.gains[...] = jnp.zeros(s.gains.shape, F32)
            s.start[...] = jnp.zeros(s.start.shape, F32)


def step_body(axes, capacity, rows_i, rows_j, chunks, tiles, names, *refs):
    s = types.SimpleNamespace(**dict(zip(names, refs)))
    flow, rho, padded = s.flow, s.rho, s.padded
    variables, total, lanes = flow.shape
    line_i, line_j = Line("ia"), Line("ja")

    def part(letter):
        return types.SimpleNamespace(**{k[2:]: r for k, r in vars(s).items() if k[:2] == letter + "_"})

    si, sj = part("i"), part("j")
    first = 4 + 2 * PARTS
    sweep_i, sweep_j = (
        Sweep(line, part, chunks, [s.own_sems.at[first + 3 * n + m] for m in range(3)])
        for n, (line, part) in enumerate(((line_i, si), (line_j, sj)))
    )
    sizes = [lax.axis_size(axis) for axis in axes]
    here = [lax.axis_index(axis) for axis in axes]
    devices = math.prod(sizes)
    slots = devices * capacity

    packed_tiles = s.packed.shape[1] // BS
    fields = []
    for q in range(packed_tiles):
        at = pl.ds(2 * q, min(2, variables - 2 * q))
        fields.append(pltpu.make_async_copy(s.flow_in.at[at], flow.at[at], s.own_sems.at[q]))
    fields.append(pltpu.make_async_copy(s.rho_in, rho, s.own_sems.at[packed_tiles]))
    small = [
        pltpu.make_async_copy(getattr(s, name + "_in"), getattr(s, name), s.own_sems.at[packed_tiles + 1 + n])
        for n, name in enumerate(("speeds", "left", "right", "donor", "receiver", "count", "weights"))
    ]
    for copy in fields[:-1] + small + fields[-1:]:
        copy.start()

    order_j = sorted(range(sizes[1]), key=lambda d: min(d, sizes[1] - d))
    rest = devices // sizes[1]

    def peer(offset_j, n, sign):
        off = (n // sizes[2], offset_j, n % sizes[2])
        place = [(h + sign * o + size) % size for h, o, size in zip(here, off, sizes)]
        number = (place[0] * sizes[1] + place[1]) * sizes[2] + place[2]
        return number, dict(zip(axes, place))

    around = [[(h + o) % size for o in range(size)] for h, size in zip(here, sizes)]
    me = (here[0] * sizes[1] + here[1]) * sizes[2] + here[2]
    barrier = pltpu.get_barrier_semaphore()
    with jax.named_scope("greet"):
        for offset_j in order_j:
            for n in range(0 if offset_j else 1, rest):
                place = around[0][n // sizes[2]], around[1][offset_j], around[2][n % sizes[2]]
                pl.semaphore_signal(barrier, inc=1, device_id=dict(zip(axes, place)), device_id_type=MESH)

    with jax.named_scope("pack"):
        for q in range(packed_tiles):
            with jax.named_scope(f"flow{q}"):
                fields[q].wait()
            with jax.named_scope(f"pack{q}"):
                pack_set(rows_j, q, flow, s.packed)
    for copy in small:
        copy.wait()
    with jax.named_scope("entered"):
        pl.semaphore_wait(barrier, devices - 1)

    used = variables * BS**3 // LANES

    def cubes(step, to, place, of, count=1):
        def at(device):
            return pl.ds(device * capacity, count * capacity), pl.ds(0, used)

        return pltpu.make_async_remote_copy(
            src_ref=s.outbound.at[at(to)],
            dst_ref=s.arrived.at[at(of)],
            send_sem=s.own_sems.at[1],
            recv_sem=s.cube_sems.at[step // BATCH],
            device_id=place,
            device_id_type=MESH,
        )

    with jax.named_scope("send_cubes"):
        for m, offset_j in enumerate(order_j):

            def begin(batch, carry, skip=0):
                first = batch * BATCH
                numbers = [peer(offset_j, first + n, 1)[0] for n in range(BATCH)]
                for c in range(capacity):
                    gather(capacity, s.donor, s.packed, [to * capacity + c for to in numbers], s.outbound)
                for n in range(skip, BATCH):
                    to, place = peer(offset_j, first + n, 1)
                    cubes(m * rest + first + n, to, place, me).start()
                return carry

            if offset_j == 0:
                begin(0, 0, 1)
            lax.fori_loop(0 if offset_j else 1, rest // BATCH, begin, 0)
        own = pl.ds(me * capacity, capacity)
        s.arrived[own] = s.outbound[own]

    def pace(n, carry):
        value = jnp.full((BS, LANES), s.speeds[n // variables, 0, n % variables], F32)
        value = 1.0 / value
        for first in range(0, s.paces.shape[1], BS):
            s.paces[n, first : first + BS, :] = value
        return carry

    def factor_j():
        with jax.named_scope("factor_j"):
            sweep_j.gains_in()
            factor_pass(1, rows_j, line_j.lower, 2, s.paces, sj.inverse, sj.gains, sj.u, sj.l, sj.last)
            sweep_j.gains_out()

    with jax.named_scope("prepare"):
        lax.fori_loop(0, 3 * variables, pace, 0)
        for v in range(variables):
            for u in range(variables):
                s.maps[v, u] = jnp.full((BS, LANES), s.right[v, 0, u], F32)
        sweep_i.clear()
        sweep_j.clear()
        fields[-1].wait()
        invert_rho(1, rows_j, rows_j, rho, sj.inverse)
        pl.when(line_j.end)(factor_j)
    with jax.named_scope("factor_i"):
        invert_rho(0, rows_i, None, rho, si.inverse)
        sweep_i.gains_in()
        factor_pass(0, rows_i, line_i.lower, 3, s.paces, si.inverse, si.gains, si.u, si.l, si.last)
        sweep_i.gains_out()
    with jax.named_scope("sources"):
        s.found[...] = source_of(capacity, slots, s.receiver, s.count)
        found = pltpu.make_async_copy(s.found, s.source, s.own_sems.at[0])
        found.start()
    with jax.named_scope("factor_k"):
        factor_k(tiles, s)
    with jax.named_scope("arrivals"):
        for m, offset_j in enumerate(order_j):

            def arrive(batch, carry, count=BATCH):
                first = batch * BATCH
                cubes(m * rest + first, 0, peer(offset_j, first + BATCH - 1, 1)[1], 0, count).wait_recv()
                sources = [peer(offset_j, first + n, -1)[0] for n in range(BATCH)]
                for c in range(capacity):
                    interpolate(capacity, s.weights, s.receiver, [of * capacity + c for of in sources], s.arrived)
                return carry

            if offset_j == 0:
                arrive(0, 0, BATCH - 1)
            lax.fori_loop(0 if offset_j else 1, rest // BATCH, arrive, 0)
    rows_part = rows_i // PARTS

    def halo_i(side, device):
        mine, other = (rows_j, rows_j + total) if side == 0 else (total, 0)
        source = padded.at[:, pl.ds(mine, rows_j), :]
        target = padded.at[:, pl.ds(other, rows_j), :]
        return line_i.send(source, target, s.own_sems.at[2 + side], s.halo_sems.at[side], device)

    def halo_j(side, device, part):
        n = 2 + 2 * part + side
        source, target = s.edge.at[part, side], s.halo.at[part, 1 - side]
        return line_j.send(source, target, s.own_sems.at[2 + n], s.halo_sems.at[n], device)

    def at_borders(line, act, otherwise=None):
        for side, (there, device) in enumerate(line.sides()):
            pl.when(there)(functools.partial(act, side, device))
            if otherwise is not None:
                pl.when(jnp.logical_not(there))(functools.partial(otherwise, side))

    for part in range(PARTS):
        with jax.named_scope("unpack"):
            if part == 0:
                found.wait()
            unpack_part(rows_j, part, s.source, s.arrived, flow, padded)
        with jax.named_scope("send_halos"):
            for side, row in enumerate((rows_j, 2 * rows_j - 1)):
                at = pl.ds(row + part * rows_part * rows_j, rows_part, stride=rows_j)
                for v in range(variables):
                    s.edge[part, side, v] = padded[v, at, :]
            at_borders(line_j, lambda side, device: halo_j(side, device, part).start())
    with jax.named_scope("send_halos"):
        at_borders(line_i, lambda side, device: halo_i(side, device).start())

    rest_of = (padded, rho, s.left, s.paces, si.inverse, si.values)
    with jax.named_scope("residual"):
        residual_rows(rows_i, 1, rows_i - 2, *rest_of)
    if line_j.half > 1:
        pl.when(jnp.logical_not(line_j.end))(factor_j)
    with jax.named_scope("halos"):

        def no_i(side):
            first = 0 if side == 0 else rows_j + total
            padded[:, first : first + rows_j, :] = jnp.zeros((variables, rows_j, lanes), F32)

        def no_j(part, side):
            s.halo[part, side] = jnp.zeros(s.halo.shape[2:], F32)

        at_borders(line_i, lambda side, device: halo_i(1 - side, device).wait_recv(), no_i)
        for part in range(PARTS):
            at_borders(
                line_j, lambda side, device: halo_j(1 - side, device, part).wait_recv(), functools.partial(no_j, part)
            )
    with jax.named_scope("edges"):
        residual_rows(rows_i, 0, 1, *rest_of)
        residual_rows(rows_i, rows_i - 1, 1, *rest_of)

    def plain(v, at, value):
        return value

    def scaled(v, at, value):
        return value * (sj.inverse[at, :] * s.paces[variables + v, :rows_i, :])

    def store_turned(v, row, at, value):
        sj.values[v, pl.ds(row, rows_j, stride=rows_i), :] = value

    def store_lines(v, row, at, value):
        s.lines[v, pl.ds(row, rows_i, stride=rows_j), :] = value

    def forward_i(c):
        edge_rows(chunks[c], rows_i, s.halo, rho, s.left, s.paces, si.inverse, si.values)
        sweep_i.start_in(c)
        forward_pass(chunks[c], rows_i, line_i.lower, si.values, si.reduced, plain, si.u, si.l, si.gains, si.start, si.ends)
        sweep_i.ends_out(c)

    def back_i(c):
        sweep_i.nexts_in(c)
        solved = si.solved if line_i.half > 1 else None
        backward_pass(chunks[c], rows_i, line_i.lower, si.reduced, si.u, si.l, si.nexts, solved, store_turned)
        sweep_i.solved_out(c)

    def forward_j(c):
        sweep_j.start_in(c)
        forward_pass(chunks[c], rows_j, line_j.lower, sj.values, sj.reduced, scaled, sj.u, sj.l, sj.gains, sj.start, sj.ends)
        sweep_j.ends_out(c)

    def back_j(c):
        sweep_j.nexts_in(c)
        solved = sj.solved if line_j.half > 1 else None
        backward_pass(chunks[c], rows_j, line_j.lower, sj.reduced, sj.u, sj.l, sj.nexts, solved, store_lines)
        sweep_j.solved_out(c)

    numbers = range(len(chunks))
    with jax.named_scope("forward_i"):
        for c in numbers:
            forward_i(c)
    with jax.named_scope("prepare_i"):
        sweep_i.prepare()
    with jax.named_scope("back_i"):
        for c in numbers:
            back_i(c)
            pl.when(line_j.end)(functools.partial(forward_j, c))
    with jax.named_scope("solve_j"):
        if line_j.half > 1:
            for c in numbers:
                pl.when(jnp.logical_not(line_j.end))(functools.partial(forward_j, c))
        sweep_j.prepare()
        for c in numbers:
            back_j(c)
            for t, vs in enumerate(tiles[:-1]):
                if vs[-1] == chunks[c][-1]:
                    pl.when(line_j.end)(functools.partial(solve_k, t, vs, s))
        for t, vs in enumerate(tiles[:-1]):
            pl.when(jnp.logical_not(line_j.end))(functools.partial(solve_k, t, vs, s))
        solve_k(len(tiles) - 1, tiles[-1], s)

    with jax.named_scope("close"):
        at_borders(line_i, lambda side, device: halo_i(side, device).wait_send())
        for part in range(PARTS):
            at_borders(line_j, lambda side, device: halo_j(side, device, part).wait_send())
        cubes(0, 0, peer(order_j[0], 0, 1)[1], 0, devices - 1).wait_send()
        sweep_i.close()
        sweep_j.close()


def sides_of(lanes, step):
    for k in (step, lanes - 1 - step):
        yield rows_at(k * BS, BS)


def factor_k(chunks, s):
    total, lanes = s.rho.shape[1:]
    variables = s.flow.shape[0]
    quarters = total // LANES
    for q in range(quarters):
        ratio = (1.0 / s.rho[2, q * LANES : (q + 1) * LANES, :]).T
        for c, vs in enumerate(chunks):
            for m, v in enumerate(vs):
                at = pl.ds(m * quarters + q, lanes, stride=BS)
                s.k_ratio[c, at, :] = ratio * s.paces[2 * variables + v, :1, :]
    for c, vs in enumerate(chunks):
        for spare in range(len(vs) * quarters, BS):
            at = pl.ds(spare, lanes, stride=BS)
            s.k_ratio[c, at, :] = jnp.zeros((lanes, lanes), F32)
            s.k_turned[c, at, :] = jnp.zeros((lanes, lanes), F32)
    half = lanes // 2
    s.k_zero[...] = jnp.zeros((BS, lanes), F32)
    zero = s.k_zero[...]
    numbers = range(len(chunks))

    def one(n, carry):
        fresh = []
        for c in numbers:
            for at, held in zip(sides_of(lanes, n), carry[c]):
                u, l, held = eliminated(s.k_ratio[c, at, :] + 2.5, held)
                s.k_u[c, at, :] = u
                s.k_l[c, at, :] = l
                fresh.append(held)
        return tuple(zip(fresh[::2], fresh[1::2]))

    lax.fori_loop(0, half, one, ((begin_factor(zero, zero, zero),) * 2,) * len(chunks))
    for c in numbers:
        pair = []
        for older, newer in zip(sides_of(lanes, half - 2), sides_of(lanes, half - 1)):
            pair.append((s.k_u[c, older, :], s.k_u[c, newer, :], s.k_l[c, older, :]))
        for side in range(2):
            for m, factor in enumerate(meet_factors(pair[side], pair[1 - side])):
                s.k_meeting[c, side, m] = factor


def solve_k(c, vs, s):
    total, lanes = s.rho.shape[1:]
    quarters = total // LANES
    half = lanes // 2
    turned, reduced_ref, values = s.k_turned.at[c], s.k_reduced.at[c], s.k_values.at[c]
    ratio, u_ref, l_ref = s.k_ratio.at[c], s.k_u.at[c], s.k_l.at[c]
    with jax.named_scope("turn_k"):
        for m, v in enumerate(vs):
            for q in range(quarters):
                at = pl.ds(m * quarters + q, lanes, stride=BS)
                turned[at, :] = s.lines[v, q * LANES : (q + 1) * LANES, :].T * ratio[at, :]
    zero = s.k_zero[...]

    def ahead(n, carry):
        fresh = []
        for at, (product, older, newer) in zip(sides_of(lanes, n), carry):
            value = turned[at, :] + QUARTER * older - product
            reduced = u_ref[at, :] * value
            reduced_ref[at, :] = reduced
            fresh.append((l_ref[at, :] * value, newer, reduced))
        return tuple(fresh)

    with jax.named_scope("forward_k"):
        ends = [end[1:] for end in lax.fori_loop(0, half, ahead, ((zero,) * 3,) * 2, unroll=8)]
        nexts = tuple(
            meet([s.k_meeting[c, side, m] for m in range(7)], ends[side], ends[1 - side]) for side in range(2)
        )

    def back(step, carry):
        fresh = []
        for at, (nearer, farther) in zip(sides_of(lanes, half - 1 - step), carry):
            value = reduced_ref[at, :] + QUARTER * u_ref[at, :] * farther - l_ref[at, :] * nearer
            values[at, :] = value
            fresh.append((value, nearer))
        return tuple(fresh)

    with jax.named_scope("back_k"):
        lax.fori_loop(0, half, back, nexts, unroll=8)


def finish(chunks, padded, values, maps, advanced_out, increment_out, advanced, increment, sems):
    variables, total, lanes = advanced.shape
    rows_j = (padded.shape[1] - total) // 2
    quarters = total // LANES
    places = {v: (c, m) for c, vs in enumerate(chunks) for m, v in enumerate(vs)}

    def copies(at):
        return [
            pltpu.make_async_copy(source.at[at], target.at[at], sems.at[n])
            for n, (source, target) in enumerate(((advanced, advanced_out), (increment, increment_out)))
        ]

    for q in range(quarters):
        first = q * LANES
        solved = []
        for u in range(variables):
            c, m = places[u]
            solved.append(values[c, pl.ds(m * quarters + q, lanes, stride=BS), :])
        for v in range(variables):
            total_v = maps[v, 0, :1, :] * solved[0]
            for u in range(1, variables):
                total_v = total_v + maps[v, u, :1, :] * solved[u]
            piece = total_v.T
            increment[v, first : first + LANES, :] = piece
            advanced[v, first : first + LANES, :] = padded[v, rows_j + first : rows_j + first + LANES, :] + piece
            for copy in copies((v, pl.ds(first, LANES))):
                copy.start()
    for copy in copies((pl.ds(0, variables), pl.ds(0, total))):
        copy.wait()


def local(
    flow_state, spectral, wave_speed, left_map, right_map,
    donor_block, receiver_block, fringe_count, fringe_weight,
):
    variables, grids, rows_i, rows_j, rows_k = flow_state.shape
    assert grids == 1 and rows_k == LANES
    total = rows_i * rows_j
    devices, capacity = donor_block.shape[1:]
    slots = devices * capacity
    cube_count = total // (BS * BS) * (rows_k // BS)
    assert cube_count == LANES
    packed_rows = -(-variables * BS // GROUPS) * BS
    together = BS * LANES // total
    axes = ("ia", "ja", "ka")
    chunks = tuple((v,) for v in range(variables))
    tiles = tuple(tuple(range(v, min(v + together, variables))) for v in range(0, variables, together))
    operands = dict(
        flow_in=flow_state.reshape(variables, total, rows_k),
        rho_in=spectral.reshape(3, total, rows_k),
        speeds_in=wave_speed,
        left_in=left_map.transpose(1, 0, 2),
        right_in=right_map.transpose(1, 0, 2),
        donor_in=donor_block.transpose(0, 2, 1),
        receiver_in=receiver_block.transpose(0, 2, 1),
        count_in=fringe_count,
        weights_in=fringe_weight.transpose(0, 1, 3, 2).reshape(3, capacity, devices),
    )
    dma = pltpu.SemaphoreType.DMA

    def held(*dims):
        return pltpu.VMEM(dims, F32)

    scratch = dict(
        flow=held(variables, total, rows_k),
        rho=held(3, total, rows_k),
        lines=held(variables, total, rows_k),
        packed=held(cube_count, packed_rows, LANES),
        outbound=held(slots, packed_rows, LANES),
        arrived=held(slots, packed_rows, LANES),
        found=pltpu.VMEM((BS, LANES), jnp.int32),
        source=pltpu.SMEM((BS, LANES), jnp.int32),
        paces=held(3 * variables, max(rows_i, rows_j), LANES),
        edge=held(PARTS, 2, variables, rows_i // PARTS, rows_k),
        halo=held(PARTS, 2, variables, rows_i // PARTS, rows_k),
        own_sems=dma((10 + 2 * PARTS,)),
        cube_sems=dma((devices // BATCH,)),
        halo_sems=dma((2 + 2 * PARTS,)),
    )
    for name in ("speeds", "left", "right", "donor", "receiver", "count", "weights"):
        array = operands[name + "_in"]
        scratch[name] = pltpu.SMEM(array.shape, array.dtype)
    for letter, plane in (("i_", rows_j), ("j_", rows_i)):
        for name in ("u", "l", "values", "reduced"):
            scratch[letter + name] = held(variables, total, rows_k)
        scratch[letter + "inverse"] = held(total, rows_k)
        for name in ("last", "gains", "far_gains"):
            scratch[letter + name] = held(variables, 3, plane, rows_k)
        for name in ("ends", "start", "far", "nexts", "solved"):
            scratch[letter + name] = held(variables, 2, plane, rows_k)
        scratch[letter + "meeting"] = held(variables, 7, plane, rows_k)
        chain = lax.axis_size(letter[0] + "a") > 2
        scratch[letter + "gain_sems"] = dma((2 if chain else 1,))
        scratch[letter + "sems"] = dma(((3 if chain else 1) * len(chunks),))
    for name in ("u", "l", "ratio", "turned", "reduced"):
        scratch["k_" + name] = held(len(tiles), rows_k * BS, LANES)
    scratch["k_zero"] = held(BS, LANES)
    scratch["k_meeting"] = held(len(tiles), 2, 7, BS, LANES)

    field = pltpu.HBM((variables, total, rows_k), F32)
    outs = dict(
        padded=pltpu.VMEM((variables, total + 2 * rows_j, rows_k), F32),
        k_values=pltpu.VMEM((len(tiles), rows_k * BS, LANES), F32),
        maps=pltpu.VMEM((variables, variables, BS, LANES), F32),
    )
    names = (*operands, *outs, *scratch)
    moved = sum(a.size * 4 for a in operands.values()) + 2 * variables * total * rows_k * 4
    handed = pl.pallas_call(
        functools.partial(step_body, axes, capacity, rows_i, rows_j, chunks, tiles, names),
        out_shape=list(outs.values()),
        in_specs=[HBM] * len(operands),
        out_specs=[VMEM] * len(outs),
        scratch_shapes=list(scratch.values()),
        compiler_params=pltpu.CompilerParams(
            vmem_limit_bytes=LIMIT, collective_id=0, has_side_effects=True
        ),
        cost_estimate=pl.CostEstimate(flops=60_000_000, bytes_accessed=moved, transcendentals=0),
    )(*(in_hbm(a) for a in operands.values()))
    advanced, increment = pl.pallas_call(
        functools.partial(finish, tiles),
        out_shape=[field, field],
        in_specs=[VMEM] * len(outs),
        out_specs=[HBM] * 2,
        scratch_shapes=[
            held(variables, total, rows_k),
            held(variables, total, rows_k),
            dma((2,)),
        ],
        compiler_params=pltpu.CompilerParams(vmem_limit_bytes=16 << 20),
        cost_estimate=pl.CostEstimate(flops=6_000_000, bytes_accessed=moved, transcendentals=0),
    )(*handed)
    return advanced.reshape(flow_state.shape), increment.reshape(flow_state.shape)


def solution(mesh):
    return jax.shard_map(
        local,
        mesh=mesh,
        in_specs=(
            P(None, "ka", "ia", "ja", None),
            P(None, "ka", "ia", "ja", None),
            P(None, "ka", None),
            P("ka", None, None),
            P("ka", None, None),
            P(("ia", "ja", "ka"), None, None),
            P(("ia", "ja", "ka"), None, None),
            P(("ia", "ja", "ka"), None),
            P(None, ("ia", "ja", "ka"), None, None),
        ),
        out_specs=(P(None, "ka", "ia", "ja", None), P(None, "ka", "ia", "ja", None)),
        check_vma=False,
    )
```

```python
import functools
import math
import types

import jax
import jax.numpy as jnp
from jax import lax
from jax.experimental import pallas as pl
from jax.experimental.pallas import tpu as pltpu
from jax.sharding import PartitionSpec as P

BS = 8
LANES = 128
GROUPS = LANES // BS
QUARTER = 0.25
BATCH = 8
PARTS = 2
LIMIT = 44 << 20
VMEM = pl.BlockSpec(memory_space=pltpu.VMEM)
HBM = pl.BlockSpec(memory_space=pltpu.HBM)
MESH = pl.DeviceIdType.MESH
F32 = jnp.float32


def in_hbm(array):
    return pltpu.with_memory_space_constraint(array, pltpu.HBM)


def lane_iota(rows=BS):
    return lax.broadcasted_iota(jnp.int32, (rows, LANES), 1)


def row_iota(rows=BS):
    return lax.broadcasted_iota(jnp.int32, (rows, LANES), 0)


def diagonals(tiles):
    group = lane_iota() // BS
    distance = 1
    while distance < GROUPS:
        odd = (group // distance) % 2 == 1
        tiles = [jnp.where(odd, tiles[(a + distance) % GROUPS], tiles[a]) for a in range(GROUPS)]
        distance *= 2
    return [tiles[(GROUPS - g) % GROUPS] for g in range(GROUPS)]


def turned_by(tile, groups):
    return tile if groups % GROUPS == 0 else pltpu.roll(tile, groups % GROUPS * BS, 1)


def tile_row(block, rows_j, g):
    blocks_j = rows_j // BS
    return (block // blocks_j) * (BS * rows_j) + (block % blocks_j) * BS + (g % BS) * rows_j


def rows_at(start, size):
    return pl.ds(pl.multiple_of(start, BS), size)


def pack_set(rows_j, q, flow, packed):
    groups = flow.shape[0] * BS
    first = q * GROUPS
    count = min(GROUPS, groups - first)

    def one(block, carry):
        tiles = [
            turned_by(flow[g // BS, rows_at(tile_row(block, rows_j, g), BS), :], g - first)
            for g in range(first, first + count)
        ]
        tiles = diagonals(tiles + tiles[:1] * (GROUPS - count))
        for k in range(GROUPS):
            packed[block * GROUPS + k, q * BS : (q + 1) * BS, :] = tiles[k]
        return carry

    lax.fori_loop(0, packed.shape[0] // GROUPS, one, 0, unroll=4)


def gather(capacity, donor, packed, slots, outbound):
    low = lane_iota() < LANES // 2
    tiles = outbound.shape[1] // BS
    fresh = []
    for slot in slots:
        cube = donor[0, slot % capacity, slot // capacity]
        shift = (GROUPS - cube % GROUPS) % GROUPS * BS
        for q in range(tiles):
            held = packed[cube, q * BS : (q + 1) * BS, :]
            tile = pltpu.roll(held, shift, 1)
            if q == tiles - 1:
                folded = pltpu.roll(pltpu.roll(held, BS // 2, 0), (shift + LANES // 2) % LANES, 1)
                tile = jnp.where(low, tile, folded)
            fresh.append((slot, q, tile))
    for slot, q, tile in fresh:
        outbound[slot, q * BS : (q + 1) * BS, :] = tile


def blend(cubes, shifted, weight):
    return (1.0 - weight) * cubes + weight * shifted


def interpolate(capacity, weights, receiver, slots, arrived):
    lane, row = lane_iota(), row_iota()
    tiles = arrived.shape[1] // BS
    held = [arrived[slot, q * BS : (q + 1) * BS, :] for slot in slots for q in range(tiles)]
    fresh = []
    for n, cubes in enumerate(held):
        slot, q = slots[n // tiles], n % tiles
        d, c = slot // capacity, slot % capacity
        shift = receiver[0, c, d] % GROUPS * BS
        if q == tiles - 1:
            unfolded = pltpu.roll(pltpu.roll(cubes, BS // 2, 0), LANES // 2, 1)
            cubes = jnp.where(row < BS // 2, cubes, unfolded)
        after = jnp.where(lane % (BS * BS) >= BS * (BS - 1), cubes, pltpu.roll(cubes, LANES - BS, 1))
        cubes = blend(cubes, after, weights[0, c, d])
        after = jnp.where(row == BS - 1, cubes, pltpu.roll(cubes, BS - 1, 0))
        cubes = blend(cubes, after, weights[1, c, d])
        after = jnp.where(lane % BS == BS - 1, cubes, pltpu.roll(cubes, LANES - 1, 1))
        cubes = blend(cubes, after, weights[2, c, d])
        fresh.append(pltpu.roll(cubes, shift, 1))
    for n, cubes in enumerate(fresh):
        q = n % tiles
        arrived[slots[n // tiles], q * BS : (q + 1) * BS, :] = cubes


def source_of(capacity, slots, receiver, count):
    lane = lane_iota()

    def one(slot, found):
        d, c = slot // capacity, slot % capacity
        target = jnp.where(count[0, d] > c, receiver[0, c, d], -1)
        return jnp.where(lane == target, slot, found)

    return lax.fori_loop(0, slots, one, jnp.full((BS, LANES), -1, jnp.int32), unroll=BATCH)


def unpack_part(rows_j, part, source, arrived, flow, padded):
    groups = flow.shape[0] * BS
    group = lane_iota() // BS

    def one(block, carry):
        slots = [source[0, block * GROUPS + k] for k in range(GROUPS)]
        owner = jnp.full((BS, LANES), -1, jnp.int32)
        for k in range(GROUPS):
            owner = jnp.where(group == k, slots[k], owner)
        live = owner >= 0
        for first in range(0, groups, GROUPS):
            q = first // GROUPS
            tiles = diagonals(
                [arrived[jnp.maximum(slots[k], 0), q * BS : (q + 1) * BS, :] for k in range(GROUPS)]
            )
            for g in range(first, min(first + GROUPS, groups)):
                row = tile_row(block, rows_j, g)
                fresh = turned_by(tiles[g - first], GROUPS - (g - first))
                kept = flow[g // BS, rows_at(row, BS), :]
                padded[g // BS, rows_at(row + rows_j, BS), :] = jnp.where(live, fresh, kept)
        return carry

    count = flow.shape[1] * flow.shape[2] // BS**3 // GROUPS // PARTS
    lax.fori_loop(part * count, (part + 1) * count, one, 0, unroll=2)


def row_of(n, count, lower):
    return jnp.where(lower, n, count - 1 - n)


def gains_of(state):
    older, newer, lead = state
    return lead, -QUARTER * older, (QUARTER * lead - 1.0) * newer, -QUARTER * newer


def meet_factors(near, far):
    f0, s0, f1, s1 = gains_of(near)
    g0, t0, g1, t1 = gains_of(far)
    cross = g1 - t1 * f0
    a11 = 1.0 - t1 * s0 - cross * f1
    a12 = -cross * s1
    a21 = g0 - t0 * f1
    a22 = 1.0 - t0 * s1
    scale = 1.0 / (a11 * a22 - a12 * a21)
    return a22 * scale, a12 * scale, a21 * scale, a11 * scale, t1, cross, t0


def meet(factors, near, far):
    m11, m12, m21, m22, t1, cross, t0 = factors
    r0, r1 = near
    q0, q1 = far
    b1 = q1 - t1 * r0 - cross * r1
    b2 = q0 - t0 * r1
    return b1 * m11 - m12 * b2, m22 * b2 - m21 * b1


def eliminated(pivot, carry):
    older, newer, lead, square = carry
    inverse = 1.0 / (pivot - 0.0625 * older - square)
    gain = QUARTER * lead - 1.0
    lead = gain * inverse
    return inverse, lead, (newer, inverse, lead, gain * gain * inverse)


def begin_factor(older, newer, lead):
    gain = QUARTER * lead - 1.0
    lead = gain * newer
    return older, newer, lead, gain * lead


def invert_rho(direction, rows, stride, spectral, inverse):
    plane = inverse.shape[0] // rows

    def one(row, carry):
        at = rows_at(row * plane, plane)
        if stride is None:
            inverse[at, :] = 1.0 / spectral[direction, at, :]
        else:
            inverse[at, :] = 1.0 / spectral[direction, pl.ds(row, plane, stride=stride), :]
        return carry

    lax.fori_loop(0, rows, one, 0, unroll=2)


def factor_pass(direction, rows, lower, group, paces, inverse, start, u_ref, l_ref, last):
    variables, total, lanes = u_ref.shape
    plane = total // rows
    for first in range(0, variables, group):
        vs = range(first, min(first + group, variables))

        def one(n, carry):
            at = rows_at(row_of(n, rows, lower) * plane, plane)
            ratio = inverse[at, :]
            fresh = []
            for v, held in zip(vs, carry):
                pace = paces[direction * variables + v, :plane, :]
                u, l, held = eliminated(pace * ratio + 2.5, held)
                u_ref[v, at, :] = u
                l_ref[v, at, :] = l
                fresh.append(held)
            return tuple(fresh)

        lax.fori_loop(0, rows, one, tuple(begin_factor(start[v, 0], start[v, 1], start[v, 2]) for v in vs))
    newest = rows_at(row_of(rows - 1, rows, lower) * plane, plane)
    older = rows_at(row_of(rows - 2, rows, lower) * plane, plane)
    for v in range(variables):
        last[v, 0] = u_ref[v, older, :]
        last[v, 1] = u_ref[v, newest, :]
        last[v, 2] = l_ref[v, older, :]


def forward_pass(vs, rows, lower, values, reduced_ref, scale, u_ref, l_ref, gains, start, ends):
    variables, total, lanes = values.shape
    plane = total // rows

    def one(n, carry):
        at = rows_at(row_of(n, rows, lower) * plane, plane)
        fresh = []
        for v, (product, older, newer) in zip(vs, carry):
            value = scale(v, at, values[v, at, :]) + QUARTER * older - product
            reduced = u_ref[v, at, :] * value
            reduced_ref[v, at, :] = reduced
            fresh.append((l_ref[v, at, :] * value, newer, reduced))
        return tuple(fresh)

    begin = tuple(((QUARTER * gains[v, 2] - 1.0) * start[v, 1], start[v, 0], start[v, 1]) for v in vs)
    for v, (product, older, newer) in zip(vs, lax.fori_loop(0, rows, one, begin, unroll=4)):
        ends[v, 0] = older
        ends[v, 1] = newer


def backward_pass(vs, rows, lower, values, u_ref, l_ref, nexts, solved, store):
    variables, total, lanes = values.shape
    plane = total // rows

    def one(step, carry):
        row = row_of(rows - 1 - step, rows, lower)
        at = rows_at(row * plane, plane)
        fresh = []
        for v, (nearer, farther) in zip(vs, carry):
            value = values[v, at, :] + QUARTER * u_ref[v, at, :] * farther - l_ref[v, at, :] * nearer
            store(v, row, at, value)
            fresh.append((value, nearer))
        return tuple(fresh)

    begin = tuple((nexts[v, 0], nexts[v, 1]) for v in vs)
    for v, (nearer, farther) in zip(vs, lax.fori_loop(0, rows, one, begin, unroll=4)):
        if solved is not None:
            solved[v, 0] = nearer
            solved[v, 1] = farther


def residual_rows(rows_i, first, count, padded, spectral, left, paces, inverse, values):
    variables, total, lanes = values.shape
    rows_j = total // rows_i
    lane, row_id = lane_iota(rows_j), row_iota(rows_j)

    def one(row, carry):
        base = row * rows_j
        at = rows_at(base, rows_j)
        rho = [spectral[e, at, :] for e in range(3)]
        ratio = inverse[at, :]
        residual = []
        for v in range(variables):
            center = padded[v, rows_at(base + rows_j, rows_j), :]
            twice = 2.0 * center
            along_i = padded[v, rows_at(base + 2 * rows_j, rows_j), :] + padded[v, at, :] - twice
            after = jnp.where(row_id == rows_j - 1, 0.0, padded[v, pl.ds(base + rows_j + 1, rows_j), :])
            before = jnp.where(row_id == 0, 0.0, padded[v, pl.ds(base + rows_j - 1, rows_j), :])
            along_j = after + before - twice
            after = jnp.where(lane == lanes - 1, 0.0, pltpu.roll(center, lanes - 1, 1))
            before = jnp.where(lane == 0, 0.0, pltpu.roll(center, 1, 1))
            along_k = after + before - twice
            residual.append(rho[0] * along_i + rho[1] * along_j + rho[2] * along_k)
        for v in range(variables):
            total_v = left[v, 0, 0] * residual[0]
            for u in range(1, variables):
                total_v = total_v + left[v, 0, u] * residual[u]
            values[v, at, :] = total_v * (ratio * paces[v, :rows_j, :])
        return carry

    lax.fori_loop(first, first + count, one, 0, unroll=3 if count % 3 == 0 else 1)


def edge_rows(vs, rows_i, halo, spectral, left, paces, inverse, values):
    variables, total, lanes = values.shape
    rows_j = total // rows_i
    size = rows_i // PARTS
    for part in range(PARTS):
        for side, first in enumerate((0, rows_j - 1)):
            at = pl.ds(part * size * rows_j + first, size, stride=rows_j)
            rho = spectral[1, at, :] * inverse[at, :]
            parts = [rho * halo[part, side, u] for u in range(variables)]
            for v in vs:
                total_v = left[v, 0, 0] * parts[0]
                for u in range(1, variables):
                    total_v = total_v + left[v, 0, u] * parts[u]
                values[v, at, :] = values[v, at, :] + total_v * paces[v, :size, :]


class Line:
    def __init__(self, axis):
        self.axis = axis
        self.members = lax.axis_size(axis)
        self.half = self.members // 2
        self.place = lax.axis_index(axis)
        self.lower = self.place < self.half
        depth = jnp.where(self.lower, self.place, self.members - 1 - self.place)
        self.inner = jnp.where(self.lower, self.place + 1, self.place - 1)
        self.outer = jnp.where(self.lower, self.place - 1, self.place + 1)
        self.middle = depth == self.half - 1
        self.end = depth == 0

    def send(self, source, target, send_sem, recv_sem, device):
        return pltpu.make_async_remote_copy(
            src_ref=source,
            dst_ref=target,
            send_sem=send_sem,
            recv_sem=recv_sem,
            device_id={self.axis: device},
            device_id_type=MESH,
        )

    def sides(self):
        return (self.place > 0, self.place - 1), (self.place < self.members - 1, self.place + 1)


def span(vs):
    return pl.ds(vs[0], len(vs))


class Sweep:
    def __init__(self, line, s, chunks, sent):
        self.line, self.s, self.chunks, self.sent = line, s, chunks, sent

    def gains_to(self, target, number):
        s = self.s
        return self.line.send(s.last, target, self.sent[0], s.gain_sems.at[number], self.line.inner)

    def gains_in(self):
        line, s = self.line, self.s
        if line.half > 1:

            @pl.when(jnp.logical_not(line.end))
            def _():
                self.gains_to(s.gains, 1).wait_recv()

    def gains_out(self):
        line, s = self.line, self.s
        if line.half > 1:

            @pl.when(jnp.logical_not(line.middle))
            def _():
                self.gains_to(s.gains, 1).start()

        @pl.when(line.middle)
        def _():
            self.gains_to(s.far_gains, 0).start()

    def prepare(self):
        line, s = self.line, self.s

        @pl.when(line.middle)
        def _():
            self.gains_to(s.far_gains, 0).wait_recv()
            for v in range(s.last.shape[0]):
                near = [s.last[v, m] for m in range(3)]
                far = [s.far_gains[v, m] for m in range(3)]
                for m, factor in enumerate(meet_factors(near, far)):
                    s.meeting[v, m] = factor

    def part(self, c):
        return span(self.chunks[c]) if c is not None else span(range(self.s.last.shape[0]))

    def inward(self, c):
        s, at = self.s, self.part(c)
        recv = s.sems.at[len(self.chunks) + (c or 0)]
        return self.line.send(s.ends.at[at], s.start.at[at], self.sent[1], recv, self.line.inner)

    def across(self, c):
        s, at = self.s, self.part(c)
        recv = s.sems.at[c or 0]
        return self.line.send(s.ends.at[at], s.far.at[at], self.sent[1], recv, self.line.inner)

    def outward(self, c):
        s, at = self.s, self.part(c)
        recv = s.sems.at[2 * len(self.chunks) + (c or 0)]
        return self.line.send(s.solved.at[at], s.nexts.at[at], self.sent[2], recv, self.line.outer)

    def start_in(self, c):
        if self.line.half > 1:

            @pl.when(jnp.logical_not(self.line.end))
            def _():
                self.inward(c).wait_recv()

    def ends_out(self, c):
        line = self.line
        if line.half > 1:

            @pl.when(jnp.logical_not(line.middle))
            def _():
                self.inward(c).start()

        @pl.when(line.middle)
        def _():
            self.across(c).start()

    def nexts_in(self, c):
        line, s = self.line, self.s

        @pl.when(line.middle)
        def _():
            self.across(c).wait_recv()
            for v in self.chunks[c]:
                pair = meet(
                    [s.meeting[v, m] for m in range(7)],
                    [s.ends[v, m] for m in range(2)],
                    [s.far[v, m] for m in range(2)],
                )
                s.nexts[v, 0], s.nexts[v, 1] = pair

        if line.half > 1:

            @pl.when(jnp.logical_not(line.middle))
            def _():
                self.outward(c).wait_recv()

    def solved_out(self, c):
        line = self.line
        if line.half > 1:

            @pl.when(jnp.logical_not(line.end))
            def _():
                self.outward(c).start()

    def close(self):
        line = self.line
        self.gains_to(self.s.far_gains, 0).wait_send()
        self.across(None).wait_send()
        if line.half > 1:

            @pl.when(jnp.logical_not(line.end))
            def _():
                self.outward(None).wait_send()

    def clear(self):
        line, s = self.line, self.s

        @pl.when(line.end)
        def _():
            s.gains[...] = jnp.zeros(s.gains.shape, F32)
            s.start[...] = jnp.zeros(s.start.shape, F32)


def step_body(axes, capacity, rows_i, rows_j, chunks, tiles, names, *refs):
    s = types.SimpleNamespace(**dict(zip(names, refs)))
    flow, rho, padded = s.flow, s.rho, s.padded
    variables, total, lanes = flow.shape
    line_i, line_j = Line("ia"), Line("ja")

    def part(letter):
        return types.SimpleNamespace(**{k[2:]: r for k, r in vars(s).items() if k[:2] == letter + "_"})

    si, sj = part("i"), part("j")
    first = 4 + 2 * PARTS
    sweep_i, sweep_j = (
        Sweep(line, part, chunks, [s.own_sems.at[first + 3 * n + m] for m in range(3)])
        for n, (line, part) in enumerate(((line_i, si), (line_j, sj)))
    )
    sizes = [lax.axis_size(axis) for axis in axes]
    here = [lax.axis_index(axis) for axis in axes]
    devices = math.prod(sizes)
    slots = devices * capacity

    packed_tiles = s.packed.shape[1] // BS
    fields = []
    for q in range(packed_tiles):
        at = pl.ds(2 * q, min(2, variables - 2 * q))
        fields.append(pltpu.make_async_copy(s.flow_in.at[at], flow.at[at], s.own_sems.at[q]))
    fields.append(pltpu.make_async_copy(s.rho_in, rho, s.own_sems.at[packed_tiles]))
    small = [
        pltpu.make_async_copy(getattr(s, name + "_in"), getattr(s, name), s.own_sems.at[packed_tiles + 1 + n])
        for n, name in enumerate(("speeds", "left", "right", "donor", "receiver", "count", "weights"))
    ]
    for copy in fields[:-1] + small + fields[-1:]:
        copy.start()

    order_j = sorted(range(sizes[1]), key=lambda d: min(d, sizes[1] - d))
    rest = devices // sizes[1]

    def peer(offset_j, n, sign):
        off = (n // sizes[2], offset_j, n % sizes[2])
        place = [(h + sign * o + size) % size for h, o, size in zip(here, off, sizes)]
        number = (place[0] * sizes[1] + place[1]) * sizes[2] + place[2]
        return number, dict(zip(axes, place))

    around = [[(h + o) % size for o in range(size)] for h, size in zip(here, sizes)]
    me = (here[0] * sizes[1] + here[1]) * sizes[2] + here[2]
    barrier = pltpu.get_barrier_semaphore()
    with jax.named_scope("greet"):
        for offset_j in order_j:
            for n in range(0 if offset_j else 1, rest):
                place = around[0][n // sizes[2]], around[1][offset_j], around[2][n % sizes[2]]
                pl.semaphore_signal(barrier, inc=1, device_id=dict(zip(axes, place)), device_id_type=MESH)

    with jax.named_scope("pack"):
        for q in range(packed_tiles):
            with jax.named_scope(f"flow{q}"):
                fields[q].wait()
            with jax.named_scope(f"pack{q}"):
                pack_set(rows_j, q, flow, s.packed)
    for copy in small:
        copy.wait()
    with jax.named_scope("entered"):
        pl.semaphore_wait(barrier, devices - 1)

    used = variables * BS**3 // LANES

    def cubes(step, to, place, of, count=1):
        def at(device):
            return pl.ds(device * capacity, count * capacity), pl.ds(0, used)

        return pltpu.make_async_remote_copy(
            src_ref=s.outbound.at[at(to)],
            dst_ref=s.arrived.at[at(of)],
            send_sem=s.own_sems.at[1],
            recv_sem=s.cube_sems.at[step // BATCH],
            device_id=place,
            device_id_type=MESH,
        )

    with jax.named_scope("send_cubes"):
        for m, offset_j in enumerate(order_j):

            def begin(batch, carry, skip=0):
                first = batch * BATCH
                numbers = [peer(offset_j, first + n, 1)[0] for n in range(BATCH)]
                for c in range(capacity):
                    gather(capacity, s.donor, s.packed, [to * capacity + c for to in numbers], s.outbound)
                for n in range(skip, BATCH):
                    to, place = peer(offset_j, first + n, 1)
                    cubes(m * rest + first + n, to, place, me).start()
                return carry

            if offset_j == 0:
                begin(0, 0, 1)
            lax.fori_loop(0 if offset_j else 1, rest // BATCH, begin, 0)
        own = pl.ds(me * capacity, capacity)
        s.arrived[own] = s.outbound[own]

    def pace(n, carry):
        value = jnp.full((BS, LANES), s.speeds[n // variables, 0, n % variables], F32)
        value = 1.0 / value
        for first in range(0, s.paces.shape[1], BS):
            s.paces[n, first : first + BS, :] = value
        return carry

    def factor_j():
        with jax.named_scope("factor_j"):
            sweep_j.gains_in()
            factor_pass(1, rows_j, line_j.lower, 2, s.paces, sj.inverse, sj.gains, sj.u, sj.l, sj.last)
            sweep_j.gains_out()

    with jax.named_scope("prepare"):
        lax.fori_loop(0, 3 * variables, pace, 0)
        for v in range(variables):
            for u in range(variables):
                s.maps[v, u] = jnp.full((BS, LANES), s.right[v, 0, u], F32)
        sweep_i.clear()
        sweep_j.clear()
        fields[-1].wait()
        invert_rho(1, rows_j, rows_j, rho, sj.inverse)
        pl.when(line_j.end)(factor_j)
    with jax.named_scope("factor_i"):
        invert_rho(0, rows_i, None, rho, si.inverse)
        sweep_i.gains_in()
        factor_pass(0, rows_i, line_i.lower, 3, s.paces, si.inverse, si.gains, si.u, si.l, si.last)
        sweep_i.gains_out()
    with jax.named_scope("sources"):
        s.found[...] = source_of(capacity, slots, s.receiver, s.count)
        found = pltpu.make_async_copy(s.found, s.source, s.own_sems.at[0])
        found.start()
    with jax.named_scope("factor_k"):
        factor_k(tiles, s)
    with jax.named_scope("arrivals"):
        for m, offset_j in enumerate(order_j):

            def arrive(batch, carry, count=BATCH):
                first = batch * BATCH
                cubes(m * rest + first, 0, peer(offset_j, first + BATCH - 1, 1)[1], 0, count).wait_recv()
                sources = [peer(offset_j, first + n, -1)[0] for n in range(BATCH)]
                for c in range(capacity):
                    interpolate(capacity, s.weights, s.receiver, [of * capacity + c for of in sources], s.arrived)
                return carry

            if offset_j == 0:
                arrive(0, 0, BATCH - 1)
            lax.fori_loop(0 if offset_j else 1, rest // BATCH, arrive, 0)
    rows_part = rows_i // PARTS

    def halo_i(side, device):
        mine, other = (rows_j, rows_j + total) if side == 0 else (total, 0)
        source = padded.at[:, pl.ds(mine, rows_j), :]
        target = padded.at[:, pl.ds(other, rows_j), :]
        return line_i.send(source, target, s.own_sems.at[2 + side], s.halo_sems.at[side], device)

    def halo_j(side, device, part):
        n = 2 + 2 * part + side
        source, target = s.edge.at[part, side], s.halo.at[part, 1 - side]
        return line_j.send(source, target, s.own_sems.at[2 + n], s.halo_sems.at[n], device)

    def at_borders(line, act, otherwise=None):
        for side, (there, device) in enumerate(line.sides()):
            pl.when(there)(functools.partial(act, side, device))
            if otherwise is not None:
                pl.when(jnp.logical_not(there))(functools.partial(otherwise, side))

    for part in range(PARTS):
        with jax.named_scope("unpack"):
            if part == 0:
                found.wait()
            unpack_part(rows_j, part, s.source, s.arrived, flow, padded)
        with jax.named_scope("send_halos"):
            for side, row in enumerate((rows_j, 2 * rows_j - 1)):
                at = pl.ds(row + part * rows_part * rows_j, rows_part, stride=rows_j)
                for v in range(variables):
                    s.edge[part, side, v] = padded[v, at, :]
            at_borders(line_j, lambda side, device: halo_j(side, device, part).start())
    with jax.named_scope("send_halos"):
        at_borders(line_i, lambda side, device: halo_i(side, device).start())

    rest_of = (padded, rho, s.left, s.paces, si.inverse, si.values)
    with jax.named_scope("residual"):
        residual_rows(rows_i, 1, rows_i - 2, *rest_of)
    if line_j.half > 1:
        pl.when(jnp.logical_not(line_j.end))(factor_j)
    with jax.named_scope("halos"):

        def no_i(side):
            first = 0 if side == 0 else rows_j + total
            padded[:, first : first + rows_j, :] = jnp.zeros((variables, rows_j, lanes), F32)

        def no_j(part, side):
            s.halo[part, side] = jnp.zeros(s.halo.shape[2:], F32)

        at_borders(line_i, lambda side, device: halo_i(1 - side, device).wait_recv(), no_i)
        for part in range(PARTS):
            at_borders(
                line_j, lambda side, device: halo_j(1 - side, device, part).wait_recv(), functools.partial(no_j, part)
            )
    with jax.named_scope("edges"):
        residual_rows(rows_i, 0, 1, *rest_of)
        residual_rows(rows_i, rows_i - 1, 1, *rest_of)

    def plain(v, at, value):
        return value

    def scaled(v, at, value):
        return value * (sj.inverse[at, :] * s.paces[variables + v, :rows_i, :])

    def store_turned(v, row, at, value):
        sj.values[v, pl.ds(row, rows_j, stride=rows_i), :] = value

    def store_lines(v, row, at, value):
        s.lines[v, pl.ds(row, rows_i, stride=rows_j), :] = value

    def forward_i(c):
        edge_rows(chunks[c], rows_i, s.halo, rho, s.left, s.paces, si.inverse, si.values)
        sweep_i.start_in(c)
        forward_pass(chunks[c], rows_i, line_i.lower, si.values, si.reduced, plain, si.u, si.l, si.gains, si.start, si.ends)
        sweep_i.ends_out(c)

    def back_i(c):
        sweep_i.nexts_in(c)
        solved = si.solved if line_i.half > 1 else None
        backward_pass(chunks[c], rows_i, line_i.lower, si.reduced, si.u, si.l, si.nexts, solved, store_turned)
        sweep_i.solved_out(c)

    def forward_j(c):
        sweep_j.start_in(c)
        forward_pass(chunks[c], rows_j, line_j.lower, sj.values, sj.reduced, scaled, sj.u, sj.l, sj.gains, sj.start, sj.ends)
        sweep_j.ends_out(c)

    def back_j(c):
        sweep_j.nexts_in(c)
        solved = sj.solved if line_j.half > 1 else None
        backward_pass(chunks[c], rows_j, line_j.lower, sj.reduced, sj.u, sj.l, sj.nexts, solved, store_lines)
        sweep_j.solved_out(c)

    numbers = range(len(chunks))
    with jax.named_scope("forward_i"):
        for c in numbers:
            forward_i(c)
    with jax.named_scope("prepare_i"):
        sweep_i.prepare()
    with jax.named_scope("back_i"):
        for c in numbers:
            back_i(c)
            pl.when(line_j.end)(functools.partial(forward_j, c))
    with jax.named_scope("solve_j"):
        if line_j.half > 1:
            for c in numbers:
                pl.when(jnp.logical_not(line_j.end))(functools.partial(forward_j, c))
        sweep_j.prepare()
        for c in numbers:
            back_j(c)
            for t, vs in enumerate(tiles[:-1]):
                if vs[-1] == chunks[c][-1]:
                    pl.when(line_j.end)(functools.partial(solve_k, t, vs, s))
        for t, vs in enumerate(tiles[:-1]):
            pl.when(jnp.logical_not(line_j.end))(functools.partial(solve_k, t, vs, s))
        solve_k(len(tiles) - 1, tiles[-1], s)

    with jax.named_scope("close"):
        at_borders(line_i, lambda side, device: halo_i(side, device).wait_send())
        for part in range(PARTS):
            at_borders(line_j, lambda side, device: halo_j(side, device, part).wait_send())
        cubes(0, 0, peer(order_j[0], 0, 1)[1], 0, devices - 1).wait_send()
        sweep_i.close()
        sweep_j.close()


def sides_of(lanes, step):
    for k in (step, lanes - 1 - step):
        yield rows_at(k * BS, BS)


def factor_k(chunks, s):
    total, lanes = s.rho.shape[1:]
    variables = s.flow.shape[0]
    quarters = total // LANES
    for q in range(quarters):
        ratio = (1.0 / s.rho[2, q * LANES : (q + 1) * LANES, :]).T
        for c, vs in enumerate(chunks):
            for m, v in enumerate(vs):
                at = pl.ds(m * quarters + q, lanes, stride=BS)
                s.k_ratio[c, at, :] = ratio * s.paces[2 * variables + v, :1, :]
    for c, vs in enumerate(chunks):
        for spare in range(len(vs) * quarters, BS):
            at = pl.ds(spare, lanes, stride=BS)
            s.k_ratio[c, at, :] = jnp.zeros((lanes, lanes), F32)
            s.k_turned[c, at, :] = jnp.zeros((lanes, lanes), F32)
    half = lanes // 2
    s.k_zero[...] = jnp.zeros((BS, lanes), F32)
    zero = s.k_zero[...]
    numbers = range(len(chunks))

    def one(n, carry):
        fresh = []
        for c in numbers:
            for at, held in zip(sides_of(lanes, n), carry[c]):
                u, l, held = eliminated(s.k_ratio[c, at, :] + 2.5, held)
                s.k_u[c, at, :] = u
                s.k_l[c, at, :] = l
                fresh.append(held)
        return tuple(zip(fresh[::2], fresh[1::2]))

    lax.fori_loop(0, half, one, ((begin_factor(zero, zero, zero),) * 2,) * len(chunks))
    for c in numbers:
        pair = []
        for older, newer in zip(sides_of(lanes, half - 2), sides_of(lanes, half - 1)):
            pair.append((s.k_u[c, older, :], s.k_u[c, newer, :], s.k_l[c, older, :]))
        for side in range(2):
            for m, factor in enumerate(meet_factors(pair[side], pair[1 - side])):
                s.k_meeting[c, side, m] = factor


def solve_k(c, vs, s):
    total, lanes = s.rho.shape[1:]
    quarters = total // LANES
    half = lanes // 2
    turned, reduced_ref, values = s.k_turned.at[c], s.k_reduced.at[c], s.k_values.at[c]
    ratio, u_ref, l_ref = s.k_ratio.at[c], s.k_u.at[c], s.k_l.at[c]
    with jax.named_scope("turn_k"):
        for m, v in enumerate(vs):
            for q in range(quarters):
                at = pl.ds(m * quarters + q, lanes, stride=BS)
                turned[at, :] = s.lines[v, q * LANES : (q + 1) * LANES, :].T * ratio[at, :]
    zero = s.k_zero[...]

    def ahead(n, carry):
        fresh = []
        for at, (product, older, newer) in zip(sides_of(lanes, n), carry):
            value = turned[at, :] + QUARTER * older - product
            reduced = u_ref[at, :] * value
            reduced_ref[at, :] = reduced
            fresh.append((l_ref[at, :] * value, newer, reduced))
        return tuple(fresh)

    with jax.named_scope("forward_k"):
        ends = [end[1:] for end in lax.fori_loop(0, half, ahead, ((zero,) * 3,) * 2, unroll=8)]
        nexts = tuple(
            meet([s.k_meeting[c, side, m] for m in range(7)], ends[side], ends[1 - side]) for side in range(2)
        )

    def back(step, carry):
        fresh = []
        for at, (nearer, farther) in zip(sides_of(lanes, half - 1 - step), carry):
            value = reduced_ref[at, :] + QUARTER * u_ref[at, :] * farther - l_ref[at, :] * nearer
            values[at, :] = value
            fresh.append((value, nearer))
        return tuple(fresh)

    with jax.named_scope("back_k"):
        lax.fori_loop(0, half, back, nexts, unroll=8)


def finish(chunks, padded, values, maps, advanced_out, increment_out, advanced, increment, sems):
    variables, total, lanes = advanced.shape
    rows_j = (padded.shape[1] - total) // 2
    quarters = total // LANES
    places = {v: (c, m) for c, vs in enumerate(chunks) for m, v in enumerate(vs)}

    def copies(at):
        return [
            pltpu.make_async_copy(source.at[at], target.at[at], sems.at[n])
            for n, (source, target) in enumerate(((advanced, advanced_out), (increment, increment_out)))
        ]

    for q in range(quarters):
        first = q * LANES
        solved = []
        for u in range(variables):
            c, m = places[u]
            solved.append(values[c, pl.ds(m * quarters + q, lanes, stride=BS), :])
        for v in range(variables):
            total_v = maps[v, 0, :1, :] * solved[0]
            for u in range(1, variables):
                total_v = total_v + maps[v, u, :1, :] * solved[u]
            piece = total_v.T
            increment[v, first : first + LANES, :] = piece
            advanced[v, first : first + LANES, :] = padded[v, rows_j + first : rows_j + first + LANES, :] + piece
            for copy in copies((v, pl.ds(first, LANES))):
                copy.start()
    for copy in copies((pl.ds(0, variables), pl.ds(0, total))):
        copy.wait()


def local(
    flow_state, spectral, wave_speed, left_map, right_map,
    donor_block, receiver_block, fringe_count, fringe_weight,
):
    variables, grids, rows_i, rows_j, rows_k = flow_state.shape
    assert grids == 1 and rows_k == LANES
    total = rows_i * rows_j
    devices, capacity = donor_block.shape[1:]
    slots = devices * capacity
    cube_count = total // (BS * BS) * (rows_k // BS)
    assert cube_count == LANES
    packed_rows = -(-variables * BS // GROUPS) * BS
    together = BS * LANES // total
    axes = ("ia", "ja", "ka")
    chunks = tuple((v,) for v in range(variables))
    tiles = tuple(tuple(range(v, min(v + together, variables))) for v in range(0, variables, together))
    operands = dict(
        flow_in=flow_state.reshape(variables, total, rows_k),
        rho_in=spectral.reshape(3, total, rows_k),
        speeds_in=wave_speed,
        left_in=left_map.transpose(1, 0, 2),
        right_in=right_map.transpose(1, 0, 2),
        donor_in=donor_block.transpose(0, 2, 1),
        receiver_in=receiver_block.transpose(0, 2, 1),
        count_in=fringe_count,
        weights_in=fringe_weight.transpose(0, 1, 3, 2).reshape(3, capacity, devices),
    )
    dma = pltpu.SemaphoreType.DMA

    def held(*dims):
        return pltpu.VMEM(dims, F32)

    scratch = dict(
        flow=held(variables, total, rows_k),
        rho=held(3, total, rows_k),
        lines=held(variables, total, rows_k),
        packed=held(cube_count, packed_rows, LANES),
        outbound=held(slots, packed_rows, LANES),
        arrived=held(slots, packed_rows, LANES),
        found=pltpu.VMEM((BS, LANES), jnp.int32),
        source=pltpu.SMEM((BS, LANES), jnp.int32),
        paces=held(3 * variables, max(rows_i, rows_j), LANES),
        edge=held(PARTS, 2, variables, rows_i // PARTS, rows_k),
        halo=held(PARTS, 2, variables, rows_i // PARTS, rows_k),
        own_sems=dma((10 + 2 * PARTS,)),
        cube_sems=dma((devices // BATCH,)),
        halo_sems=dma((2 + 2 * PARTS,)),
    )
    for name in ("speeds", "left", "right", "donor", "receiver", "count", "weights"):
        array = operands[name + "_in"]
        scratch[name] = pltpu.SMEM(array.shape, array.dtype)
    for letter, plane in (("i_", rows_j), ("j_", rows_i)):
        for name in ("u", "l", "values", "reduced"):
            scratch[letter + name] = held(variables, total, rows_k)
        scratch[letter + "inverse"] = held(total, rows_k)
        for name in ("last", "gains", "far_gains"):
            scratch[letter + name] = held(variables, 3, plane, rows_k)
        for name in ("ends", "start", "far", "nexts", "solved"):
            scratch[letter + name] = held(variables, 2, plane, rows_k)
        scratch[letter + "meeting"] = held(variables, 7, plane, rows_k)
        chain = lax.axis_size(letter[0] + "a") > 2
        scratch[letter + "gain_sems"] = dma((2 if chain else 1,))
        scratch[letter + "sems"] = dma(((3 if chain else 1) * len(chunks),))
    for name in ("u", "l", "ratio", "turned", "reduced"):
        scratch["k_" + name] = held(len(tiles), rows_k * BS, LANES)
    scratch["k_zero"] = held(BS, LANES)
    scratch["k_meeting"] = held(len(tiles), 2, 7, BS, LANES)

    field = pltpu.HBM((variables, total, rows_k), F32)
    outs = dict(
        padded=pltpu.VMEM((variables, total + 2 * rows_j, rows_k), F32),
        k_values=pltpu.VMEM((len(tiles), rows_k * BS, LANES), F32),
        maps=pltpu.VMEM((variables, variables, BS, LANES), F32),
    )
    names = (*operands, *outs, *scratch)
    moved = sum(a.size * 4 for a in operands.values()) + 2 * variables * total * rows_k * 4
    handed = pl.pallas_call(
        functools.partial(step_body, axes, capacity, rows_i, rows_j, chunks, tiles, names),
        out_shape=list(outs.values()),
        in_specs=[HBM] * len(operands),
        out_specs=[VMEM] * len(outs),
        scratch_shapes=list(scratch.values()),
        compiler_params=pltpu.CompilerParams(
            vmem_limit_bytes=LIMIT, collective_id=0, has_side_effects=True
        ),
        cost_estimate=pl.CostEstimate(flops=60_000_000, bytes_accessed=moved, transcendentals=0),
    )(*(in_hbm(a) for a in operands.values()))
    advanced, increment = pl.pallas_call(
        functools.partial(finish, tiles),
        out_shape=[field, field],
        in_specs=[VMEM] * len(outs),
        out_specs=[HBM] * 2,
        scratch_shapes=[
            held(variables, total, rows_k),
            held(variables, total, rows_k),
            dma((2,)),
        ],
        compiler_params=pltpu.CompilerParams(vmem_limit_bytes=16 << 20),
        cost_estimate=pl.CostEstimate(flops=6_000_000, bytes_accessed=moved, transcendentals=0),
    )(*handed)
    return advanced.reshape(flow_state.shape), increment.reshape(flow_state.shape)


def solution(mesh):
    return jax.shard_map(
        local,
        mesh=mesh,
        in_specs=(
            P(None, "ka", "ia", "ja", None),
            P(None, "ka", "ia", "ja", None),
            P(None, "ka", None),
            P("ka", None, None),
            P("ka", None, None),
            P(("ia", "ja", "ka"), None, None),
            P(("ia", "ja", "ka"), None, None),
            P(("ia", "ja", "ka"), None),
            P(None, ("ia", "ja", "ka"), None, None),
        ),
        out_specs=(P(None, "ka", "ia", "ja", None), P(None, "ka", "ia", "ja", None)),
        check_vma=False,
    )
```
